256 devices in a mesh: dp: 8 (over x, z_lo), seq: 32 (over y, z_hi, core).
Axes of the slice: x: 4, y: 4, z: 8 (z_hi: 4, z_lo: 2; z = z_hi * 2 + z_lo), core: 2. Of those that a mesh axis runs over, the one named last changes fastest.
Arguments:
- queries: bfloat16 [8, 32, 512, 1024], P('dp', 'seq'), may hold values from -16 to 16
- keys: bfloat16 [8, 32, 512, 1024], P('dp', 'seq'), may hold values from -12 to 12
- values: bfloat16 [8, 32, 512, 1024], P('dp', 'seq'), may hold values from -24 to 24
- out_proj: bfloat16 [1024, 2048], P(('dp', 'seq')), may hold values from -0.1875 to 0.1875
- out_grad: bfloat16 [8, 32, 512, 2048], P('dp', 'seq'), may hold values from -48 to 48
- block_pattern: int32 [4, 4], replicated, may hold values from 0 to 3, as said below
- col_offset: int32 [4], replicated, may hold values from 0 to 511
Outputs:
- layer_out: bfloat16 [8, 32, 512, 2048], P('dp', 'seq')
- q_grad: bfloat16 [8, 32, 512, 1024], P('dp', 'seq')
- k_grad: bfloat16 [8, 32, 512, 1024], P('dp', 'seq')
- v_grad: bfloat16 [8, 32, 512, 1024], P('dp', 'seq')
- w_grad: float32 [1024, 2048], P(('dp', 'seq'))
The draws below stay inside these ranges and needn't reach their ends.
Inputs may be any that keep to these rules, and one draw needn't show every extreme that they name: `block_pattern`: for each row head, the entries name each of the 4 blocks of a grid row once, and entry j is never j.
All inputs are finite; a program needn't handle non-finite values.
Results may differ from the reference program's by a relative error of at most 0.006.
Values may be sent and summed in bfloat16 or wider, within the bound.
No kernel may reach another device: no remote copies, remote signals or barrier semaphores. Data moves between devices by JAX's collectives and lax.ppermute only.
A program may use at most 128 MiB of HBM per device.

```python
import jax
import jax.numpy as jnp
from jax import lax

D = 2048
HD = 128
HR = 4
HC = 4
BLK = 128
NB = 4
W = 1024
COLS = 512
GR = 32
BATCH = 8
ALL_TOK = 131072


def draw_queries(key, part):
    full_shape = (BATCH, GR, COLS, W)
    base_key = jax.random.fold_in(key, 101)
    result_field = jnp.clip(jax.random.normal(jax.random.fold_in(base_key, 1), full_shape, jnp.float32), -6.0, 6.0)
    return result_field.astype(jnp.bfloat16)


def draw_keys(key, part):
    full_shape = (BATCH, GR, COLS, W)
    base_key = jax.random.fold_in(key, 202)
    result_field = jnp.clip(jax.random.normal(jax.random.fold_in(base_key, 1), full_shape, jnp.float32), -6.0, 6.0)
    return result_field.astype(jnp.bfloat16)


def draw_block_pattern(key, part):
    head_keys = jax.random.split(jax.random.fold_in(key, 303), HR)

    def one_head(head_key):
        block_order = jax.random.permutation(head_key, NB).astype(jnp.int32)
        next_block = jnp.roll(block_order, -1)
        return jnp.zeros((NB,), jnp.int32).at[block_order].set(next_block)
    return jax.vmap(one_head)(head_keys).astype(jnp.int32)


def place_ends(result, key, least, largest):
    longest = result.shape.index(max(result.shape))
    spots = []
    for shift in (0, 1):
        where = [jax.random.randint(jax.random.fold_in(key, axis), (), 0, length) for axis, length in enumerate(result.shape)]
        where[longest] = (where[longest] + shift) % result.shape[longest]
        spots.append(tuple(where))
    return result.at[spots[0]].set(least).at[spots[1]].set(largest)


def strengthened(values, own_key, source, target, blocks, factor):
    owner, partner = [(jnp.arange(values.shape[axis_at]) // (values.shape[axis_at] // blocks)).reshape([-1 if axis == axis_at else 1 for axis in range(values.ndim)]) for axis_at in (source, target)]
    chosen = jax.random.permutation(own_key, blocks)[partner]
    strong = (owner == chosen) | (owner == (partner + blocks // 2) % blocks)
    return jnp.where(strong, factor * values, values)


def block_scale(key, shape, cuts, low, largest):
    factor_of, own = 1.0, jax.random.fold_in(key, 6)
    for position, shards_of in cuts:
        draws = jnp.exp(jax.random.uniform(jax.random.fold_in(own, position), (shards_of,), jnp.float32, low / len(cuts), largest / len(cuts)))
        factor_of = factor_of * jnp.repeat(draws, shape[position] // shards_of).reshape([-1 if axis == position else 1 for axis in range(len(shape))])
    return factor_of


def normal_values(rng, dims, deviation, bound, cuts=(), kind=jnp.bfloat16):
    array = jax.random.normal(rng, dims, jnp.float32) * deviation
    if len(cuts) > 0:
        array = block_scale(rng, dims, cuts, -0.22, 0.18) * array
    return jnp.clip(array, min=-bound, max=bound).astype(kind)


def noise_with(own_key, dims, scale, bound, cuts, heavy, kind=jnp.bfloat16):
    drawn = scale * jax.random.normal(own_key, dims, jnp.float32)
    if cuts:
        drawn = drawn * block_scale(own_key, dims, cuts, -0.22, 0.18)
    return jnp.clip(strengthened(drawn, jax.random.fold_in(own_key, 3), *heavy), -bound, bound).astype(kind)


def setup_inputs(seed: int = 0) -> dict:
    seeds = jax.random.split(jax.random.key(seed), 8)
    return {
        "queries": draw_queries(jax.random.fold_in(seeds[7], 71), 0),
        "keys": draw_keys(jax.random.fold_in(seeds[7], 71), 0),
        "values": normal_values(seeds[2], (BATCH, GR, COLS, W), 4.0, 24.0, ((0, 8), (1, 32))),
        "out_proj": normal_values(seeds[3], (W, D), W ** -0.5, 0.1875, ((0, 256),)),
        "out_grad": noise_with(seeds[4], (BATCH, GR, COLS, D), 8.0, 48.0, ((0, 8), (1, 32)), (1, 3, 32, 2.75)),
        "block_pattern": draw_block_pattern(jax.random.fold_in(seeds[7], 71), 0),
        "col_offset": place_ends(jax.random.randint(seeds[6], (HC,), 0, COLS), jax.random.fold_in(seeds[6], 1), 0, COLS - 1).astype(jnp.int32),
    }


def half_and_back(tensor):
    return lax.optimization_barrier(tensor.astype(jnp.bfloat16)).astype(jnp.float32)


def row_head(query_h, key_h, value_h, grad_h, pattern_h):
    score_scale = HD ** -0.5
    query_full = query_h.astype(jnp.float32)
    grad_full = grad_h.astype(jnp.float32)
    key_joined = jnp.concatenate([jnp.take(key_h, pattern_h, axis=1), key_h], axis=2).astype(jnp.float32)
    value_joined = jnp.concatenate([jnp.take(value_h, pattern_h, axis=1), value_h], axis=2).astype(jnp.float32)
    scores = jnp.einsum('rjqd,rjkd->rjqk', query_full, key_joined) * score_scale
    row_probs = jax.nn.softmax(scores, axis=-1)
    prob_half = half_and_back(row_probs)
    head_out = jnp.einsum('rjqk,rjkd->rjqd', prob_half, value_joined).astype(jnp.bfloat16)
    value_terms = jnp.einsum('rjqk,rjqd->rjkd', prob_half, grad_full)
    prob_grad = jnp.einsum('rjqd,rjkd->rjqk', grad_full, value_joined)
    delta_sum = jnp.sum(row_probs * prob_grad, axis=-1, keepdims=True)
    score_grad = half_and_back(row_probs * (prob_grad - delta_sum))
    query_grad = (jnp.einsum('rjqk,rjkd->rjqd', score_grad, key_joined) * score_scale).astype(jnp.bfloat16)
    key_terms = jnp.einsum('rjqk,rjqd->rjkd', score_grad, query_full) * score_scale
    key_grad = key_terms[:, :, BLK:].at[:, pattern_h].add(key_terms[:, :, :BLK]).astype(jnp.bfloat16)
    value_grad = value_terms[:, :, BLK:].at[:, pattern_h].add(value_terms[:, :, :BLK]).astype(jnp.bfloat16)
    return head_out, query_grad, key_grad, value_grad


def column_head(query_h, key_h, value_h, grad_h, offset_h):
    score_scale = HD ** -0.5
    query_full = query_h.astype(jnp.float32)
    grad_full = grad_h.astype(jnp.float32)
    key_moved = jnp.roll(key_h, offset_h, axis=1).astype(jnp.float32)
    value_moved = jnp.roll(value_h, offset_h, axis=1).astype(jnp.float32)
    scores = jnp.einsum('rcd,scd->crs', query_full, key_moved) * score_scale
    col_probs = jax.nn.softmax(scores, axis=-1)
    prob_half = half_and_back(col_probs)
    head_out = jnp.einsum('crs,scd->rcd', prob_half, value_moved).astype(jnp.bfloat16)
    value_terms = jnp.einsum('crs,rcd->scd', prob_half, grad_full)
    prob_grad = jnp.einsum('rcd,scd->crs', grad_full, value_moved)
    delta_sum = jnp.sum(col_probs * prob_grad, axis=-1, keepdims=True)
    score_grad = half_and_back(col_probs * (prob_grad - delta_sum))
    query_grad = (jnp.einsum('crs,scd->rcd', score_grad, key_moved) * score_scale).astype(jnp.bfloat16)
    key_terms = jnp.einsum('crs,rcd->scd', score_grad, query_full) * score_scale
    key_grad = jnp.roll(key_terms, -offset_h, axis=1).astype(jnp.bfloat16)
    value_grad = jnp.roll(value_terms, -offset_h, axis=1).astype(jnp.bfloat16)
    return head_out, query_grad, key_grad, value_grad


def one_sequence(query_seq, key_seq, value_seq, grad_seq, out_proj, block_pattern, col_offset):
    head_count = HR + HC
    grad_flat = grad_seq.reshape(GR * COLS, D)
    attn_grad = jnp.dot(grad_flat, out_proj.T, preferred_element_type=jnp.float32).astype(jnp.bfloat16)
    grad_heads = attn_grad.reshape(GR, COLS, head_count, HD)
    query_heads = query_seq.reshape(GR, COLS, head_count, HD)
    key_heads = key_seq.reshape(GR, COLS, head_count, HD)
    value_heads = value_seq.reshape(GR, COLS, head_count, HD)
    collected = ([], [], [], [])
    block_shape = (GR, NB, BLK, HD)
    for head_idx in range(HR):
        results = row_head(query_heads[:, :, head_idx].reshape(block_shape),
                           key_heads[:, :, head_idx].reshape(block_shape),
                           value_heads[:, :, head_idx].reshape(block_shape),
                           grad_heads[:, :, head_idx].reshape(block_shape),
                           block_pattern[head_idx])
        for target, result_part in zip(collected, results):
            target.append(result_part.reshape(GR, COLS, HD))
    for col_idx in range(HC):
        head_idx = HR + col_idx
        results = column_head(query_heads[:, :, head_idx], key_heads[:, :, head_idx],
                              value_heads[:, :, head_idx], grad_heads[:, :, head_idx],
                              col_offset[col_idx])
        for target, result_part in zip(collected, results):
            target.append(result_part)

    def merge_heads(pieces):
        return jnp.stack(pieces, axis=2).reshape(GR, COLS, head_count * HD)

    attention = merge_heads(collected[0])
    attn_flat = attention.reshape(GR * COLS, head_count * HD)
    layer_out = jnp.dot(attn_flat, out_proj, preferred_element_type=jnp.float32).astype(jnp.bfloat16).reshape(GR, COLS, D)
    grad_part = jnp.dot(attn_flat.T, grad_flat, preferred_element_type=jnp.float32)
    return layer_out, merge_heads(collected[1]), merge_heads(collected[2]), merge_heads(collected[3]), grad_part


def reference(queries, keys, values, out_proj, out_grad, block_pattern, col_offset):
    def per_sequence(inputs):
        return one_sequence(inputs[0], inputs[1], inputs[2], inputs[3], out_proj, block_pattern, col_offset)

    layer_out, q_grad, k_grad, v_grad, grad_parts = lax.map(per_sequence, (queries, keys, values, out_grad))
    w_grad = jnp.sum(grad_parts, axis=0) * (ALL_TOK ** -0.5)
    return layer_out, q_grad, k_grad, v_grad, w_grad
```

```python
import jax
import jax.numpy as jnp
from jax import lax
from jax.experimental import pallas as pl
from jax.experimental.pallas import tpu as pltpu
from jax.sharding import Mesh, PartitionSpec as P

HD = 128
HR = 4
HC = 4
BLK = 128
NB = 4
COLS = 512
HALF = HR * HD
D = 2048
DH = D // 2
SCALE = HD ** (-0.5)
BF = jnp.bfloat16
F32 = jnp.float32
GRP = 8
ROWS = 32
TILE = GRP * ROWS
VMEM_LIMIT = 50 * 1024 * 1024

DP = ("x", "zl")
SEQ = ("y", "zh", "c")


def mm(a, b):
    return lax.dot_general(a, b, (((1,), (0,)), ((), ())), preferred_element_type=F32)


def mm_t(a, b):
    return lax.dot_general(a, b, (((1,), (1,)), ((), ())), preferred_element_type=F32)


def t_mm(a, b):
    return lax.dot_general(a, b, (((0,), (0,)), ((), ())), preferred_element_type=F32)


def params():
    return pltpu.CompilerParams(vmem_limit_bytes=VMEM_LIMIT)


def cost(flops, nbytes, trans=0):
    return pl.CostEstimate(flops=int(flops), transcendentals=int(trans), bytes_accessed=int(nbytes))


SMEM_SPEC = pl.BlockSpec(memory_space=pltpu.SMEM)
VMEM_SPEC = pl.BlockSpec(memory_space=pltpu.VMEM)


def head(index):
    return slice(index * HD, (index + 1) * HD)


def shift_selector(offset):
    row = lax.broadcasted_iota(jnp.int32, (COLS, COLS), 0)
    col = lax.broadcasted_iota(jnp.int32, (COLS, COLS), 1)
    source = row - offset
    source = jnp.where(source < 0, source + COLS, source)
    return jnp.where(source == col, 1.0, 0.0).astype(BF)


def pack_kernel(off_ref, q_ref, k_ref, v_ref, o_ref):
    o_ref[:, :HALF] = q_ref[...]
    for h in range(HC):
        pair = jnp.concatenate([k_ref[:, head(h)], v_ref[:, head(h)]], axis=1)
        moved = mm(shift_selector(off_ref[h]), pair).astype(BF)
        o_ref[:, head(HC + h)] = moved[:, :HD]
        o_ref[:, head(2 * HC + h)] = moved[:, HD:]


def pack(q, k, v, offset):
    half = pl.BlockSpec((COLS, HALF), lambda i: (0, 1))
    return pl.pallas_call(
        pack_kernel,
        grid=(1,),
        out_shape=jax.ShapeDtypeStruct((COLS, 3 * HALF), BF),
        in_specs=[SMEM_SPEC, half, half, half],
        out_specs=pl.BlockSpec((COLS, 3 * HALF), lambda i: (0, 0)),
        compiler_params=params(),
        cost_estimate=cost(2 * COLS * COLS * 2 * HALF, 6 * COLS * HALF * 2),
        name="pack",
    )(offset, q, k, v)


def tile_of(ref, group, lane):
    tile = ref[:, group, :, lane * HD : (lane + 1) * HD]
    return tile.astype(F32).reshape(TILE, HD).astype(BF)


def store_tile(ref, group, lane, value):
    ref[:, group, :, lane * HD : (lane + 1) * HD] = value.reshape(ROWS, GRP, HD).astype(BF)


def column_mask():
    row = lax.broadcasted_iota(jnp.int32, (TILE, TILE), 0)
    col = lax.broadcasted_iota(jnp.int32, (TILE, TILE), 1)
    return lax.rem(row, GRP) == lax.rem(col, GRP)


def softmax(scores):
    e = jnp.exp(scores - jnp.max(scores, axis=-1, keepdims=True))
    return e / jnp.sum(e, axis=-1, keepdims=True)


def column_probs(r_ref, group, h, mask):
    q = tile_of(r_ref, group, h)
    k = tile_of(r_ref, group, HC + h)
    v = tile_of(r_ref, group, 2 * HC + h)
    return q, k, v, softmax(jnp.where(mask, mm_t(q, k) * SCALE, -1e30))


def column_forward_kernel(r_ref, o_ref):
    mask = column_mask()
    for group in range(2):
        for h in range(HC):
            _, _, v, probs = column_probs(r_ref, group, h, mask)
            store_tile(o_ref, group, h, mm(probs.astype(BF), v))


def column_forward(received):
    return pl.pallas_call(
        column_forward_kernel,
        out_shape=jax.ShapeDtypeStruct((ROWS, 2, GRP, HALF), BF),
        in_specs=[VMEM_SPEC],
        out_specs=VMEM_SPEC,
        compiler_params=params(),
        cost_estimate=cost(8 * 4 * TILE * TILE * HD, 4 * COLS * HALF * 2, 8 * TILE * TILE),
        name="column_forward",
    )(received)


def column_backward_kernel(r_ref, g_ref, o_ref):
    mask = column_mask()
    for group in range(2):
        for h in range(HC):
            q, k, v, probs = column_probs(r_ref, group, h, mask)
            g = tile_of(g_ref, group, h)
            store_tile(o_ref, group, 2 * HC + h, t_mm(probs.astype(BF), g))
            prob_grad = mm_t(g, v)
            delta = jnp.sum(probs * prob_grad, axis=-1, keepdims=True)
            score_grad = (probs * (prob_grad - delta)).astype(BF)
            store_tile(o_ref, group, h, mm(score_grad, k) * SCALE)
            store_tile(o_ref, group, HC + h, t_mm(score_grad, q) * SCALE)


def column_backward(received, grads):
    return pl.pallas_call(
        column_backward_kernel,
        out_shape=jax.ShapeDtypeStruct((ROWS, 2, GRP, 3 * HALF), BF),
        in_specs=[VMEM_SPEC, VMEM_SPEC],
        out_specs=VMEM_SPEC,
        compiler_params=params(),
        cost_estimate=cost(8 * 10 * TILE * TILE * HD, 7 * COLS * HALF * 2, 8 * TILE * TILE),
        name="column_backward",
    )(received, grads)


def row_tile(pat_ref, q_ref, k_ref, v_ref, h, j):
    block = slice(j * BLK, (j + 1) * BLK)
    other = pl.ds(pl.multiple_of(pat_ref[h, j] * BLK, BLK), BLK)
    q = q_ref[block, head(h)]
    k = jnp.concatenate([k_ref[other, head(h)], k_ref[block, head(h)]], axis=0)
    v = jnp.concatenate([v_ref[other, head(h)], v_ref[block, head(h)]], axis=0)
    return block, other, q, k, v, softmax(mm_t(q, k) * SCALE)


def row_forward_kernel(pat_ref, q_ref, k_ref, v_ref, o_ref):
    for h in range(HR):
        for j in range(NB):
            block, _, _, _, v, probs = row_tile(pat_ref, q_ref, k_ref, v_ref, h, j)
            o_ref[block, head(h)] = mm(probs.astype(BF), v).astype(BF)


def first_half():
    return pl.BlockSpec((COLS, HALF), lambda i: (0, 0))


def row_forward(q, k, v, pattern):
    return pl.pallas_call(
        row_forward_kernel,
        grid=(1,),
        out_shape=jax.ShapeDtypeStruct((COLS, HALF), BF),
        in_specs=[SMEM_SPEC, first_half(), first_half(), first_half()],
        out_specs=first_half(),
        compiler_params=params(),
        cost_estimate=cost(16 * 4 * BLK * 2 * BLK * HD, 4 * COLS * HALF * 2, 16 * BLK * 2 * BLK),
        name="row_forward",
    )(pattern, q, k, v)


def row_backward_kernel(pat_ref, q_ref, k_ref, v_ref, g_ref, dq_ref, dk_ref, dv_ref, own, moved):
    for h in range(HR):
        for j in range(NB):
            block, other, q, k, v, probs = row_tile(pat_ref, q_ref, k_ref, v_ref, h, j)
            g = g_ref[block, head(h)]
            value_terms = t_mm(probs.astype(BF), g)
            prob_grad = mm_t(g, v)
            delta = jnp.sum(probs * prob_grad, axis=-1, keepdims=True)
            score_grad = (probs * (prob_grad - delta)).astype(BF)
            dq_ref[block, head(h)] = (mm(score_grad, k) * SCALE).astype(BF)
            key_terms = t_mm(score_grad, q) * SCALE
            moved[0, other, :] = key_terms[:BLK]
            own[0, block, :] = key_terms[BLK:]
            moved[1, other, :] = value_terms[:BLK]
            own[1, block, :] = value_terms[BLK:]
        dk_ref[:, head(h)] = (own[0] + moved[0]).astype(BF)
        dv_ref[:, head(h)] = (own[1] + moved[1]).astype(BF)


def row_backward(q, k, v, g, pattern):
    whole = jax.ShapeDtypeStruct((COLS, 2 * HALF), BF)
    return pl.pallas_call(
        row_backward_kernel,
        grid=(1,),
        out_shape=(whole, whole, whole),
        in_specs=[SMEM_SPEC] + [first_half()] * 4,
        out_specs=(first_half(),) * 3,
        scratch_shapes=[pltpu.VMEM((2, COLS, HD), F32), pltpu.VMEM((2, COLS, HD), F32)],
        compiler_params=params(),
        cost_estimate=cost(16 * 10 * BLK * 2 * BLK * HD, 7 * COLS * HALF * 2, 16 * BLK * 2 * BLK),
        name="row_backward",
    )(pattern, q, k, v, g)


def finish_kernel(off_ref, b_ref, dq_in, dk_in, dv_in, dq_ref, dk_ref, dv_ref):
    dq_ref[...] = b_ref[:, :HALF]
    for h in range(HC):
        pair = jnp.concatenate([b_ref[:, head(HC + h)], b_ref[:, head(2 * HC + h)]], axis=1)
        back = t_mm(shift_selector(off_ref[h]), pair).astype(BF)
        dk_ref[:, head(h)] = back[:, :HD]
        dv_ref[:, head(h)] = back[:, HD:]


def finish(back, dq, dk, dv, offset):
    whole = jax.ShapeDtypeStruct((COLS, 2 * HALF), BF)
    kept = pl.BlockSpec(memory_space=pl.ANY)
    second = pl.BlockSpec((COLS, HALF), lambda i: (0, 1))
    return pl.pallas_call(
        finish_kernel,
        grid=(1,),
        out_shape=(whole, whole, whole),
        in_specs=[SMEM_SPEC, pl.BlockSpec((COLS, 3 * HALF), lambda i: (0, 0)), kept, kept, kept],
        out_specs=(second, second, second),
        input_output_aliases={2: 0, 3: 1, 4: 2},
        compiler_params=params(),
        cost_estimate=cost(2 * COLS * COLS * 2 * HALF, 6 * COLS * HALF * 2),
        name="finish",
    )(offset, back, dq, dk, dv)


def attn_grad_kernel(core_ref, og_mine, og_theirs, mine_ref, theirs_ref, o_ref):
    total = mm_t(og_mine[...], mine_ref[...]) + mm_t(og_theirs[...], theirs_ref[...])
    o_ref[...] = total.astype(BF)


def attn_grad_of(og, mine, theirs, core):
    steps = 4
    rows = 2 * HALF // steps
    return pl.pallas_call(
        attn_grad_kernel,
        grid_spec=pltpu.PrefetchScalarGridSpec(
            num_scalar_prefetch=1,
            grid=(steps,),
            in_specs=[
                pl.BlockSpec((COLS, DH), lambda i, c: (0, c[0])),
                pl.BlockSpec((COLS, DH), lambda i, c: (0, 1 - c[0])),
                pl.BlockSpec((rows, DH), lambda i, c: (i, 0)),
                pl.BlockSpec((rows, DH), lambda i, c: (i, 0)),
            ],
            out_specs=pl.BlockSpec((COLS, rows), lambda i, c: (0, i)),
        ),
        out_shape=jax.ShapeDtypeStruct((COLS, 2 * HALF), BF),
        compiler_params=params(),
        cost_estimate=cost(2 * COLS * 2 * HALF * D, 7 * 2**20),
        name="attn_grad",
    )(core, og, og, mine, theirs)


def layer_out_kernel(core_ref, row_ref, col_ref, mine_ref, theirs_ref, o_ref):
    def product(w_ref):
        total = mm(row_ref[...], w_ref[:HALF, :]) + mm(col_ref[...], w_ref[HALF:, :])
        o_ref[...] = total.astype(BF)

    pl.when(pl.program_id(0) == 0)(lambda: product(mine_ref))
    pl.when(pl.program_id(0) == 1)(lambda: product(theirs_ref))


def layer_out_of(row_out, col_out, mine, theirs, core):
    steps = 2
    width = DH // steps

    def place(half, i, c):
        which = jnp.where(half == 0, c[0], 1 - c[0])
        return (0, which * steps + i)

    return pl.pallas_call(
        layer_out_kernel,
        grid_spec=pltpu.PrefetchScalarGridSpec(
            num_scalar_prefetch=1,
            grid=(2, steps),
            in_specs=[
                pl.BlockSpec((COLS, HALF), lambda half, i, c: (0, 0)),
                pl.BlockSpec((COLS, HALF), lambda half, i, c: (0, 0)),
                pl.BlockSpec((2 * HALF, width), lambda half, i, c: (0, jnp.where(half == 0, i, steps - 1))),
                pl.BlockSpec((2 * HALF, width), lambda half, i, c: (0, jnp.where(half == 0, 0, i))),
            ],
            out_specs=pl.BlockSpec((COLS, width), place),
        ),
        out_shape=jax.ShapeDtypeStruct((COLS, D), BF),
        compiler_params=params(),
        cost_estimate=cost(2 * COLS * 2 * HALF * D, 7 * 2**20),
        name="layer_out",
    )(core, row_out, col_out, mine, theirs)


def weight_grad_kernel(core_ref, row_mine, row_theirs, col_mine, col_theirs, og_mine, og_theirs, o_ref):
    def product(a_ref, b_ref):
        o_ref[...] = (t_mm(a_ref[...], og_mine[...]) + t_mm(b_ref[...], og_theirs[...])).astype(BF)

    pl.when(pl.program_id(0) == 0)(lambda: product(row_mine, row_theirs))
    pl.when(pl.program_id(0) == 1)(lambda: product(col_mine, col_theirs))


def weight_grad_of(row_mine, row_theirs, col_mine, col_theirs, og, og_theirs, core):
    part = pl.BlockSpec((COLS, HALF), lambda i, c: (0, 0))
    return pl.pallas_call(
        weight_grad_kernel,
        grid_spec=pltpu.PrefetchScalarGridSpec(
            num_scalar_prefetch=1,
            grid=(2,),
            in_specs=[part] * 4
            + [
                pl.BlockSpec((COLS, DH), lambda i, c: (0, c[0])),
                pl.BlockSpec((COLS, DH), lambda i, c: (0, 0)),
            ],
            out_specs=pl.BlockSpec((HALF, DH), lambda i, c: (i, 0)),
        ),
        out_shape=jax.ShapeDtypeStruct((2 * HALF, DH), BF),
        compiler_params=params(),
        cost_estimate=cost(4 * COLS * 2 * HALF * DH, 6 * 2**20),
        name="weight_grad",
    )(core, row_mine, row_theirs, col_mine, col_theirs, og, og_theirs)


def exchange(tensor, axes):
    return lax.all_to_all(tensor, axes, split_axis=0, concat_axis=0, tiled=True)


def other_core(tensor):
    return lax.ppermute(tensor, "c", [(0, 1), (1, 0)])


def dp_shift(step, dx, dz):
    return [(x * dz + z, (x + step // dz) % dx * dz + (z + step % dz) % dz) for x in range(dx) for z in range(dz)]


def shards(queries, keys, values, out_proj, out_grad, block_pattern, col_offset):
    q, k, v = (t.reshape(COLS, 2 * HALF) for t in (queries, keys, values))
    og = out_grad.reshape(COLS, D)
    rows_of = out_proj.shape[0]
    seq = ROWS
    chips = seq // 2
    dp = lax.axis_size("x") * lax.axis_size("zl")
    core_index = lax.axis_index("c")
    core = core_index.astype(jnp.int32).reshape(1)

    halves = out_proj.reshape(rows_of, 2, DH).transpose(1, 0, 2)
    spread = jnp.broadcast_to(halves[None], (chips, 2, rows_of, DH)).reshape(seq, rows_of, DH)
    own_rows = exchange(spread, SEQ).reshape(seq * rows_of, DH)
    mine = lax.all_gather(own_rows, DP, axis=0, tiled=True)
    theirs = other_core(mine)

    packed = pack(q, k, v, col_offset)
    received = exchange(packed.reshape(seq, COLS // seq, 3 * HALF), SEQ)
    received = received.reshape(ROWS, 2, GRP, 3 * HALF)

    og_sent = lax.dynamic_slice(og, (0, (1 - core_index) * DH), (COLS, DH))
    og_theirs = other_core(og_sent)
    row_out = row_forward(q, k, v, block_pattern)
    row_theirs = other_core(row_out)

    col_sent = column_forward(received).reshape(seq, COLS // seq, HALF)
    col_out = exchange(col_sent, SEQ).reshape(COLS, HALF)
    col_theirs = other_core(col_out)

    grads = attn_grad_of(og, mine, theirs, core)
    col_grads = exchange(grads[:, HALF:].reshape(seq, COLS // seq, HALF), SEQ)
    col_grads = col_grads.reshape(ROWS, 2, GRP, HALF)

    weight_part = weight_grad_of(row_out, row_theirs, col_out, col_theirs, og, og_theirs, core)
    weight_dp = exchange(weight_part.reshape(dp, 2 * HALF // dp, DH), DP)
    weight_dp = jnp.sum(weight_dp.astype(F32), axis=0).astype(BF)
    weight_seq = exchange(weight_dp.reshape(seq, rows_of, DH), SEQ)
    weight_sum = jnp.sum(weight_seq.astype(F32).reshape(chips, 2, rows_of, DH), axis=0)
    tokens = COLS * seq * dp
    w_grad = weight_sum.transpose(1, 0, 2).reshape(rows_of, D) * tokens ** (-0.5)

    dq, dk, dv = row_backward(q, k, v, grads, block_pattern)
    col_back = column_backward(received, col_grads).reshape(seq, COLS // seq, 3 * HALF)
    back = exchange(col_back, SEQ).reshape(COLS, 3 * HALF)
    dq, dk, dv = finish(back, dq, dk, dv, col_offset)

    layer = layer_out_of(row_out, col_out, mine, theirs, core)
    lead = (1, 1, COLS)
    return (
        layer.reshape(lead + (D,)),
        dq.reshape(lead + (2 * HALF,)),
        dk.reshape(lead + (2 * HALF,)),
        dv.reshape(lead + (2 * HALF,)),
        w_grad,
    )


def solution(mesh):
    fine = Mesh(mesh.devices.reshape(4, 2, 4, 4, 2), DP + SEQ)
    token = P(DP, SEQ, None, None)
    rows = P(DP + SEQ, None)
    in_specs = (token, token, token, rows, token, P(), P())
    out_specs = (token, token, token, token, rows)
    return jax.shard_map(shards, mesh=fine, in_specs=in_specs, out_specs=out_specs, check_vma=False)
```

```python
import jax
import jax.numpy as jnp
from jax import lax
from jax.experimental import pallas as pl
from jax.experimental.pallas import tpu as pltpu
from jax.sharding import Mesh, PartitionSpec as P

HD = 128
HR = 4
HC = 4
BLK = 128
NB = 4
COLS = 512
HALF = HR * HD
D = 2048
DH = D // 2
SCALE = HD ** (-0.5)
BF = jnp.bfloat16
F32 = jnp.float32
GRP = 8
ROWS = 32
TILE = GRP * ROWS
VMEM_LIMIT = 50 * 1024 * 1024

DP = ("x", "zl")
SEQ = ("y", "zh", "c")


def mm(a, b):
    return lax.dot_general(a, b, (((1,), (0,)), ((), ())), preferred_element_type=F32)


def mm_t(a, b):
    return lax.dot_general(a, b, (((1,), (1,)), ((), ())), preferred_element_type=F32)


def t_mm(a, b):
    return lax.dot_general(a, b, (((0,), (0,)), ((), ())), preferred_element_type=F32)


def params():
    return pltpu.CompilerParams(vmem_limit_bytes=VMEM_LIMIT)


def cost(flops, nbytes, trans=0):
    return pl.CostEstimate(flops=int(flops), transcendentals=int(trans), bytes_accessed=int(nbytes))


SMEM_SPEC = pl.BlockSpec(memory_space=pltpu.SMEM)
VMEM_SPEC = pl.BlockSpec(memory_space=pltpu.VMEM)


def head(index):
    return slice(index * HD, (index + 1) * HD)


def shift_selector(offset):
    row = lax.broadcasted_iota(jnp.int32, (COLS, COLS), 0)
    col = lax.broadcasted_iota(jnp.int32, (COLS, COLS), 1)
    source = row - offset
    source = jnp.where(source < 0, source + COLS, source)
    return jnp.where(source == col, 1.0, 0.0).astype(BF)


def pack_kernel(off_ref, q_ref, k_ref, v_ref, o_ref):
    o_ref[:, :HALF] = q_ref[...]
    for h in range(HC):
        pair = jnp.concatenate([k_ref[:, head(h)], v_ref[:, head(h)]], axis=1)
        moved = mm(shift_selector(off_ref[h]), pair).astype(BF)
        o_ref[:, head(HC + h)] = moved[:, :HD]
        o_ref[:, head(2 * HC + h)] = moved[:, HD:]


def pack(q, k, v, offset):
    half = pl.BlockSpec((COLS, HALF), lambda i: (0, 1))
    return pl.pallas_call(
        pack_kernel,
        grid=(1,),
        out_shape=jax.ShapeDtypeStruct((COLS, 3 * HALF), BF),
        in_specs=[SMEM_SPEC, half, half, half],
        out_specs=pl.BlockSpec((COLS, 3 * HALF), lambda i: (0, 0)),
        compiler_params=params(),
        cost_estimate=cost(2 * COLS * COLS * 2 * HALF, 6 * COLS * HALF * 2),
        name="pack",
    )(offset, q, k, v)


def tile_of(ref, group, lane):
    tile = ref[:, group, :, lane * HD : (lane + 1) * HD]
    return tile.astype(F32).reshape(TILE, HD).astype(BF)


def store_tile(ref, group, lane, value):
    ref[:, group, :, lane * HD : (lane + 1) * HD] = value.reshape(ROWS, GRP, HD).astype(BF)


def column_mask():
    row = lax.broadcasted_iota(jnp.int32, (TILE, TILE), 0)
    col = lax.broadcasted_iota(jnp.int32, (TILE, TILE), 1)
    return lax.rem(row, GRP) == lax.rem(col, GRP)


def softmax(scores):
    e = jnp.exp(scores - jnp.max(scores, axis=-1, keepdims=True))
    return e / jnp.sum(e, axis=-1, keepdims=True)


def column_probs(r_ref, group, h, mask):
    q = tile_of(r_ref, group, h)
    k = tile_of(r_ref, group, HC + h)
    v = tile_of(r_ref, group, 2 * HC + h)
    return q, k, v, softmax(jnp.where(mask, mm_t(q, k) * SCALE, -1e30))


def column_forward_kernel(r_ref, kept_ref, o_ref):
    mask = column_mask()
    for group in range(2):
        for h in range(HC):
            _, _, v, probs = column_probs(r_ref, group, h, mask)
            store_tile(o_ref, group, h, mm(probs.astype(BF), v))


def column_forward(received, send):
    return pl.pallas_call(
        column_forward_kernel,
        grid=(1,),
        out_shape=jax.ShapeDtypeStruct((ROWS, 2, GRP, 2 * HALF), BF),
        in_specs=[
            pl.BlockSpec((ROWS, 2, GRP, 3 * HALF), lambda i: (0, 0, 0, 0)),
            pl.BlockSpec(memory_space=pl.ANY),
        ],
        out_specs=pl.BlockSpec((ROWS, 2, GRP, HALF), lambda i: (0, 0, 0, 0)),
        input_output_aliases={1: 0},
        compiler_params=params(),
        cost_estimate=cost(8 * 4 * TILE * TILE * HD, 4 * COLS * HALF * 2, 8 * TILE * TILE),
        name="column_forward",
    )(received, send)


def column_backward_kernel(r_ref, g_ref, o_ref):
    mask = column_mask()
    for group in range(2):
        for h in range(HC):
            q, k, v, probs = column_probs(r_ref, group, h, mask)
            g = tile_of(g_ref, group, h)
            store_tile(o_ref, group, 2 * HC + h, t_mm(probs.astype(BF), g))
            prob_grad = mm_t(g, v)
            delta = jnp.sum(probs * prob_grad, axis=-1, keepdims=True)
            score_grad = (probs * (prob_grad - delta)).astype(BF)
            store_tile(o_ref, group, h, mm(score_grad, k) * SCALE)
            store_tile(o_ref, group, HC + h, t_mm(score_grad, q) * SCALE)


def column_backward(received, grads):
    return pl.pallas_call(
        column_backward_kernel,
        grid=(1,),
        out_shape=jax.ShapeDtypeStruct((ROWS, 2, GRP, 3 * HALF), BF),
        in_specs=[
            pl.BlockSpec((ROWS, 2, GRP, 3 * HALF), lambda i: (0, 0, 0, 0)),
            pl.BlockSpec((ROWS, 2, GRP, HALF), lambda i: (0, 0, 0, 1)),
        ],
        out_specs=pl.BlockSpec((ROWS, 2, GRP, 3 * HALF), lambda i: (0, 0, 0, 0)),
        compiler_params=params(),
        cost_estimate=cost(8 * 10 * TILE * TILE * HD, 7 * COLS * HALF * 2, 8 * TILE * TILE),
        name="column_backward",
    )(received, grads)


def row_tile(pat_ref, q_ref, k_ref, v_ref, h, j):
    block = slice(j * BLK, (j + 1) * BLK)
    other = pl.ds(pl.multiple_of(pat_ref[h, j] * BLK, BLK), BLK)
    q = q_ref[block, head(h)]
    k = jnp.concatenate([k_ref[other, head(h)], k_ref[block, head(h)]], axis=0)
    v = jnp.concatenate([v_ref[other, head(h)], v_ref[block, head(h)]], axis=0)
    return block, other, q, k, v, softmax(mm_t(q, k) * SCALE)


def row_forward_kernel(pat_ref, q_ref, k_ref, v_ref, o_ref):
    for h in range(HR):
        for j in range(NB):
            block, _, _, _, v, probs = row_tile(pat_ref, q_ref, k_ref, v_ref, h, j)
            o_ref[block, head(h)] = mm(probs.astype(BF), v).astype(BF)


def first_half():
    return pl.BlockSpec((COLS, HALF), lambda i: (0, 0))


def row_forward(q, k, v, pattern):
    return pl.pallas_call(
        row_forward_kernel,
        grid=(1,),
        out_shape=jax.ShapeDtypeStruct((COLS, HALF), BF),
        in_specs=[SMEM_SPEC, first_half(), first_half(), first_half()],
        out_specs=first_half(),
        compiler_params=params(),
        cost_estimate=cost(16 * 4 * BLK * 2 * BLK * HD, 4 * COLS * HALF * 2, 16 * BLK * 2 * BLK),
        name="row_forward",
    )(pattern, q, k, v)


def row_backward_kernel(pat_ref, q_ref, k_ref, v_ref, g_ref, dq_ref, dk_ref, dv_ref, own, moved):
    for h in range(HR):
        for j in range(NB):
            block, other, q, k, v, probs = row_tile(pat_ref, q_ref, k_ref, v_ref, h, j)
            g = g_ref[block, head(h)]
            value_terms = t_mm(probs.astype(BF), g)
            prob_grad = mm_t(g, v)
            delta = jnp.sum(probs * prob_grad, axis=-1, keepdims=True)
            score_grad = (probs * (prob_grad - delta)).astype(BF)
            dq_ref[block, head(h)] = (mm(score_grad, k) * SCALE).astype(BF)
            key_terms = t_mm(score_grad, q) * SCALE
            moved[0, other, :] = key_terms[:BLK]
            own[0, block, :] = key_terms[BLK:]
            moved[1, other, :] = value_terms[:BLK]
            own[1, block, :] = value_terms[BLK:]
        dk_ref[:, head(h)] = (own[0] + moved[0]).astype(BF)
        dv_ref[:, head(h)] = (own[1] + moved[1]).astype(BF)


def row_backward(q, k, v, g, pattern):
    whole = jax.ShapeDtypeStruct((COLS, 2 * HALF), BF)
    return pl.pallas_call(
        row_backward_kernel,
        grid=(1,),
        out_shape=(whole, whole, whole),
        in_specs=[SMEM_SPEC] + [first_half()] * 4,
        out_specs=(first_half(),) * 3,
        scratch_shapes=[pltpu.VMEM((2, COLS, HD), F32), pltpu.VMEM((2, COLS, HD), F32)],
        compiler_params=params(),
        cost_estimate=cost(16 * 10 * BLK * 2 * BLK * HD, 7 * COLS * HALF * 2, 16 * BLK * 2 * BLK),
        name="row_backward",
    )(pattern, q, k, v, g)


def finish_kernel(off_ref, b_ref, dq_in, dk_in, dv_in, dq_ref, dk_ref, dv_ref):
    dq_ref[...] = b_ref[:, :HALF]
    for h in range(HC):
        pair = jnp.concatenate([b_ref[:, head(HC + h)], b_ref[:, head(2 * HC + h)]], axis=1)
        back = t_mm(shift_selector(off_ref[h]), pair).astype(BF)
        dk_ref[:, head(h)] = back[:, :HD]
        dv_ref[:, head(h)] = back[:, HD:]


def finish(back, dq, dk, dv, offset):
    whole = jax.ShapeDtypeStruct((COLS, 2 * HALF), BF)
    kept = pl.BlockSpec(memory_space=pl.ANY)
    second = pl.BlockSpec((COLS, HALF), lambda i: (0, 1))
    return pl.pallas_call(
        finish_kernel,
        grid=(1,),
        out_shape=(whole, whole, whole),
        in_specs=[SMEM_SPEC, pl.BlockSpec((COLS, 3 * HALF), lambda i: (0, 0)), kept, kept, kept],
        out_specs=(second, second, second),
        input_output_aliases={2: 0, 3: 1, 4: 2},
        compiler_params=params(),
        cost_estimate=cost(2 * COLS * COLS * 2 * HALF, 6 * COLS * HALF * 2),
        name="finish",
    )(offset, back, dq, dk, dv)


def attn_grad_kernel(place, og_mine, og_theirs, mine_ref, theirs_ref, row_ref, send_ref):
    total = (mm_t(og_mine[...], mine_ref[...]) + mm_t(og_theirs[...], theirs_ref[...])).astype(BF)

    @pl.when(pl.program_id(0) < 2)
    def _():
        row_ref[...] = total

    @pl.when(pl.program_id(0) >= 2)
    def _():
        send_ref[...] = total


def attn_grad_of(og, mine, theirs, place):
    steps = 4
    rows = 2 * HALF // steps
    return pl.pallas_call(
        attn_grad_kernel,
        grid_spec=pltpu.PrefetchScalarGridSpec(
            num_scalar_prefetch=1,
            grid=(steps,),
            in_specs=[
                pl.BlockSpec((COLS, DH), lambda i, at: (0, at[0])),
                pl.BlockSpec((COLS, DH), lambda i, at: (0, 1 - at[0])),
                pl.BlockSpec((rows, DH), lambda i, at: (i, 0)),
                pl.BlockSpec((rows, DH), lambda i, at: (i, 0)),
            ],
            out_specs=(
                pl.BlockSpec((COLS, rows), lambda i, at: (0, jnp.minimum(i, 1))),
                pl.BlockSpec((COLS, rows), lambda i, at: (0, jnp.maximum(i, 2))),
            ),
        ),
        out_shape=(jax.ShapeDtypeStruct((COLS, HALF), BF), jax.ShapeDtypeStruct((COLS, 2 * HALF), BF)),
        compiler_params=params(),
        cost_estimate=cost(2 * COLS * 2 * HALF * D, 7 * 2**20),
        name="attn_grad",
    )(place, og, og, mine, theirs)


def layer_out_kernel(core_ref, row_ref, col_ref, mine_ref, theirs_ref, o_ref):
    def product(w_ref):
        total = mm(row_ref[...], w_ref[:HALF, :]) + mm(col_ref[...], w_ref[HALF:, :])
        o_ref[...] = total.astype(BF)

    pl.when(pl.program_id(0) == 0)(lambda: product(mine_ref))
    pl.when(pl.program_id(0) == 1)(lambda: product(theirs_ref))


def layer_out_of(row_out, col_out, mine, theirs, core):
    steps = 2
    width = DH // steps

    def place(half, i, c):
        which = jnp.where(half == 0, c[0], 1 - c[0])
        return (0, which * steps + i)

    return pl.pallas_call(
        layer_out_kernel,
        grid_spec=pltpu.PrefetchScalarGridSpec(
            num_scalar_prefetch=1,
            grid=(2, steps),
            in_specs=[
                pl.BlockSpec((COLS, HALF), lambda half, i, c: (0, 0)),
                pl.BlockSpec((COLS, HALF), lambda half, i, c: (0, 0)),
                pl.BlockSpec((2 * HALF, width), lambda half, i, c: (0, jnp.where(half == 0, i, steps - 1))),
                pl.BlockSpec((2 * HALF, width), lambda half, i, c: (0, jnp.where(half == 0, 0, i))),
            ],
            out_specs=pl.BlockSpec((COLS, width), place),
        ),
        out_shape=jax.ShapeDtypeStruct((COLS, D), BF),
        compiler_params=params(),
        cost_estimate=cost(2 * COLS * 2 * HALF * D, 7 * 2**20),
        name="layer_out",
    )(core, row_out, col_out, mine, theirs)


def weight_grad_kernel(place, row_mine, row_theirs, col_mine, col_theirs, og_mine, og_theirs, *refs):
    outs, total = refs[:4], refs[4]
    step = pl.program_id(0)
    block = lax.rem(place[1] + step, 4)

    def product(a_ref, b_ref):
        total[...] = t_mm(a_ref[...], og_mine[...]) + t_mm(b_ref[...], og_theirs[...])

    pl.when(block < 2)(lambda: product(row_mine, row_theirs))
    pl.when(block >= 2)(lambda: product(col_mine, col_theirs))
    for target, out in enumerate(outs):

        @pl.when(step == target)
        def _(out=out):
            out[...] = total[...].astype(out.dtype)


def weight_grad_of(row_mine, row_theirs, col_mine, col_theirs, og, og_theirs, place):
    rows = 2 * HALF // 4

    def row_block(i, at):
        return (0, jnp.minimum(lax.rem(at[1] + i, 4), 1))

    def col_block(i, at):
        return (0, jnp.maximum(lax.rem(at[1] + i, 4), 2) - 2)

    return pl.pallas_call(
        weight_grad_kernel,
        grid_spec=pltpu.PrefetchScalarGridSpec(
            num_scalar_prefetch=1,
            grid=(4,),
            in_specs=[
                pl.BlockSpec((COLS, rows), row_block),
                pl.BlockSpec((COLS, rows), row_block),
                pl.BlockSpec((COLS, rows), col_block),
                pl.BlockSpec((COLS, rows), col_block),
                pl.BlockSpec((COLS, DH), lambda i, at: (0, at[0])),
                pl.BlockSpec((COLS, DH), lambda i, at: (0, 0)),
            ],
            out_specs=(pl.BlockSpec((rows, DH), lambda i, at: (0, 0)),) * 4,
            scratch_shapes=[pltpu.VMEM((rows, DH), F32)],
        ),
        out_shape=(jax.ShapeDtypeStruct((rows, DH), F32),) + (jax.ShapeDtypeStruct((rows, DH), BF),) * 3,
        compiler_params=params(),
        cost_estimate=cost(4 * COLS * 2 * HALF * DH, 7 * 2**20),
        name="weight_grad",
    )(place, row_mine, row_theirs, col_mine, col_theirs, og, og_theirs)


def weight_sum_kernel(place, a_ref, b_ref, c_ref, d_ref, keep_ref, send_ref):
    half = keep_ref.shape[0]

    def total(index):
        rows = pl.ds(pl.multiple_of(index * half, half), half)
        return (a_ref[rows, :] + b_ref[rows, :].astype(F32)) + (c_ref[rows, :].astype(F32) + d_ref[rows, :].astype(F32))

    keep_ref[...] = total(place[2])
    send_ref[...] = total(1 - place[2]).astype(BF)


def weight_sum(parts, place):
    half = parts[0].shape[0] // 2
    return pl.pallas_call(
        weight_sum_kernel,
        out_shape=(jax.ShapeDtypeStruct((half, DH), F32), jax.ShapeDtypeStruct((half, DH), BF)),
        in_specs=[SMEM_SPEC] + [VMEM_SPEC] * 4,
        out_specs=(VMEM_SPEC, VMEM_SPEC),
        compiler_params=params(),
        cost_estimate=cost(8 * half * DH, 4 * 2**20),
        name="weight_sum",
    )(place, *parts)


def exchange(tensor, axes):
    return lax.all_to_all(tensor, axes, split_axis=0, concat_axis=0, tiled=True)


def other_core(tensor):
    return lax.ppermute(tensor, "c", [(0, 1), (1, 0)])


def together(*values):
    return lax.optimization_barrier(values)


def other_z(tensor):
    return lax.ppermute(tensor, "zl", [(0, 1), (1, 0)])


def along_x(tensor, step):
    return lax.ppermute(tensor, "x", [(i, (i + step) % 4) for i in range(4)])


def shards(queries, keys, values, out_proj, out_grad, block_pattern, col_offset):
    q, k, v = (t.reshape(COLS, 2 * HALF) for t in (queries, keys, values))
    og = out_grad.reshape(COLS, D)
    rows_of = out_proj.shape[0]
    seq = ROWS
    chips = seq // 2
    dp = lax.axis_size("x") * lax.axis_size("zl")
    core, at_x, at_z = (lax.axis_index(name).astype(jnp.int32) for name in ("c", "x", "zl"))
    place = jnp.stack([core, at_x, at_z])

    z_proj = other_z(out_proj)
    first = at_z == 0
    pair = jnp.stack([jnp.where(first, out_proj, z_proj), jnp.where(first, z_proj, out_proj)])
    halves = pair.reshape(2 * rows_of, 2, DH).transpose(1, 0, 2)
    spread = jnp.broadcast_to(halves[None], (chips, 2, 2 * rows_of, DH)).reshape(seq, 2 * rows_of, DH)
    own_rows = exchange(spread, SEQ)
    packed = pack(q, k, v, col_offset)
    own_rows, packed = together(own_rows, packed)
    own_rows = own_rows.reshape(seq, 2, rows_of, DH).transpose(1, 0, 2, 3).reshape(2 * seq * rows_of, DH)
    mine = lax.all_gather(own_rows, "x", axis=0, tiled=True)
    theirs = other_core(mine)

    received = exchange(packed.reshape(seq, COLS // seq, 3 * HALF), SEQ)
    og_sent = lax.dynamic_slice(og, (0, (1 - core) * DH), (COLS, DH))
    og_theirs = other_core(og_sent)
    row_out = row_forward(q, k, v, block_pattern)
    row_theirs = other_core(row_out)
    grad_rows, send = attn_grad_of(og, mine, theirs, place)
    received, row_out, row_theirs, og_theirs, send = together(received, row_out, row_theirs, og_theirs, send)
    received = received.reshape(ROWS, 2, GRP, 3 * HALF)

    send = column_forward(received, send.reshape(ROWS, 2, GRP, 2 * HALF))
    mixed = exchange(send.reshape(seq, COLS // seq, 2 * HALF), SEQ)
    dq, dk, dv = row_backward(q, k, v, grad_rows, block_pattern)
    mixed, dq, dk, dv = together(mixed, dq, dk, dv)

    col_mine = mixed.reshape(COLS, 2 * HALF)
    col_theirs = other_core(col_mine)
    col_back = column_backward(received, mixed.reshape(ROWS, 2, GRP, 2 * HALF)).reshape(seq, COLS // seq, 3 * HALF)
    col_back, col_mine, col_theirs = together(col_back, col_mine, col_theirs)
    back = exchange(col_back, SEQ).reshape(COLS, 3 * HALF)

    parts = weight_grad_of(row_out, row_theirs, col_mine, col_theirs, og, og_theirs, place)
    parts = [parts[0]] + [along_x(parts[step], step) for step in (1, 2, 3)]
    keep, give = weight_sum(parts, place)
    weight_part = (keep + other_z(give).astype(F32)).astype(BF).reshape(seq, rows_of, DH)
    weight_part, back = together(weight_part, back)
    weight_seq = exchange(weight_part, SEQ)
    weight_total = jnp.sum(weight_seq.astype(F32).reshape(chips, 2, rows_of, DH), axis=0)
    tokens = COLS * seq * dp
    w_grad = weight_total.transpose(1, 0, 2).reshape(rows_of, D) * tokens ** (-0.5)

    dq, dk, dv = finish(back, dq, dk, dv, col_offset)

    layer = layer_out_of(row_out, col_mine, mine, theirs, place)
    lead = (1, 1, COLS)
    return (
        layer.reshape(lead + (D,)),
        dq.reshape(lead + (2 * HALF,)),
        dk.reshape(lead + (2 * HALF,)),
        dv.reshape(lead + (2 * HALF,)),
        w_grad,
    )


def solution(mesh):
    fine = Mesh(mesh.devices.reshape(4, 2, 4, 4, 2), DP + SEQ)
    token = P(DP, SEQ, None, None)
    rows = P(DP + SEQ, None)
    in_specs = (token, token, token, rows, token, P(), P())
    out_specs = (token, token, token, token, rows)
    return jax.shard_map(shards, mesh=fine, in_specs=in_specs, out_specs=out_specs, check_vma=False)
```

```python
import jax
import jax.numpy as jnp
from jax import lax
from jax.experimental import pallas as pl
from jax.experimental.pallas import tpu as pltpu
from jax.sharding import Mesh, PartitionSpec as P

HD = 128
HR = 4
HC = 4
BLK = 128
NB = 4
COLS = 512
HALF = HR * HD
D = 2048
DH = D // 2
SCALE = HD ** (-0.5)
BF = jnp.bfloat16
F32 = jnp.float32
GRP = 8
ROWS = 32
TILE = GRP * ROWS
VMEM_LIMIT = 50 * 1024 * 1024

DP = ("x", "zl")
SEQ = ("y", "zh", "c")
NEAR = ("zl", "zh", "c")


def mm(a, b):
    return lax.dot_general(a, b, (((1,), (0,)), ((), ())), preferred_element_type=F32)


def mm_t(a, b):
    return lax.dot_general(a, b, (((1,), (1,)), ((), ())), preferred_element_type=F32)


def t_mm(a, b):
    return lax.dot_general(a, b, (((0,), (0,)), ((), ())), preferred_element_type=F32)


def params():
    return pltpu.CompilerParams(vmem_limit_bytes=VMEM_LIMIT)


def cost(flops, nbytes, trans=0):
    return pl.CostEstimate(flops=int(flops), transcendentals=int(trans), bytes_accessed=int(nbytes))


SMEM_SPEC = pl.BlockSpec(memory_space=pltpu.SMEM)
VMEM_SPEC = pl.BlockSpec(memory_space=pltpu.VMEM)


def head(index):
    return slice(index * HD, (index + 1) * HD)


def shift_selector(offset):
    row = lax.broadcasted_iota(jnp.int32, (COLS, COLS), 0)
    col = lax.broadcasted_iota(jnp.int32, (COLS, COLS), 1)
    source = row - offset
    source = jnp.where(source < 0, source + COLS, source)
    return jnp.where(source == col, 1.0, 0.0).astype(BF)


def pack_kernel(off_ref, q_ref, k_ref, v_ref, o_ref):
    o_ref[:, :HALF] = q_ref[...]
    for h in range(HC):
        pair = jnp.concatenate([k_ref[:, head(h)], v_ref[:, head(h)]], axis=1)
        moved = mm(shift_selector(off_ref[h]), pair).astype(BF)
        o_ref[:, head(HC + h)] = moved[:, :HD]
        o_ref[:, head(2 * HC + h)] = moved[:, HD:]


def pack(q, k, v, offset):
    half = pl.BlockSpec((COLS, HALF), lambda i: (0, 1))
    return pl.pallas_call(
        pack_kernel,
        grid=(1,),
        out_shape=jax.ShapeDtypeStruct((COLS, 3 * HALF), BF),
        in_specs=[SMEM_SPEC, half, half, half],
        out_specs=pl.BlockSpec((COLS, 3 * HALF), lambda i: (0, 0)),
        compiler_params=params(),
        cost_estimate=cost(2 * COLS * COLS * 2 * HALF, 6 * COLS * HALF * 2),
        name="pack",
    )(offset, q, k, v)


def tile_of(ref, lane):
    tile = ref[:, 0, :, lane * HD : (lane + 1) * HD]
    return tile.astype(F32).reshape(TILE, HD).astype(BF)


def store_tile(ref, lane, value):
    ref[:, 0, :, lane * HD : (lane + 1) * HD] = value.reshape(ROWS, GRP, HD).astype(BF)


def column_mask():
    row = lax.broadcasted_iota(jnp.int32, (TILE, TILE), 0)
    col = lax.broadcasted_iota(jnp.int32, (TILE, TILE), 1)
    return lax.rem(row, GRP) == lax.rem(col, GRP)


def softmax(scores):
    e = jnp.exp(scores - jnp.max(scores, axis=-1, keepdims=True))
    return e / jnp.sum(e, axis=-1, keepdims=True)


def column_probs(r_ref, h, mask):
    q = tile_of(r_ref, h)
    k = tile_of(r_ref, HC + h)
    v = tile_of(r_ref, 2 * HC + h)
    return q, k, v, softmax(jnp.where(mask, mm_t(q, k) * SCALE, -1e30))


def column_forward_kernel(r_ref, g_ref, o_ref):
    mask = column_mask()
    o_ref[:, :, :, HALF:] = g_ref[...]
    for h in range(HC):
        _, _, v, probs = column_probs(r_ref, h, mask)
        store_tile(o_ref, h, mm(probs.astype(BF), v))


def group_block(lanes, part=0):
    return pl.BlockSpec((ROWS, 1, GRP, lanes), lambda i: (0, i, 0, part))


def column_forward(received, grads):
    return pl.pallas_call(
        column_forward_kernel,
        grid=(2,),
        out_shape=jax.ShapeDtypeStruct((ROWS, 2, GRP, 2 * HALF), BF),
        in_specs=[group_block(3 * HALF), group_block(HALF)],
        out_specs=group_block(2 * HALF),
        compiler_params=params(),
        cost_estimate=cost(8 * 4 * TILE * TILE * HD, 4 * COLS * HALF * 2, 8 * TILE * TILE),
        name="column_forward",
    )(received, grads)


def column_backward_kernel(r_ref, g_ref, o_ref):
    mask = column_mask()
    for h in range(HC):
        q, k, v, probs = column_probs(r_ref, h, mask)
        g = tile_of(g_ref, h)
        store_tile(o_ref, 2 * HC + h, t_mm(probs.astype(BF), g))
        prob_grad = mm_t(g, v)
        delta = jnp.sum(probs * prob_grad, axis=-1, keepdims=True)
        score_grad = (probs * (prob_grad - delta)).astype(BF)
        store_tile(o_ref, h, mm(score_grad, k) * SCALE)
        store_tile(o_ref, HC + h, t_mm(score_grad, q) * SCALE)


def column_backward(received, mixed):
    return pl.pallas_call(
        column_backward_kernel,
        grid=(2,),
        out_shape=jax.ShapeDtypeStruct((ROWS, 2, GRP, 3 * HALF), BF),
        in_specs=[group_block(3 * HALF), group_block(HALF, 1)],
        out_specs=group_block(3 * HALF),
        compiler_params=params(),
        cost_estimate=cost(8 * 10 * TILE * TILE * HD, 7 * COLS * HALF * 2, 8 * TILE * TILE),
        name="column_backward",
    )(received, mixed)


def row_tile(pat_ref, q_ref, k_ref, v_ref, h, j):
    block = slice(j * BLK, (j + 1) * BLK)
    other = pl.ds(pl.multiple_of(pat_ref[h, j] * BLK, BLK), BLK)
    q = q_ref[block, head(h)]
    k = jnp.concatenate([k_ref[other, head(h)], k_ref[block, head(h)]], axis=0)
    v = jnp.concatenate([v_ref[other, head(h)], v_ref[block, head(h)]], axis=0)
    return block, other, q, k, v, softmax(mm_t(q, k) * SCALE)


def row_forward_kernel(pat_ref, q_ref, k_ref, v_ref, o_ref):
    for h in range(HR):
        for j in range(NB):
            block, _, _, _, v, probs = row_tile(pat_ref, q_ref, k_ref, v_ref, h, j)
            o_ref[block, head(h)] = mm(probs.astype(BF), v).astype(BF)


def first_half():
    return pl.BlockSpec((COLS, HALF), lambda i: (0, 0))


def row_forward(q, k, v, pattern):
    return pl.pallas_call(
        row_forward_kernel,
        grid=(1,),
        out_shape=jax.ShapeDtypeStruct((COLS, HALF), BF),
        in_specs=[SMEM_SPEC, first_half(), first_half(), first_half()],
        out_specs=first_half(),
        compiler_params=params(),
        cost_estimate=cost(16 * 4 * BLK * 2 * BLK * HD, 4 * COLS * HALF * 2, 16 * BLK * 2 * BLK),
        name="row_forward",
    )(pattern, q, k, v)


def row_backward_kernel(pat_ref, q_ref, k_ref, v_ref, g_ref, dq_ref, dk_ref, dv_ref, own, moved):
    for h in range(HR):
        for j in range(NB):
            block, other, q, k, v, probs = row_tile(pat_ref, q_ref, k_ref, v_ref, h, j)
            g = g_ref[block, head(h)]
            value_terms = t_mm(probs.astype(BF), g)
            prob_grad = mm_t(g, v)
            delta = jnp.sum(probs * prob_grad, axis=-1, keepdims=True)
            score_grad = (probs * (prob_grad - delta)).astype(BF)
            dq_ref[block, head(h)] = (mm(score_grad, k) * SCALE).astype(BF)
            key_terms = t_mm(score_grad, q) * SCALE
            moved[0, other, :] = key_terms[:BLK]
            own[0, block, :] = key_terms[BLK:]
            moved[1, other, :] = value_terms[:BLK]
            own[1, block, :] = value_terms[BLK:]
        dk_ref[:, head(h)] = (own[0] + moved[0]).astype(BF)
        dv_ref[:, head(h)] = (own[1] + moved[1]).astype(BF)


def row_backward(q, k, v, g, pattern):
    whole = jax.ShapeDtypeStruct((COLS, 2 * HALF), BF)
    return pl.pallas_call(
        row_backward_kernel,
        grid=(1,),
        out_shape=(whole, whole, whole),
        in_specs=[SMEM_SPEC] + [first_half()] * 4,
        out_specs=(first_half(),) * 3,
        scratch_shapes=[pltpu.VMEM((2, COLS, HD), F32), pltpu.VMEM((2, COLS, HD), F32)],
        compiler_params=params(),
        cost_estimate=cost(16 * 10 * BLK * 2 * BLK * HD, 7 * COLS * HALF * 2, 16 * BLK * 2 * BLK),
        name="row_backward",
    )(pattern, q, k, v, g)


def finish_kernel(off_ref, b_ref, dq_in, dk_in, dv_in, dq_ref, dk_ref, dv_ref):
    dq_ref[...] = b_ref[:, :HALF]
    for h in range(HC):
        pair = jnp.concatenate([b_ref[:, head(HC + h)], b_ref[:, head(2 * HC + h)]], axis=1)
        back = t_mm(shift_selector(off_ref[h]), pair).astype(BF)
        dk_ref[:, head(h)] = back[:, :HD]
        dv_ref[:, head(h)] = back[:, HD:]


def finish(back, dq, dk, dv, offset):
    whole = jax.ShapeDtypeStruct((COLS, 2 * HALF), BF)
    kept = pl.BlockSpec(memory_space=pl.ANY)
    second = pl.BlockSpec((COLS, HALF), lambda i: (0, 1))
    return pl.pallas_call(
        finish_kernel,
        grid=(1,),
        out_shape=(whole, whole, whole),
        in_specs=[SMEM_SPEC, pl.BlockSpec((COLS, 3 * HALF), lambda i: (0, 0)), kept, kept, kept],
        out_specs=(second, second, second),
        input_output_aliases={2: 0, 3: 1, 4: 2},
        compiler_params=params(),
        cost_estimate=cost(2 * COLS * COLS * 2 * HALF, 6 * COLS * HALF * 2),
        name="finish",
    )(offset, back, dq, dk, dv)


def pair_rows(ref, pair):
    chunk = 2 * HD // 8
    starts = [2 * HD * pair + (2 * at_y + at_z) * chunk for at_z in range(2) for at_y in range(4)]
    return jnp.concatenate([ref[start : start + chunk, :] for start in starts], axis=0)


def attn_grad_kernel(place, og_mine, og_theirs, mine_ref, theirs_ref, row_ref, send_ref):
    total = mm_t(og_mine[...], pair_rows(mine_ref, 0)) + mm_t(og_theirs[...], pair_rows(theirs_ref, 0))
    total = total.astype(BF)

    @pl.when(pl.program_id(0) < 2)
    def _():
        row_ref[...] = total

    @pl.when(pl.program_id(0) >= 2)
    def _():
        send_ref[...] = total


def attn_grad_of(og, mine, theirs, place):
    steps = 4
    rows = 2 * HALF // steps
    return pl.pallas_call(
        attn_grad_kernel,
        grid_spec=pltpu.PrefetchScalarGridSpec(
            num_scalar_prefetch=1,
            grid=(steps,),
            in_specs=[
                pl.BlockSpec((COLS, DH), lambda i, at: (0, at[0])),
                pl.BlockSpec((COLS, DH), lambda i, at: (0, 1 - at[0])),
                pl.BlockSpec((rows, DH), lambda i, at: (i, 0)),
                pl.BlockSpec((rows, DH), lambda i, at: (i, 0)),
            ],
            out_specs=(
                pl.BlockSpec((COLS, rows), lambda i, at: (0, jnp.minimum(i, 1))),
                pl.BlockSpec((COLS, rows), lambda i, at: (0, jnp.maximum(i, 2) - 2)),
            ),
        ),
        out_shape=(jax.ShapeDtypeStruct((COLS, HALF), BF),) * 2,
        compiler_params=params(),
        cost_estimate=cost(2 * COLS * 2 * HALF * D, 7 * 2**20),
        name="attn_grad",
    )(place, og, og, mine, theirs)


def layer_out_kernel(core_ref, row_ref, col_ref, mine_ref, theirs_ref, o_ref):
    def product(w_ref):
        two = 2 * HD
        total = mm(row_ref[:, :two], pair_rows(w_ref, 0)) + mm(row_ref[:, two:], pair_rows(w_ref, 1))
        total += mm(col_ref[:, :two], pair_rows(w_ref, 2)) + mm(col_ref[:, two:], pair_rows(w_ref, 3))
        o_ref[...] = total.astype(BF)

    pl.when(pl.program_id(0) == 0)(lambda: product(mine_ref))
    pl.when(pl.program_id(0) == 1)(lambda: product(theirs_ref))


def layer_out_of(row_out, col_out, mine, theirs, core):
    steps = 2
    width = DH // steps

    def place(half, i, c):
        which = jnp.where(half == 0, c[0], 1 - c[0])
        return (0, which * steps + i)

    return pl.pallas_call(
        layer_out_kernel,
        grid_spec=pltpu.PrefetchScalarGridSpec(
            num_scalar_prefetch=1,
            grid=(2, steps),
            in_specs=[
                pl.BlockSpec((COLS, HALF), lambda half, i, c: (0, 0)),
                pl.BlockSpec((COLS, HALF), lambda half, i, c: (0, 0)),
                pl.BlockSpec((2 * HALF, width), lambda half, i, c: (0, jnp.where(half == 0, i, steps - 1))),
                pl.BlockSpec((2 * HALF, width), lambda half, i, c: (0, jnp.where(half == 0, 0, i))),
            ],
            out_specs=pl.BlockSpec((COLS, width), place),
        ),
        out_shape=jax.ShapeDtypeStruct((COLS, D), BF),
        compiler_params=params(),
        cost_estimate=cost(2 * COLS * 2 * HALF * D, 7 * 2**20),
        name="layer_out",
    )(core, row_out, col_out, mine, theirs)


def weight_grad_kernel(place, row_mine, row_theirs, col_mine, col_theirs, og_mine, og_theirs, *refs):
    outs, total = refs[:4], refs[4]
    step = pl.program_id(0)
    block = lax.rem(place[1] + step, 4)

    def product(a_ref, b_ref):
        total[...] = t_mm(a_ref[...], og_mine[...]) + t_mm(b_ref[...], og_theirs[...])

    pl.when(block < 2)(lambda: product(row_mine, row_theirs))
    pl.when(block >= 2)(lambda: product(col_mine, col_theirs))
    for target, out in enumerate(outs):

        @pl.when(step == target)
        def _(out=out):
            out[...] = total[...].astype(out.dtype)


def weight_grad_of(row_mine, row_theirs, col_mine, col_theirs, og, og_theirs, place):
    rows = 2 * HALF // 4

    def row_block(i, at):
        return (0, jnp.minimum(lax.rem(at[1] + i, 4), 1))

    def col_block(i, at):
        return (0, jnp.maximum(lax.rem(at[1] + i, 4), 2) - 2)

    return pl.pallas_call(
        weight_grad_kernel,
        grid_spec=pltpu.PrefetchScalarGridSpec(
            num_scalar_prefetch=1,
            grid=(4,),
            in_specs=[
                pl.BlockSpec((COLS, rows), row_block),
                pl.BlockSpec((COLS, rows), row_block),
                pl.BlockSpec((COLS, rows), col_block),
                pl.BlockSpec((COLS, rows), col_block),
                pl.BlockSpec((COLS, DH), lambda i, at: (0, at[0])),
                pl.BlockSpec((COLS, DH), lambda i, at: (0, 0)),
            ],
            out_specs=(pl.BlockSpec((rows, DH), lambda i, at: (0, 0)),) * 4,
            scratch_shapes=[pltpu.VMEM((rows, DH), F32)],
        ),
        out_shape=(jax.ShapeDtypeStruct((rows, DH), F32),) + (jax.ShapeDtypeStruct((rows, DH), BF),) * 3,
        compiler_params=params(),
        cost_estimate=cost(4 * COLS * 2 * HALF * DH, 7 * 2**20),
        name="weight_grad",
    )(place, row_mine, row_theirs, col_mine, col_theirs, og, og_theirs)


def weight_sum_kernel(place, a_ref, b_ref, c_ref, d_ref, *outs):
    chunk = 2 * HD // 8
    for step, out in enumerate(outs):
        at_y = lax.rem(place[3] + step, 4)
        for at_z in range(2):
            rows = pl.ds(pl.multiple_of(at_z * HD + at_y * chunk, chunk), chunk)
            near = a_ref[rows, :] + b_ref[rows, :].astype(F32)
            far = c_ref[rows, :].astype(F32) + d_ref[rows, :].astype(F32)
            out[at_z * chunk : (at_z + 1) * chunk, :] = (near + far).astype(out.dtype)


def weight_sum(parts, place):
    rows = parts[0].shape[0] // 4
    return pl.pallas_call(
        weight_sum_kernel,
        out_shape=(jax.ShapeDtypeStruct((rows, DH), F32),) + (jax.ShapeDtypeStruct((rows, DH), BF),) * 3,
        in_specs=[SMEM_SPEC] + [VMEM_SPEC] * 4,
        out_specs=(VMEM_SPEC,) * 4,
        compiler_params=params(),
        cost_estimate=cost(16 * rows * DH, 4 * 2**20),
        name="weight_sum",
    )(place, *parts)


def exchange(tensor, axes):
    return lax.all_to_all(tensor, axes, split_axis=0, concat_axis=0, tiled=True)


def other_core(tensor):
    return lax.ppermute(tensor, "c", [(0, 1), (1, 0)])


def together(*values):
    return lax.optimization_barrier(values)


def along(tensor, axis, step):
    return lax.ppermute(tensor, axis, [(i, (i + step) % 4) for i in range(4)])


def shards(queries, keys, values, out_proj, out_grad, block_pattern, col_offset):
    q, k, v = (t.reshape(COLS, 2 * HALF) for t in (queries, keys, values))
    og = out_grad.reshape(COLS, D)
    rows_of = out_proj.shape[0]
    seq = ROWS
    chips = seq // 2
    dp = lax.axis_size("x") * lax.axis_size("zl")
    core = lax.axis_index("c").astype(jnp.int32)
    place = jnp.stack([core] + [lax.axis_index(name).astype(jnp.int32) for name in ("x", "zl", "y")])

    halves = out_proj.reshape(rows_of, 2, DH).transpose(1, 0, 2)
    spread = jnp.broadcast_to(halves[None], (chips // 2, 2, rows_of, DH)).reshape(chips, rows_of, DH)
    own_rows = exchange(spread, NEAR)
    packed = pack(q, k, v, col_offset)
    own_rows, packed = together(own_rows, packed)
    mine = lax.all_gather(own_rows.reshape(chips * rows_of, DH), ("x", "y"), axis=0, tiled=True)

    received = exchange(packed.reshape(seq, COLS // seq, 3 * HALF), SEQ)
    og_sent = lax.dynamic_slice(og, (0, (1 - core) * DH), (COLS, DH))
    row_out = row_forward(q, k, v, block_pattern)
    mine, row_out, og_sent = together(mine, row_out, og_sent)
    theirs, row_theirs, og_theirs = other_core(mine), other_core(row_out), other_core(og_sent)
    grad_rows, grad_cols = attn_grad_of(og, mine, theirs, place)
    received, row_theirs, og_theirs, grad_cols = together(received, row_theirs, og_theirs, grad_cols)
    received = received.reshape(ROWS, 2, GRP, 3 * HALF)

    send = column_forward(received, grad_cols.reshape(ROWS, 2, GRP, HALF))
    mixed = exchange(send.reshape(seq, COLS // seq, 2 * HALF), SEQ)
    dq, dk, dv = row_backward(q, k, v, grad_rows, block_pattern)
    mixed, dq, dk, dv = together(mixed, dq, dk, dv)

    col_mine = mixed.reshape(COLS, 2 * HALF)
    col_theirs = other_core(col_mine)
    col_back = column_backward(received, mixed.reshape(ROWS, 2, GRP, 2 * HALF)).reshape(seq, COLS // seq, 3 * HALF)
    col_back, col_mine, col_theirs = together(col_back, col_mine, col_theirs)
    back = exchange(col_back, SEQ).reshape(COLS, 3 * HALF)

    parts = weight_grad_of(row_out, row_theirs, col_mine, col_theirs, og, og_theirs, place)
    parts = [parts[0]] + [along(parts[step], "x", step) for step in (1, 2, 3)]
    parts = weight_sum(parts, place)
    part = parts[0]
    for step in (1, 2, 3):
        part = part + along(parts[step], "y", step).astype(F32)
    part = part.astype(BF).reshape(chips, rows_of, DH)
    part, back = together(part, back)
    part = exchange(part, NEAR).astype(F32).reshape(chips // 2, 2, rows_of, DH)
    weight_total = jnp.sum(part, axis=0)
    tokens = COLS * seq * dp
    w_grad = weight_total.transpose(1, 0, 2).reshape(rows_of, D) * tokens ** (-0.5)

    dq, dk, dv = finish(back, dq, dk, dv, col_offset)

    layer = layer_out_of(row_out, col_mine, mine, theirs, place)
    lead = (1, 1, COLS)
    return (
        layer.reshape(lead + (D,)),
        dq.reshape(lead + (2 * HALF,)),
        dk.reshape(lead + (2 * HALF,)),
        dv.reshape(lead + (2 * HALF,)),
        w_grad,
    )


def solution(mesh):
    fine = Mesh(mesh.devices.reshape(4, 2, 4, 4, 2), DP + SEQ)
    token = P(DP, SEQ, None, None)
    rows = P(DP + SEQ, None)
    in_specs = (token, token, token, rows, token, P(), P())
    out_specs = (token, token, token, token, rows)
    return jax.shard_map(shards, mesh=fine, in_specs=in_specs, out_specs=out_specs, check_vma=False)
```

```python
import functools

import jax
import jax.numpy as jnp
from jax import lax
from jax.experimental import pallas as pl
from jax.experimental.pallas import tpu as pltpu
from jax.sharding import Mesh, PartitionSpec as P

HD = 128
HR = 4
HC = 4
BLK = 128
NB = 4
COLS = 512
HALF = HR * HD
D = 2048
DH = D // 2
SCALE = HD ** (-0.5)
BF = jnp.bfloat16
F32 = jnp.float32
GRP = 8
ROWS = 32
TILE = GRP * ROWS
VMEM_LIMIT = 50 * 1024 * 1024

DP = ("x", "zl")
SEQ = ("y", "zh", "c")
NEAR = ("zl", "zh", "c")


def mm(a, b):
    return lax.dot_general(a, b, (((1,), (0,)), ((), ())), preferred_element_type=F32)


def mm_t(a, b):
    return lax.dot_general(a, b, (((1,), (1,)), ((), ())), preferred_element_type=F32)


def t_mm(a, b):
    return lax.dot_general(a, b, (((0,), (0,)), ((), ())), preferred_element_type=F32)


def params():
    return pltpu.CompilerParams(vmem_limit_bytes=VMEM_LIMIT)


def cost(flops, nbytes, trans=0):
    return pl.CostEstimate(flops=int(flops), transcendentals=int(trans), bytes_accessed=int(nbytes))


SMEM_SPEC = pl.BlockSpec(memory_space=pltpu.SMEM)
VMEM_SPEC = pl.BlockSpec(memory_space=pltpu.VMEM)


def head(index):
    return slice(index * HD, (index + 1) * HD)


def shift_selector(offset):
    row = lax.broadcasted_iota(jnp.int32, (COLS, COLS), 0)
    col = lax.broadcasted_iota(jnp.int32, (COLS, COLS), 1)
    source = row - offset
    source = jnp.where(source < 0, source + COLS, source)
    return jnp.where(source == col, 1.0, 0.0).astype(BF)


def pack_kernel(off_ref, q_ref, k_ref, v_ref, o_ref):
    o_ref[:, :HALF] = q_ref[...]
    for h in range(HC):
        pair = jnp.concatenate([k_ref[:, head(h)], v_ref[:, head(h)]], axis=1)
        moved = mm(shift_selector(off_ref[h]), pair).astype(BF)
        o_ref[:, head(HC + h)] = moved[:, :HD]
        o_ref[:, head(2 * HC + h)] = moved[:, HD:]


def pack(q, k, v, offset):
    half = pl.BlockSpec((COLS, HALF), lambda i: (0, 1))
    return pl.pallas_call(
        pack_kernel,
        grid=(1,),
        out_shape=jax.ShapeDtypeStruct((COLS, 3 * HALF), BF),
        in_specs=[SMEM_SPEC, half, half, half],
        out_specs=pl.BlockSpec((COLS, 3 * HALF), lambda i: (0, 0)),
        compiler_params=params(),
        cost_estimate=cost(2 * COLS * COLS * 2 * HALF, 6 * COLS * HALF * 2),
        name="pack",
    )(offset, q, k, v)


def tile_of(ref, lane):
    tile = ref[:, 0, :, lane * HD : (lane + 1) * HD]
    return tile.astype(F32).reshape(TILE, HD).astype(BF)


def store_tile(ref, lane, value):
    ref[:, 0, :, lane * HD : (lane + 1) * HD] = value.reshape(ROWS, GRP, HD).astype(BF)


def column_mask():
    row = lax.broadcasted_iota(jnp.int32, (TILE, TILE), 0)
    col = lax.broadcasted_iota(jnp.int32, (TILE, TILE), 1)
    return lax.rem(row, GRP) == lax.rem(col, GRP)


def softmax(scores):
    e = jnp.exp(scores - jnp.max(scores, axis=-1, keepdims=True))
    return e / jnp.sum(e, axis=-1, keepdims=True)


def column_probs(r_ref, h, mask):
    q = tile_of(r_ref, h)
    k = tile_of(r_ref, HC + h)
    v = tile_of(r_ref, 2 * HC + h)
    return q, k, v, softmax(jnp.where(mask, mm_t(q, k) * SCALE, -1e30))


def column_forward_kernel(r_ref, o_ref):
    mask = column_mask()
    for h in range(HC):
        _, _, v, probs = column_probs(r_ref, h, mask)
        store_tile(o_ref, h, mm(probs.astype(BF), v))


def group_block(lanes):
    return pl.BlockSpec((ROWS, 1, GRP, lanes), lambda i: (0, i, 0, 0))


def column_forward(received):
    return pl.pallas_call(
        column_forward_kernel,
        grid=(2,),
        out_shape=jax.ShapeDtypeStruct((ROWS, 2, GRP, HALF), BF),
        in_specs=[group_block(3 * HALF)],
        out_specs=group_block(HALF),
        compiler_params=params(),
        cost_estimate=cost(8 * 4 * TILE * TILE * HD, 4 * COLS * HALF * 2, 8 * TILE * TILE),
        name="column_forward",
    )(received)


def column_backward_kernel(r_ref, g_ref, o_ref):
    mask = column_mask()
    for h in range(HC):
        q, k, v, probs = column_probs(r_ref, h, mask)
        g = tile_of(g_ref, h)
        store_tile(o_ref, 2 * HC + h, t_mm(probs.astype(BF), g))
        prob_grad = mm_t(g, v)
        delta = jnp.sum(probs * prob_grad, axis=-1, keepdims=True)
        score_grad = (probs * (prob_grad - delta)).astype(BF)
        store_tile(o_ref, h, mm(score_grad, k) * SCALE)
        store_tile(o_ref, HC + h, t_mm(score_grad, q) * SCALE)


def column_backward(received, grads):
    return pl.pallas_call(
        column_backward_kernel,
        grid=(2,),
        out_shape=jax.ShapeDtypeStruct((ROWS, 2, GRP, 3 * HALF), BF),
        in_specs=[group_block(3 * HALF), group_block(HALF)],
        out_specs=group_block(3 * HALF),
        compiler_params=params(),
        cost_estimate=cost(8 * 10 * TILE * TILE * HD, 7 * COLS * HALF * 2, 8 * TILE * TILE),
        name="column_backward",
    )(received, grads)


def row_tile(pat_ref, q_ref, k_ref, v_ref, h, j):
    block = slice(j * BLK, (j + 1) * BLK)
    other = pl.ds(pl.multiple_of(pat_ref[h, j] * BLK, BLK), BLK)
    q = q_ref[block, head(h)]
    k = jnp.concatenate([k_ref[other, head(h)], k_ref[block, head(h)]], axis=0)
    v = jnp.concatenate([v_ref[other, head(h)], v_ref[block, head(h)]], axis=0)
    return block, other, q, k, v, softmax(mm_t(q, k) * SCALE)


def row_forward_kernel(pat_ref, q_ref, k_ref, v_ref, o_ref):
    for h in range(HR):
        for j in range(NB):
            block, _, _, _, v, probs = row_tile(pat_ref, q_ref, k_ref, v_ref, h, j)
            o_ref[block, head(h)] = mm(probs.astype(BF), v).astype(BF)


def first_half():
    return pl.BlockSpec((COLS, HALF), lambda i: (0, 0))


def row_forward(q, k, v, pattern):
    return pl.pallas_call(
        row_forward_kernel,
        grid=(1,),
        out_shape=jax.ShapeDtypeStruct((COLS, HALF), BF),
        in_specs=[SMEM_SPEC, first_half(), first_half(), first_half()],
        out_specs=first_half(),
        compiler_params=params(),
        cost_estimate=cost(16 * 4 * BLK * 2 * BLK * HD, 4 * COLS * HALF * 2, 16 * BLK * 2 * BLK),
        name="row_forward",
    )(pattern, q, k, v)


def row_backward_kernel(pat_ref, q_ref, k_ref, v_ref, g_ref, dq_ref, dk_ref, dv_ref, own, moved):
    for h in range(HR):
        for j in range(NB):
            block, other, q, k, v, probs = row_tile(pat_ref, q_ref, k_ref, v_ref, h, j)
            g = g_ref[block, head(h)]
            value_terms = t_mm(probs.astype(BF), g)
            prob_grad = mm_t(g, v)
            delta = jnp.sum(probs * prob_grad, axis=-1, keepdims=True)
            score_grad = (probs * (prob_grad - delta)).astype(BF)
            dq_ref[block, head(h)] = (mm(score_grad, k) * SCALE).astype(BF)
            key_terms = t_mm(score_grad, q) * SCALE
            moved[0, other, :] = key_terms[:BLK]
            own[0, block, :] = key_terms[BLK:]
            moved[1, other, :] = value_terms[:BLK]
            own[1, block, :] = value_terms[BLK:]
        dk_ref[:, head(h)] = (own[0] + moved[0]).astype(BF)
        dv_ref[:, head(h)] = (own[1] + moved[1]).astype(BF)


def row_backward(q, k, v, g, pattern):
    whole = jax.ShapeDtypeStruct((COLS, 2 * HALF), BF)
    return pl.pallas_call(
        row_backward_kernel,
        grid=(1,),
        out_shape=(whole, whole, whole),
        in_specs=[SMEM_SPEC] + [first_half()] * 4,
        out_specs=(first_half(),) * 3,
        scratch_shapes=[pltpu.VMEM((2, COLS, HD), F32), pltpu.VMEM((2, COLS, HD), F32)],
        compiler_params=params(),
        cost_estimate=cost(16 * 10 * BLK * 2 * BLK * HD, 7 * COLS * HALF * 2, 16 * BLK * 2 * BLK),
        name="row_backward",
    )(pattern, q, k, v, g)


def finish_kernel(off_ref, b_ref, dq_in, dk_in, dv_in, dq_ref, dk_ref, dv_ref):
    dq_ref[...] = b_ref[:, :HALF]
    for h in range(HC):
        pair = jnp.concatenate([b_ref[:, head(HC + h)], b_ref[:, head(2 * HC + h)]], axis=1)
        back = t_mm(shift_selector(off_ref[h]), pair).astype(BF)
        dk_ref[:, head(h)] = back[:, :HD]
        dv_ref[:, head(h)] = back[:, HD:]


def finish(back, dq, dk, dv, offset):
    whole = jax.ShapeDtypeStruct((COLS, 2 * HALF), BF)
    kept = pl.BlockSpec(memory_space=pl.ANY)
    second = pl.BlockSpec((COLS, HALF), lambda i: (0, 1))
    return pl.pallas_call(
        finish_kernel,
        grid=(1,),
        out_shape=(whole, whole, whole),
        in_specs=[SMEM_SPEC, pl.BlockSpec((COLS, 3 * HALF), lambda i: (0, 0)), kept, kept, kept],
        out_specs=(second, second, second),
        input_output_aliases={2: 0, 3: 1, 4: 2},
        compiler_params=params(),
        cost_estimate=cost(2 * COLS * COLS * 2 * HALF, 6 * COLS * HALF * 2),
        name="finish",
    )(offset, back, dq, dk, dv)


def attn_grad_kernel(place, og_mine, og_theirs, mine_ref, theirs_ref, row_ref, send_ref):
    total = mm_t(og_mine[...], mine_ref[...]) + mm_t(og_theirs[...], theirs_ref[...])
    total = total.astype(BF)

    @pl.when(pl.program_id(0) < 2)
    def _():
        row_ref[...] = total

    @pl.when(pl.program_id(0) >= 2)
    def _():
        send_ref[...] = total


def attn_grad_of(og, mine, theirs, place):
    steps = 4
    rows = 2 * HALF // steps
    return pl.pallas_call(
        attn_grad_kernel,
        grid_spec=pltpu.PrefetchScalarGridSpec(
            num_scalar_prefetch=1,
            grid=(steps,),
            in_specs=[
                pl.BlockSpec((COLS, DH), lambda i, at: (0, at[0])),
                pl.BlockSpec((COLS, DH), lambda i, at: (0, 1 - at[0])),
                pl.BlockSpec((rows, DH), lambda i, at: (i, 0)),
                pl.BlockSpec((rows, DH), lambda i, at: (i, 0)),
            ],
            out_specs=(
                pl.BlockSpec((COLS, rows), lambda i, at: (0, jnp.minimum(i, 1))),
                pl.BlockSpec((COLS, rows), lambda i, at: (0, jnp.maximum(i, 2) - 2)),
            ),
        ),
        out_shape=(jax.ShapeDtypeStruct((COLS, HALF), BF),) * 2,
        compiler_params=params(),
        cost_estimate=cost(2 * COLS * 2 * HALF * D, 7 * 2**20),
        name="attn_grad",
    )(place, og, og, mine, theirs)


def layer_out_kernel(core_ref, row_ref, col_ref, mine_ref, theirs_ref, o_ref):
    def product(w_ref):
        total = mm(row_ref[...], w_ref[:HALF, :]) + mm(col_ref[...], w_ref[HALF:, :])
        o_ref[...] = total.astype(BF)

    pl.when(pl.program_id(0) == 0)(lambda: product(mine_ref))
    pl.when(pl.program_id(0) == 1)(lambda: product(theirs_ref))


def layer_out_of(row_out, col_out, mine, theirs, core):
    steps = 2
    width = DH // steps

    def place(half, i, c):
        which = jnp.where(half == 0, c[0], 1 - c[0])
        return (0, which * steps + i)

    return pl.pallas_call(
        layer_out_kernel,
        grid_spec=pltpu.PrefetchScalarGridSpec(
            num_scalar_prefetch=1,
            grid=(2, steps),
            in_specs=[
                pl.BlockSpec((COLS, HALF), lambda half, i, c: (0, 0)),
                pl.BlockSpec((COLS, HALF), lambda half, i, c: (0, 0)),
                pl.BlockSpec((2 * HALF, width), lambda half, i, c: (0, jnp.where(half == 0, i, steps - 1))),
                pl.BlockSpec((2 * HALF, width), lambda half, i, c: (0, jnp.where(half == 0, 0, i))),
            ],
            out_specs=pl.BlockSpec((COLS, width), place),
        ),
        out_shape=jax.ShapeDtypeStruct((COLS, D), BF),
        compiler_params=params(),
        cost_estimate=cost(2 * COLS * 2 * HALF * D, 7 * 2**20),
        name="layer_out",
    )(core, row_out, col_out, mine, theirs)


def weight_grad_kernel(place, row_mine, row_theirs, col_mine, col_theirs, og_mine, og_theirs, *refs):
    outs, total = refs[:4], refs[4]
    step = pl.program_id(0)
    block = lax.rem(place[1] + step, 4)

    def product(a_ref, b_ref):
        total[...] = t_mm(a_ref[...], og_mine[...]) + t_mm(b_ref[...], og_theirs[...])

    pl.when(block < 2)(lambda: product(row_mine, row_theirs))
    pl.when(block >= 2)(lambda: product(col_mine, col_theirs))
    for target, out in enumerate(outs):

        @pl.when(step == target)
        def _(out=out):
            out[...] = total[...].astype(out.dtype)


def weight_grad_of(row_mine, row_theirs, col_mine, col_theirs, og, og_theirs, place):
    rows = 2 * HALF // 4

    def row_block(i, at):
        return (0, jnp.minimum(lax.rem(at[1] + i, 4), 1))

    def col_block(i, at):
        return (0, jnp.maximum(lax.rem(at[1] + i, 4), 2) - 2)

    return pl.pallas_call(
        weight_grad_kernel,
        grid_spec=pltpu.PrefetchScalarGridSpec(
            num_scalar_prefetch=1,
            grid=(4,),
            in_specs=[
                pl.BlockSpec((COLS, rows), row_block),
                pl.BlockSpec((COLS, rows), row_block),
                pl.BlockSpec((COLS, rows), col_block),
                pl.BlockSpec((COLS, rows), col_block),
                pl.BlockSpec((COLS, DH), lambda i, at: (0, at[0])),
                pl.BlockSpec((COLS, DH), lambda i, at: (0, 0)),
            ],
            out_specs=(pl.BlockSpec((rows, DH), lambda i, at: (0, 0)),) * 4,
            scratch_shapes=[pltpu.VMEM((rows, DH), F32)],
        ),
        out_shape=(jax.ShapeDtypeStruct((rows, DH), F32),) + (jax.ShapeDtypeStruct((rows, DH), BF),) * 3,
        compiler_params=params(),
        cost_estimate=cost(4 * COLS * 2 * HALF * DH, 7 * 2**20),
        name="weight_grad",
    )(place, row_mine, row_theirs, col_mine, col_theirs, og, og_theirs)


def gather_kernel(axis, pieces, place, own_ref, a_ref, b_ref, c_ref, o_ref):
    chunk = own_ref.shape[0] // pieces
    for step, ref in enumerate((own_ref, a_ref, b_ref, c_ref)):
        source = lax.rem(place[axis] + 4 - step, 4)
        for piece in range(pieces):
            rows = pl.ds(pl.multiple_of((piece * 4 + source) * chunk, chunk), chunk)
            o_ref[rows, :] = ref[piece * chunk : (piece + 1) * chunk, :]


def gather_of(own, place, axis, index, pieces):
    blocks = [own] + [along(own, axis, step) for step in (1, 2, 3)]
    return pl.pallas_call(
        functools.partial(gather_kernel, index, pieces),
        out_shape=jax.ShapeDtypeStruct((4 * own.shape[0], DH), BF),
        in_specs=[SMEM_SPEC] + [VMEM_SPEC] * 4,
        out_specs=VMEM_SPEC,
        compiler_params=params(),
        cost_estimate=cost(0, 16 * own.shape[0] * DH),
        name="gather_" + axis,
    )(place, *blocks)


def weight_sum_kernel(place, a_ref, b_ref, c_ref, d_ref, *outs):
    chunk = 2 * HD // 8
    for step, out in enumerate(outs):
        at_y = lax.rem(place[3] + step, 4)
        for at_z in range(2):
            rows = pl.ds(pl.multiple_of(at_z * HD + at_y * chunk, chunk), chunk)
            near = a_ref[rows, :] + b_ref[rows, :].astype(F32)
            far = c_ref[rows, :].astype(F32) + d_ref[rows, :].astype(F32)
            out[at_z * chunk : (at_z + 1) * chunk, :] = (near + far).astype(out.dtype)


def weight_sum(parts, place):
    rows = parts[0].shape[0] // 4
    return pl.pallas_call(
        weight_sum_kernel,
        out_shape=(jax.ShapeDtypeStruct((rows, DH), F32),) + (jax.ShapeDtypeStruct((rows, DH), BF),) * 3,
        in_specs=[SMEM_SPEC] + [VMEM_SPEC] * 4,
        out_specs=(VMEM_SPEC,) * 4,
        compiler_params=params(),
        cost_estimate=cost(16 * rows * DH, 4 * 2**20),
        name="weight_sum",
    )(place, *parts)


def y_sum_kernel(place, a_ref, b_ref, c_ref, d_ref, *refs):
    outs, total = refs[:-1], refs[-1]
    near = a_ref[...] + b_ref[...].astype(F32)
    total[...] = near + (c_ref[...].astype(F32) + d_ref[...].astype(F32))
    rows = outs[0].shape[0]
    for step, out in enumerate(outs):
        target = lax.rem(place[2] + step // 4, 2) * 4 + lax.rem(place[4] + step % 4, 4)
        out[...] = total[pl.ds(pl.multiple_of(target * rows, rows), rows), :].astype(out.dtype)


def y_sum(parts, place):
    rows = parts[0].shape[0] // 8
    return pl.pallas_call(
        y_sum_kernel,
        out_shape=(jax.ShapeDtypeStruct((rows, DH), F32),) + (jax.ShapeDtypeStruct((rows, DH), BF),) * 7,
        in_specs=[SMEM_SPEC] + [VMEM_SPEC] * 4,
        out_specs=(VMEM_SPEC,) * 8,
        scratch_shapes=[pltpu.VMEM(parts[0].shape, F32)],
        compiler_params=params(),
        cost_estimate=cost(32 * rows * DH, 2**20),
        name="y_sum",
    )(place, *parts)


def z_sum_kernel(place, *refs):
    ins, (keep_ref, send_ref) = refs[:8], refs[8:]
    total = ins[0][...]
    for ref in ins[1:]:
        total = total + ref[...].astype(F32)
    half = keep_ref.shape[0]
    first = jnp.broadcast_to(place[0], (half, DH)) == 0
    keep_ref[...] = jnp.where(first, total[:half], total[half:])
    send_ref[...] = jnp.where(first, total[half:], total[:half])


def z_sum(parts, place):
    out = jax.ShapeDtypeStruct((parts[0].shape[0] // 2, DH), F32)
    return pl.pallas_call(
        z_sum_kernel,
        out_shape=(out, out),
        in_specs=[SMEM_SPEC] + [VMEM_SPEC] * 8,
        out_specs=(VMEM_SPEC, VMEM_SPEC),
        compiler_params=params(),
        cost_estimate=cost(8 * 8 * DH, 2**18),
        name="z_sum",
    )(place, *parts)


def exchange(tensor, axes):
    return lax.all_to_all(tensor, axes, split_axis=0, concat_axis=0, tiled=True)


def other_core(tensor):
    return lax.ppermute(tensor, "c", [(0, 1), (1, 0)])


def together(*values):
    return lax.optimization_barrier(values)


def along(tensor, axis, step):
    return lax.ppermute(tensor, axis, [(i, (i + step) % 4) for i in range(4)])


def along_z(tensor, step):
    turns = [(z * 4 + h, (z + step // 4) % 2 * 4 + (h + step % 4) % 4) for z in range(2) for h in range(4)]
    return lax.ppermute(tensor, ("zl", "zh"), turns)


def shards(queries, keys, values, out_proj, out_grad, block_pattern, col_offset):
    q, k, v = (t.reshape(COLS, 2 * HALF) for t in (queries, keys, values))
    og = out_grad.reshape(COLS, D)
    rows_of = out_proj.shape[0]
    seq = ROWS
    near = seq // 2
    dp = lax.axis_size("x") * lax.axis_size("zl")
    core = lax.axis_index("c").astype(jnp.int32)
    place = jnp.stack([core] + [lax.axis_index(name).astype(jnp.int32) for name in ("x", "zl", "y", "zh")])

    halves = out_proj.reshape(rows_of, 2, DH).transpose(1, 0, 2)
    spread = jnp.broadcast_to(halves[None], (near // 2, 2, rows_of, DH)).reshape(near, rows_of, DH)
    own_rows = exchange(spread, NEAR)
    packed = pack(q, k, v, col_offset)
    own_rows, packed = together(own_rows, packed)
    own_rows = own_rows.reshape(near * rows_of, DH)
    mine = gather_of(gather_of(own_rows, place, "y", 3, 2), place, "x", 1, 1)

    received = exchange(packed.reshape(seq, COLS // seq, 3 * HALF), SEQ)
    og_sent = lax.dynamic_slice(og, (0, (1 - core) * DH), (COLS, DH))
    og_theirs = other_core(og_sent)
    row_out = row_forward(q, k, v, block_pattern)
    row_theirs = other_core(row_out)
    received, row_out, row_theirs, og_theirs = together(received, row_out, row_theirs, og_theirs)
    received = received.reshape(ROWS, 2, GRP, 3 * HALF)

    col_sent = column_forward(received).reshape(seq, COLS // seq, HALF)
    col_sent, mine = together(col_sent, mine)
    col_mine = exchange(col_sent, SEQ)
    theirs = other_core(mine)
    grad_rows, grad_cols = attn_grad_of(og, mine, theirs, place)
    col_mine, grad_rows, grad_cols = together(col_mine, grad_rows, grad_cols)
    col_mine = col_mine.reshape(COLS, HALF)

    col_grads = exchange(grad_cols.reshape(seq, COLS // seq, HALF), SEQ)
    col_theirs = other_core(col_mine)
    parts = weight_grad_of(row_out, row_theirs, col_mine, col_theirs, og, og_theirs, place)
    dq, dk, dv = row_backward(q, k, v, grad_rows, block_pattern)
    next_x, last_x = along(parts[1], "x", 1), along(parts[3], "x", 3)
    col_grads, dq, dk, dv, next_x, last_x = together(col_grads, dq, dk, dv, next_x, last_x)

    col_back = column_backward(received, col_grads.reshape(ROWS, 2, GRP, HALF)).reshape(seq, COLS // seq, 3 * HALF)
    back = exchange(col_back, SEQ).reshape(COLS, 3 * HALF)

    parts = weight_sum([parts[0], next_x, along(parts[2], "x", 2), last_x], place)
    parts = [parts[0]] + [along(parts[step], "y", step) for step in (1, 2, 3)]
    parts = y_sum(parts, place)
    parts = [parts[0]] + [along_z(parts[step], step) for step in range(1, 8)]
    keep, give = z_sum(parts, place)
    taken = other_core(give)
    first = core == 0
    tokens = COLS * seq * dp
    w_grad = jnp.concatenate([jnp.where(first, keep, taken), jnp.where(first, taken, keep)], axis=1)
    w_grad = w_grad * tokens ** (-0.5)

    dq, dk, dv = finish(back, dq, dk, dv, col_offset)
    layer = layer_out_of(row_out, col_mine, mine, theirs, place)
    lead = (1, 1, COLS)
    return (
        layer.reshape(lead + (D,)),
        dq.reshape(lead + (2 * HALF,)),
        dk.reshape(lead + (2 * HALF,)),
        dv.reshape(lead + (2 * HALF,)),
        w_grad,
    )


def solution(mesh):
    fine = Mesh(mesh.devices.reshape(4, 2, 4, 4, 2), DP + SEQ)
    token = P(DP, SEQ, None, None)
    rows = P(DP + SEQ, None)
    in_specs = (token, token, token, rows, token, P(), P())
    out_specs = (token, token, token, token, rows)
    return jax.shard_map(shards, mesh=fine, in_specs=in_specs, out_specs=out_specs, check_vma=False)
```

```python
import functools

import jax
import jax.numpy as jnp
from jax import lax
from jax.experimental import pallas as pl
from jax.experimental.pallas import tpu as pltpu
from jax.sharding import Mesh, PartitionSpec as P

HD = 128
HR = 4
HC = 4
BLK = 128
NB = 4
COLS = 512
HALF = HR * HD
D = 2048
DH = D // 2
SCALE = HD ** (-0.5)
BF = jnp.bfloat16
F32 = jnp.float32
GRP = 8
ROWS = 32
TILE = GRP * ROWS
VMEM_LIMIT = 50 * 1024 * 1024

DP = ("x", "zl")
SEQ = ("y", "zh", "c")
NEAR = ("zl", "zh", "c")


def mm(a, b):
    return lax.dot_general(a, b, (((1,), (0,)), ((), ())), preferred_element_type=F32)


def mm_t(a, b):
    return lax.dot_general(a, b, (((1,), (1,)), ((), ())), preferred_element_type=F32)


def t_mm(a, b):
    return lax.dot_general(a, b, (((0,), (0,)), ((), ())), preferred_element_type=F32)


def params():
    return pltpu.CompilerParams(vmem_limit_bytes=VMEM_LIMIT)


def cost(flops, nbytes, trans=0):
    return pl.CostEstimate(flops=int(flops), transcendentals=int(trans), bytes_accessed=int(nbytes))


SMEM_SPEC = pl.BlockSpec(memory_space=pltpu.SMEM)
VMEM_SPEC = pl.BlockSpec(memory_space=pltpu.VMEM)


def head(index):
    return slice(index * HD, (index + 1) * HD)


def shift_selector(offset):
    row = lax.broadcasted_iota(jnp.int32, (COLS, COLS), 0)
    col = lax.broadcasted_iota(jnp.int32, (COLS, COLS), 1)
    source = row - offset
    source = jnp.where(source < 0, source + COLS, source)
    return jnp.where(source == col, 1.0, 0.0).astype(BF)


def pack_kernel(off_ref, q_ref, k_ref, v_ref, o_ref):
    o_ref[:, :HALF] = q_ref[...]
    for h in range(HC):
        pair = jnp.concatenate([k_ref[:, head(h)], v_ref[:, head(h)]], axis=1)
        moved = mm(shift_selector(off_ref[h]), pair).astype(BF)
        o_ref[:, head(HC + h)] = moved[:, :HD]
        o_ref[:, head(2 * HC + h)] = moved[:, HD:]


def pack(q, k, v, offset):
    half = pl.BlockSpec((COLS, HALF), lambda i: (0, 1))
    return pl.pallas_call(
        pack_kernel,
        grid=(1,),
        out_shape=jax.ShapeDtypeStruct((COLS, 3 * HALF), BF),
        in_specs=[SMEM_SPEC, half, half, half],
        out_specs=pl.BlockSpec((COLS, 3 * HALF), lambda i: (0, 0)),
        compiler_params=params(),
        cost_estimate=cost(2 * COLS * COLS * 2 * HALF, 6 * COLS * HALF * 2),
        name="pack",
    )(offset, q, k, v)


def tile_of(ref, lane):
    tile = ref[:, 0, :, lane * HD : (lane + 1) * HD]
    return tile.astype(F32).reshape(TILE, HD).astype(BF)


def store_tile(ref, lane, value):
    ref[:, 0, :, lane * HD : (lane + 1) * HD] = value.reshape(ROWS, GRP, HD).astype(BF)


def column_mask():
    row = lax.broadcasted_iota(jnp.int32, (TILE, TILE), 0)
    col = lax.broadcasted_iota(jnp.int32, (TILE, TILE), 1)
    return lax.rem(row, GRP) == lax.rem(col, GRP)


def softmax(scores):
    e = jnp.exp(scores - jnp.max(scores, axis=-1, keepdims=True))
    return e / jnp.sum(e, axis=-1, keepdims=True)


def column_probs(r_ref, h, mask):
    q = tile_of(r_ref, h)
    k = tile_of(r_ref, HC + h)
    v = tile_of(r_ref, 2 * HC + h)
    return q, k, v, softmax(jnp.where(mask, mm_t(q, k) * SCALE, -1e30))


def column_forward_kernel(r_ref, o_ref):
    mask = column_mask()
    for h in range(HC):
        _, _, v, probs = column_probs(r_ref, h, mask)
        store_tile(o_ref, h, mm(probs.astype(BF), v))


def group_block(lanes):
    return pl.BlockSpec((ROWS, 1, GRP, lanes), lambda i: (0, i, 0, 0))


def column_forward(received):
    return pl.pallas_call(
        column_forward_kernel,
        grid=(2,),
        out_shape=jax.ShapeDtypeStruct((ROWS, 2, GRP, HALF), BF),
        in_specs=[group_block(3 * HALF)],
        out_specs=group_block(HALF),
        compiler_params=params(),
        cost_estimate=cost(10**11, 4 * COLS * HALF * 2, 8 * TILE * TILE),
        name="column_forward",
    )(received)


def column_backward_kernel(r_ref, g_ref, o_ref):
    mask = column_mask()
    for h in range(HC):
        q, k, v, probs = column_probs(r_ref, h, mask)
        g = tile_of(g_ref, h)
        store_tile(o_ref, 2 * HC + h, t_mm(probs.astype(BF), g))
        prob_grad = mm_t(g, v)
        delta = jnp.sum(probs * prob_grad, axis=-1, keepdims=True)
        score_grad = (probs * (prob_grad - delta)).astype(BF)
        store_tile(o_ref, h, mm(score_grad, k) * SCALE)
        store_tile(o_ref, HC + h, t_mm(score_grad, q) * SCALE)


def column_backward(received, grads):
    return pl.pallas_call(
        column_backward_kernel,
        grid=(2,),
        out_shape=jax.ShapeDtypeStruct((ROWS, 2, GRP, 3 * HALF), BF),
        in_specs=[group_block(3 * HALF), group_block(HALF)],
        out_specs=group_block(3 * HALF),
        compiler_params=params(),
        cost_estimate=cost(8 * 10 * TILE * TILE * HD, 7 * COLS * HALF * 2, 8 * TILE * TILE),
        name="column_backward",
    )(received, grads)


def row_tile(pat_ref, q_ref, k_ref, v_ref, h, j):
    block = slice(j * BLK, (j + 1) * BLK)
    other = pl.ds(pl.multiple_of(pat_ref[h, j] * BLK, BLK), BLK)
    q = q_ref[block, head(h)]
    k = jnp.concatenate([k_ref[other, head(h)], k_ref[block, head(h)]], axis=0)
    v = jnp.concatenate([v_ref[other, head(h)], v_ref[block, head(h)]], axis=0)
    return block, other, q, k, v, softmax(mm_t(q, k) * SCALE)


def row_forward_kernel(pat_ref, q_ref, k_ref, v_ref, o_ref):
    for h in range(HR):
        for j in range(NB):
            block, _, _, _, v, probs = row_tile(pat_ref, q_ref, k_ref, v_ref, h, j)
            o_ref[block, head(h)] = mm(probs.astype(BF), v).astype(BF)


def first_half():
    return pl.BlockSpec((COLS, HALF), lambda i: (0, 0))


def row_forward(q, k, v, pattern):
    return pl.pallas_call(
        row_forward_kernel,
        grid=(1,),
        out_shape=jax.ShapeDtypeStruct((COLS, HALF), BF),
        in_specs=[SMEM_SPEC, first_half(), first_half(), first_half()],
        out_specs=first_half(),
        compiler_params=params(),
        cost_estimate=cost(16 * 4 * BLK * 2 * BLK * HD, 4 * COLS * HALF * 2, 16 * BLK * 2 * BLK),
        name="row_forward",
    )(pattern, q, k, v)


def row_backward_kernel(pat_ref, q_ref, k_ref, v_ref, g_ref, dq_ref, dk_ref, dv_ref, own, moved):
    for h in range(HR):
        for j in range(NB):
            block, other, q, k, v, probs = row_tile(pat_ref, q_ref, k_ref, v_ref, h, j)
            g = g_ref[block, head(h)]
            value_terms = t_mm(probs.astype(BF), g)
            prob_grad = mm_t(g, v)
            delta = jnp.sum(probs * prob_grad, axis=-1, keepdims=True)
            score_grad = (probs * (prob_grad - delta)).astype(BF)
            dq_ref[block, head(h)] = (mm(score_grad, k) * SCALE).astype(BF)
            key_terms = t_mm(score_grad, q) * SCALE
            moved[0, other, :] = key_terms[:BLK]
            own[0, block, :] = key_terms[BLK:]
            moved[1, other, :] = value_terms[:BLK]
            own[1, block, :] = value_terms[BLK:]
        dk_ref[:, head(h)] = (own[0] + moved[0]).astype(BF)
        dv_ref[:, head(h)] = (own[1] + moved[1]).astype(BF)


def row_backward(q, k, v, g, pattern):
    whole = jax.ShapeDtypeStruct((COLS, 2 * HALF), BF)
    return pl.pallas_call(
        row_backward_kernel,
        grid=(1,),
        out_shape=(whole, whole, whole),
        in_specs=[SMEM_SPEC] + [first_half()] * 4,
        out_specs=(first_half(),) * 3,
        scratch_shapes=[pltpu.VMEM((2, COLS, HD), F32), pltpu.VMEM((2, COLS, HD), F32)],
        compiler_params=params(),
        cost_estimate=cost(16 * 10 * BLK * 2 * BLK * HD, 7 * COLS * HALF * 2, 16 * BLK * 2 * BLK),
        name="row_backward",
    )(pattern, q, k, v, g)


def finish_kernel(off_ref, b_ref, dq_in, dk_in, dv_in, dq_ref, dk_ref, dv_ref):
    dq_ref[...] = b_ref[:, :HALF]
    for h in range(HC):
        pair = jnp.concatenate([b_ref[:, head(HC + h)], b_ref[:, head(2 * HC + h)]], axis=1)
        back = t_mm(shift_selector(off_ref[h]), pair).astype(BF)
        dk_ref[:, head(h)] = back[:, :HD]
        dv_ref[:, head(h)] = back[:, HD:]


def finish(back, dq, dk, dv, offset):
    whole = jax.ShapeDtypeStruct((COLS, 2 * HALF), BF)
    kept = pl.BlockSpec(memory_space=pl.ANY)
    second = pl.BlockSpec((COLS, HALF), lambda i: (0, 1))
    return pl.pallas_call(
        finish_kernel,
        grid=(1,),
        out_shape=(whole, whole, whole),
        in_specs=[SMEM_SPEC, pl.BlockSpec((COLS, 3 * HALF), lambda i: (0, 0)), kept, kept, kept],
        out_specs=(second, second, second),
        input_output_aliases={2: 0, 3: 1, 4: 2},
        compiler_params=params(),
        cost_estimate=cost(2 * COLS * COLS * 2 * HALF, 6 * COLS * HALF * 2),
        name="finish",
    )(offset, back, dq, dk, dv)


def attn_grad_kernel(place, og_mine, og_theirs, mine_ref, theirs_ref, row_ref, send_ref):
    total = mm_t(og_mine[...], mine_ref[...]) + mm_t(og_theirs[...], theirs_ref[...])
    total = total.astype(BF)

    @pl.when(pl.program_id(0) < 2)
    def _():
        row_ref[...] = total

    @pl.when(pl.program_id(0) >= 2)
    def _():
        send_ref[...] = total


def attn_grad_of(og, mine, theirs, place):
    steps = 4
    rows = 2 * HALF // steps
    return pl.pallas_call(
        attn_grad_kernel,
        grid_spec=pltpu.PrefetchScalarGridSpec(
            num_scalar_prefetch=1,
            grid=(steps,),
            in_specs=[
                pl.BlockSpec((COLS, DH), lambda i, at: (0, at[0])),
                pl.BlockSpec((COLS, DH), lambda i, at: (0, 1 - at[0])),
                pl.BlockSpec((rows, DH), lambda i, at: (i, 0)),
                pl.BlockSpec((rows, DH), lambda i, at: (i, 0)),
            ],
            out_specs=(
                pl.BlockSpec((COLS, rows), lambda i, at: (0, jnp.minimum(i, 1))),
                pl.BlockSpec((COLS, rows), lambda i, at: (0, jnp.maximum(i, 2) - 2)),
            ),
        ),
        out_shape=(jax.ShapeDtypeStruct((COLS, HALF), BF),) * 2,
        compiler_params=params(),
        cost_estimate=cost(2 * COLS * 2 * HALF * D, 7 * 2**20),
        name="attn_grad",
    )(place, og, og, mine, theirs)


def layer_out_kernel(core_ref, row_ref, col_ref, mine_ref, theirs_ref, o_ref):
    def product(w_ref):
        total = mm(row_ref[...], w_ref[:HALF, :]) + mm(col_ref[...], w_ref[HALF:, :])
        o_ref[...] = total.astype(BF)

    pl.when(pl.program_id(0) == 0)(lambda: product(mine_ref))
    pl.when(pl.program_id(0) == 1)(lambda: product(theirs_ref))


def layer_out_of(row_out, col_out, mine, theirs, core):
    steps = 2
    width = DH // steps

    def place(half, i, c):
        which = jnp.where(half == 0, c[0], 1 - c[0])
        return (0, which * steps + i)

    return pl.pallas_call(
        layer_out_kernel,
        grid_spec=pltpu.PrefetchScalarGridSpec(
            num_scalar_prefetch=1,
            grid=(2, steps),
            in_specs=[
                pl.BlockSpec((COLS, HALF), lambda half, i, c: (0, 0)),
                pl.BlockSpec((COLS, HALF), lambda half, i, c: (0, 0)),
                pl.BlockSpec((2 * HALF, width), lambda half, i, c: (0, jnp.where(half == 0, i, steps - 1))),
                pl.BlockSpec((2 * HALF, width), lambda half, i, c: (0, jnp.where(half == 0, 0, i))),
            ],
            out_specs=pl.BlockSpec((COLS, width), place),
        ),
        out_shape=jax.ShapeDtypeStruct((COLS, D), BF),
        compiler_params=params(),
        cost_estimate=cost(2 * COLS * 2 * HALF * D, 7 * 2**20),
        name="layer_out",
    )(core, row_out, col_out, mine, theirs)


def weight_grad_kernel(place, row_mine, row_theirs, col_mine, col_theirs, og_mine, og_theirs, *refs):
    outs, total = refs[:4], refs[4]
    step = pl.program_id(0)
    block = lax.rem(place[1] + step, 4)

    def product(a_ref, b_ref):
        total[...] = t_mm(a_ref[...], og_mine[...]) + t_mm(b_ref[...], og_theirs[...])

    pl.when(block < 2)(lambda: product(row_mine, row_theirs))
    pl.when(block >= 2)(lambda: product(col_mine, col_theirs))
    for target, out in enumerate(outs):

        @pl.when(step == target)
        def _(out=out):
            out[...] = total[...].astype(out.dtype)


def weight_grad_of(row_mine, row_theirs, col_mine, col_theirs, og, og_theirs, place):
    rows = 2 * HALF // 4

    def row_block(i, at):
        return (0, jnp.minimum(lax.rem(at[1] + i, 4), 1))

    def col_block(i, at):
        return (0, jnp.maximum(lax.rem(at[1] + i, 4), 2) - 2)

    return pl.pallas_call(
        weight_grad_kernel,
        grid_spec=pltpu.PrefetchScalarGridSpec(
            num_scalar_prefetch=1,
            grid=(4,),
            in_specs=[
                pl.BlockSpec((COLS, rows), row_block),
                pl.BlockSpec((COLS, rows), row_block),
                pl.BlockSpec((COLS, rows), col_block),
                pl.BlockSpec((COLS, rows), col_block),
                pl.BlockSpec((COLS, DH), lambda i, at: (0, at[0])),
                pl.BlockSpec((COLS, DH), lambda i, at: (0, 0)),
            ],
            out_specs=(pl.BlockSpec((rows, DH), lambda i, at: (0, 0)),) * 4,
            scratch_shapes=[pltpu.VMEM((rows, DH), F32)],
        ),
        out_shape=(jax.ShapeDtypeStruct((rows, DH), F32),) + (jax.ShapeDtypeStruct((rows, DH), BF),) * 3,
        compiler_params=params(),
        cost_estimate=cost(4 * COLS * 2 * HALF * DH, 7 * 2**20),
        name="weight_grad",
    )(place, row_mine, row_theirs, col_mine, col_theirs, og, og_theirs)


def gather_kernel(place, own_ref, a_ref, b_ref, c_ref, o_ref):
    chunk = own_ref.shape[0] // 2
    for step, ref in enumerate((own_ref, a_ref, b_ref, c_ref)):
        source = lax.rem(place[3] + 4 - step, 4)
        for at_z in range(2):
            rows = pl.ds(pl.multiple_of((at_z * 4 + source) * chunk, chunk), chunk)
            o_ref[rows, :] = ref[at_z * chunk : (at_z + 1) * chunk, :]


def gather_y(own, place):
    blocks = [own] + [along(own, "y", step) for step in (1, 2, 3)]
    return pl.pallas_call(
        gather_kernel,
        out_shape=jax.ShapeDtypeStruct((4 * own.shape[0], DH), BF),
        in_specs=[SMEM_SPEC] + [VMEM_SPEC] * 4,
        out_specs=VMEM_SPEC,
        compiler_params=params(),
        cost_estimate=cost(0, 2**20),
        name="gather_y",
    )(place, *blocks)


def weight_sum_kernel(place, a_ref, b_ref, c_ref, d_ref, *outs):
    chunk = 2 * HD // 8
    for step, out in enumerate(outs):
        at_y = lax.rem(place[3] + step, 4)
        for at_z in range(2):
            rows = pl.ds(pl.multiple_of(at_z * HD + at_y * chunk, chunk), chunk)
            near = a_ref[rows, :] + b_ref[rows, :].astype(F32)
            far = c_ref[rows, :].astype(F32) + d_ref[rows, :].astype(F32)
            out[at_z * chunk : (at_z + 1) * chunk, :] = (near + far).astype(out.dtype)


def weight_sum(parts, place):
    rows = parts[0].shape[0] // 4
    return pl.pallas_call(
        weight_sum_kernel,
        out_shape=(jax.ShapeDtypeStruct((rows, DH), F32),) + (jax.ShapeDtypeStruct((rows, DH), BF),) * 3,
        in_specs=[SMEM_SPEC] + [VMEM_SPEC] * 4,
        out_specs=(VMEM_SPEC,) * 4,
        compiler_params=params(),
        cost_estimate=cost(16 * rows * DH, 4 * 2**20),
        name="weight_sum",
    )(place, *parts)


def y_sum_kernel(place, a_ref, b_ref, c_ref, d_ref, *refs):
    outs, total = refs[:-1], refs[-1]
    near = a_ref[...] + b_ref[...].astype(F32)
    total[...] = near + (c_ref[...].astype(F32) + d_ref[...].astype(F32))
    rows = outs[0].shape[0]
    for step, out in enumerate(outs):
        target = lax.rem(place[2] + step // 4, 2) * 4 + lax.rem(place[4] + step % 4, 4)
        out[...] = total[pl.ds(pl.multiple_of(target * rows, rows), rows), :].astype(out.dtype)


def y_sum(parts, place):
    rows = parts[0].shape[0] // 8
    return pl.pallas_call(
        y_sum_kernel,
        out_shape=(jax.ShapeDtypeStruct((rows, DH), F32),) + (jax.ShapeDtypeStruct((rows, DH), BF),) * 7,
        in_specs=[SMEM_SPEC] + [VMEM_SPEC] * 4,
        out_specs=(VMEM_SPEC,) * 8,
        scratch_shapes=[pltpu.VMEM(parts[0].shape, F32)],
        compiler_params=params(),
        cost_estimate=cost(32 * rows * DH, 2**20),
        name="y_sum",
    )(place, *parts)


def z_sum_kernel(place, *refs):
    ins, (keep_ref, send_ref) = refs[:8], refs[8:]
    total = ins[0][...]
    for ref in ins[1:]:
        total = total + ref[...].astype(F32)
    half = keep_ref.shape[0]
    first = jnp.broadcast_to(place[0], (half, DH)) == 0
    keep_ref[...] = jnp.where(first, total[:half], total[half:])
    send_ref[...] = jnp.where(first, total[half:], total[:half])


def z_sum(parts, place):
    out = jax.ShapeDtypeStruct((parts[0].shape[0] // 2, DH), F32)
    return pl.pallas_call(
        z_sum_kernel,
        out_shape=(out, out),
        in_specs=[SMEM_SPEC] + [VMEM_SPEC] * 8,
        out_specs=(VMEM_SPEC, VMEM_SPEC),
        compiler_params=params(),
        cost_estimate=cost(8 * 8 * DH, 2**18),
        name="z_sum",
    )(place, *parts)


def exchange(tensor, axes):
    return lax.all_to_all(tensor, axes, split_axis=0, concat_axis=0, tiled=True)


def other_core(tensor):
    return lax.ppermute(tensor, "c", [(0, 1), (1, 0)])


def together(*values):
    return lax.optimization_barrier(values)


def along(tensor, axis, step):
    return lax.ppermute(tensor, axis, [(i, (i + step) % 4) for i in range(4)])


def along_z(tensor, step):
    turns = [(z * 4 + h, (z + step // 4) % 2 * 4 + (h + step % 4) % 4) for z in range(2) for h in range(4)]
    return lax.ppermute(tensor, ("zl", "zh"), turns)


def shards(queries, keys, values, out_proj, out_grad, block_pattern, col_offset):
    q, k, v = (t.reshape(COLS, 2 * HALF) for t in (queries, keys, values))
    og = out_grad.reshape(COLS, D)
    rows_of = out_proj.shape[0]
    seq = ROWS
    near = seq // 2
    dp = lax.axis_size("x") * lax.axis_size("zl")
    core = lax.axis_index("c").astype(jnp.int32)
    place = jnp.stack([core] + [lax.axis_index(name).astype(jnp.int32) for name in ("x", "zl", "y", "zh")])

    halves = out_proj.reshape(rows_of, 2, DH).transpose(1, 0, 2)
    spread = jnp.broadcast_to(halves[None], (near // 2, 2, rows_of, DH)).reshape(near, rows_of, DH)
    own_rows = exchange(spread, NEAR)
    packed = pack(q, k, v, col_offset)
    og_sent = lax.dynamic_slice(og, (0, (1 - core) * DH), (COLS, DH))
    own_rows, packed, og_sent = together(own_rows, packed, og_sent)
    own_rows = own_rows.reshape(near * rows_of, DH)
    mine = lax.all_gather(gather_y(own_rows, place), "x", axis=0, tiled=True)

    received = exchange(packed.reshape(seq, COLS // seq, 3 * HALF), SEQ)
    row_out = row_forward(q, k, v, block_pattern)
    row_theirs = other_core(row_out)
    received = received.reshape(ROWS, 2, GRP, 3 * HALF)

    col_sent = column_forward(received).reshape(seq, COLS // seq, HALF)
    col_sent, mine, row_out, row_theirs = together(col_sent, mine, row_out, row_theirs)
    col_mine = exchange(col_sent, SEQ)
    theirs = other_core(mine)
    grad_rows, grad_cols = attn_grad_of(og, mine, theirs, place)
    dq, dk, dv = row_backward(q, k, v, grad_rows, block_pattern)
    og_theirs = other_core(og_sent)
    col_mine, grad_cols, og_theirs, dq, dk, dv = together(col_mine, grad_cols, og_theirs, dq, dk, dv)
    col_mine = col_mine.reshape(COLS, HALF)

    col_grads = exchange(grad_cols.reshape(seq, COLS // seq, HALF), SEQ)
    col_theirs = other_core(col_mine)
    parts = weight_grad_of(row_out, row_theirs, col_mine, col_theirs, og, og_theirs, place)
    next_x, last_x = along(parts[1], "x", 1), along(parts[3], "x", 3)
    col_grads, next_x, last_x = together(col_grads, next_x, last_x)

    col_back = column_backward(received, col_grads.reshape(ROWS, 2, GRP, HALF)).reshape(seq, COLS // seq, 3 * HALF)
    back = exchange(col_back, SEQ).reshape(COLS, 3 * HALF)

    layer = layer_out_of(row_out, col_mine, mine, theirs, place)
    far_x, layer = together(along(parts[2], "x", 2), layer)
    parts = weight_sum([parts[0], next_x, far_x, last_x], place)
    parts = [parts[0]] + [along(parts[step], "y", step) for step in (1, 2, 3)]
    parts = y_sum(parts, place)
    parts = [parts[0]] + [along_z(parts[step], step) for step in range(1, 8)]
    keep, give = z_sum(parts, place)
    taken = other_core(give)
    first = core == 0
    tokens = COLS * seq * dp
    w_grad = jnp.concatenate([jnp.where(first, keep, taken), jnp.where(first, taken, keep)], axis=1)
    w_grad = w_grad * tokens ** (-0.5)

    dq, dk, dv = finish(back, dq, dk, dv, col_offset)
    lead = (1, 1, COLS)
    return (
        layer.reshape(lead + (D,)),
        dq.reshape(lead + (2 * HALF,)),
        dk.reshape(lead + (2 * HALF,)),
        dv.reshape(lead + (2 * HALF,)),
        w_grad,
    )


def solution(mesh):
    fine = Mesh(mesh.devices.reshape(4, 2, 4, 4, 2), DP + SEQ)
    token = P(DP, SEQ, None, None)
    rows = P(DP + SEQ, None)
    in_specs = (token, token, token, rows, token, P(), P())
    out_specs = (token, token, token, token, rows)
    return jax.shard_map(shards, mesh=fine, in_specs=in_specs, out_specs=out_specs, check_vma=False)
```

```python
import functools

import jax
import jax.numpy as jnp
from jax import lax
from jax.experimental import pallas as pl
from jax.experimental.pallas import tpu as pltpu
from jax.sharding import Mesh, PartitionSpec as P

HD = 128
HR = 4
HC = 4
BLK = 128
NB = 4
COLS = 512
HALF = HR * HD
D = 2048
DH = D // 2
SCALE = HD ** (-0.5)
BF = jnp.bfloat16
F32 = jnp.float32
GRP = 8
ROWS = 32
TILE = GRP * ROWS
VMEM_LIMIT = 50 * 1024 * 1024

DP = ("x", "zl")
SEQ = ("y", "zh", "c")
NEAR = ("zl", "zh", "c")


def mm(a, b):
    return lax.dot_general(a, b, (((1,), (0,)), ((), ())), preferred_element_type=F32)


def mm_t(a, b):
    return lax.dot_general(a, b, (((1,), (1,)), ((), ())), preferred_element_type=F32)


def t_mm(a, b):
    return lax.dot_general(a, b, (((0,), (0,)), ((), ())), preferred_element_type=F32)


def params():
    return pltpu.CompilerParams(vmem_limit_bytes=VMEM_LIMIT)


def cost(flops, nbytes, trans=0):
    return pl.CostEstimate(flops=int(flops), transcendentals=int(trans), bytes_accessed=int(nbytes))


SMEM_SPEC = pl.BlockSpec(memory_space=pltpu.SMEM)
VMEM_SPEC = pl.BlockSpec(memory_space=pltpu.VMEM)


def head(index):
    return slice(index * HD, (index + 1) * HD)


def shift_selector(offset):
    row = lax.broadcasted_iota(jnp.int32, (COLS, COLS), 0)
    col = lax.broadcasted_iota(jnp.int32, (COLS, COLS), 1)
    source = row - offset
    source = jnp.where(source < 0, source + COLS, source)
    return jnp.where(source == col, 1.0, 0.0).astype(BF)


def pack_kernel(off_ref, q_ref, k_ref, v_ref, o_ref):
    o_ref[:, :HALF] = q_ref[...]
    for h in range(HC):
        pair = jnp.concatenate([k_ref[:, head(h)], v_ref[:, head(h)]], axis=1)
        moved = mm(shift_selector(off_ref[h]), pair).astype(BF)
        o_ref[:, head(HC + h)] = moved[:, :HD]
        o_ref[:, head(2 * HC + h)] = moved[:, HD:]


def pack(q, k, v, offset):
    half = pl.BlockSpec((COLS, HALF), lambda i: (0, 1))
    return pl.pallas_call(
        pack_kernel,
        grid=(1,),
        out_shape=jax.ShapeDtypeStruct((COLS, 3 * HALF), BF),
        in_specs=[SMEM_SPEC, half, half, half],
        out_specs=pl.BlockSpec((COLS, 3 * HALF), lambda i: (0, 0)),
        compiler_params=params(),
        cost_estimate=cost(2 * COLS * COLS * 2 * HALF, 6 * COLS * HALF * 2),
        name="pack",
    )(offset, q, k, v)


def tile_of(ref, lane):
    tile = ref[:, 0, :, lane * HD : (lane + 1) * HD]
    return tile.astype(F32).reshape(TILE, HD).astype(BF)


def store_tile(ref, lane, value):
    ref[:, 0, :, lane * HD : (lane + 1) * HD] = value.reshape(ROWS, GRP, HD).astype(BF)


def column_mask():
    row = lax.broadcasted_iota(jnp.int32, (TILE, TILE), 0)
    col = lax.broadcasted_iota(jnp.int32, (TILE, TILE), 1)
    return lax.rem(row, GRP) == lax.rem(col, GRP)


def softmax(scores):
    e = jnp.exp(scores - jnp.max(scores, axis=-1, keepdims=True))
    return e / jnp.sum(e, axis=-1, keepdims=True)


def column_probs(r_ref, h, mask):
    q = tile_of(r_ref, h)
    k = tile_of(r_ref, HC + h)
    v = tile_of(r_ref, 2 * HC + h)
    return q, k, v, softmax(jnp.where(mask, mm_t(q, k) * SCALE, -1e30))


def column_forward_kernel(r_ref, o_ref):
    mask = column_mask()
    for h in range(HC):
        _, _, v, probs = column_probs(r_ref, h, mask)
        store_tile(o_ref, h, mm(probs.astype(BF), v))


def group_block(lanes):
    return pl.BlockSpec((ROWS, 1, GRP, lanes), lambda i: (0, i, 0, 0))


def column_forward(received):
    return pl.pallas_call(
        column_forward_kernel,
        grid=(2,),
        out_shape=jax.ShapeDtypeStruct((ROWS, 2, GRP, HALF), BF),
        in_specs=[group_block(3 * HALF)],
        out_specs=group_block(HALF),
        compiler_params=params(),
        cost_estimate=cost(10**11, 4 * COLS * HALF * 2, 8 * TILE * TILE),
        name="column_forward",
    )(received)


def column_backward_kernel(r_ref, g_ref, o_ref):
    mask = column_mask()
    for h in range(HC):
        q, k, v, probs = column_probs(r_ref, h, mask)
        g = tile_of(g_ref, h)
        store_tile(o_ref, 2 * HC + h, t_mm(probs.astype(BF), g))
        prob_grad = mm_t(g, v)
        delta = jnp.sum(probs * prob_grad, axis=-1, keepdims=True)
        score_grad = (probs * (prob_grad - delta)).astype(BF)
        store_tile(o_ref, h, mm(score_grad, k) * SCALE)
        store_tile(o_ref, HC + h, t_mm(score_grad, q) * SCALE)


def column_backward(received, grads):
    return pl.pallas_call(
        column_backward_kernel,
        grid=(2,),
        out_shape=jax.ShapeDtypeStruct((ROWS, 2, GRP, 3 * HALF), BF),
        in_specs=[group_block(3 * HALF), group_block(HALF)],
        out_specs=group_block(3 * HALF),
        compiler_params=params(),
        cost_estimate=cost(8 * 10 * TILE * TILE * HD, 7 * COLS * HALF * 2, 8 * TILE * TILE),
        name="column_backward",
    )(received, grads)


def row_tile(pat_ref, q_ref, k_ref, v_ref, h, j):
    block = slice(j * BLK, (j + 1) * BLK)
    other = pl.ds(pl.multiple_of(pat_ref[h, j] * BLK, BLK), BLK)
    q = q_ref[block, head(h)]
    k = jnp.concatenate([k_ref[other, head(h)], k_ref[block, head(h)]], axis=0)
    v = jnp.concatenate([v_ref[other, head(h)], v_ref[block, head(h)]], axis=0)
    return block, other, q, k, v, softmax(mm_t(q, k) * SCALE)


def row_forward_kernel(pat_ref, q_ref, k_ref, v_ref, o_ref):
    for h in range(HR):
        for j in range(NB):
            block, _, _, _, v, probs = row_tile(pat_ref, q_ref, k_ref, v_ref, h, j)
            o_ref[block, head(h)] = mm(probs.astype(BF), v).astype(BF)


def first_half():
    return pl.BlockSpec((COLS, HALF), lambda i: (0, 0))


def row_forward(q, k, v, pattern):
    return pl.pallas_call(
        row_forward_kernel,
        grid=(1,),
        out_shape=jax.ShapeDtypeStruct((COLS, HALF), BF),
        in_specs=[SMEM_SPEC, first_half(), first_half(), first_half()],
        out_specs=first_half(),
        compiler_params=params(),
        cost_estimate=cost(16 * 4 * BLK * 2 * BLK * HD, 4 * COLS * HALF * 2, 16 * BLK * 2 * BLK),
        name="row_forward",
    )(pattern, q, k, v)


def row_backward_kernel(pat_ref, q_ref, k_ref, v_ref, g_ref, dq_ref, dk_ref, dv_ref, own, moved):
    for h in range(HR):
        for j in range(NB):
            block, other, q, k, v, probs = row_tile(pat_ref, q_ref, k_ref, v_ref, h, j)
            g = g_ref[block, head(h)]
            value_terms = t_mm(probs.astype(BF), g)
            prob_grad = mm_t(g, v)
            delta = jnp.sum(probs * prob_grad, axis=-1, keepdims=True)
            score_grad = (probs * (prob_grad - delta)).astype(BF)
            dq_ref[block, head(h)] = (mm(score_grad, k) * SCALE).astype(BF)
            key_terms = t_mm(score_grad, q) * SCALE
            moved[0, other, :] = key_terms[:BLK]
            own[0, block, :] = key_terms[BLK:]
            moved[1, other, :] = value_terms[:BLK]
            own[1, block, :] = value_terms[BLK:]
        dk_ref[:, head(h)] = (own[0] + moved[0]).astype(BF)
        dv_ref[:, head(h)] = (own[1] + moved[1]).astype(BF)


def row_backward(q, k, v, g, pattern):
    whole = jax.ShapeDtypeStruct((COLS, 2 * HALF), BF)
    return pl.pallas_call(
        row_backward_kernel,
        grid=(1,),
        out_shape=(whole, whole, whole),
        in_specs=[SMEM_SPEC] + [first_half()] * 4,
        out_specs=(first_half(),) * 3,
        scratch_shapes=[pltpu.VMEM((2, COLS, HD), F32), pltpu.VMEM((2, COLS, HD), F32)],
        compiler_params=params(),
        cost_estimate=cost(16 * 10 * BLK * 2 * BLK * HD, 7 * COLS * HALF * 2, 16 * BLK * 2 * BLK),
        name="row_backward",
    )(pattern, q, k, v, g)


def finish_kernel(off_ref, b_ref, dq_in, dk_in, dv_in, dq_ref, dk_ref, dv_ref):
    dq_ref[...] = b_ref[:, :HALF]
    for h in range(HC):
        pair = jnp.concatenate([b_ref[:, head(HC + h)], b_ref[:, head(2 * HC + h)]], axis=1)
        back = t_mm(shift_selector(off_ref[h]), pair).astype(BF)
        dk_ref[:, head(h)] = back[:, :HD]
        dv_ref[:, head(h)] = back[:, HD:]


def finish(back, dq, dk, dv, offset):
    whole = jax.ShapeDtypeStruct((COLS, 2 * HALF), BF)
    kept = pl.BlockSpec(memory_space=pl.ANY)
    second = pl.BlockSpec((COLS, HALF), lambda i: (0, 1))
    return pl.pallas_call(
        finish_kernel,
        grid=(1,),
        out_shape=(whole, whole, whole),
        in_specs=[SMEM_SPEC, pl.BlockSpec((COLS, 3 * HALF), lambda i: (0, 0)), kept, kept, kept],
        out_specs=(second, second, second),
        input_output_aliases={2: 0, 3: 1, 4: 2},
        compiler_params=params(),
        cost_estimate=cost(2 * COLS * COLS * 2 * HALF, 6 * COLS * HALF * 2),
        name="finish",
    )(offset, back, dq, dk, dv)


def attn_grad_kernel(place, og_mine, og_theirs, mine_ref, theirs_ref, row_ref, send_ref):
    total = mm_t(og_mine[...], mine_ref[...]) + mm_t(og_theirs[...], theirs_ref[...])
    total = total.astype(BF)

    @pl.when(pl.program_id(0) < 2)
    def _():
        row_ref[...] = total

    @pl.when(pl.program_id(0) >= 2)
    def _():
        send_ref[...] = total


def attn_grad_of(og, mine, theirs, place):
    steps = 4
    rows = 2 * HALF // steps
    return pl.pallas_call(
        attn_grad_kernel,
        grid_spec=pltpu.PrefetchScalarGridSpec(
            num_scalar_prefetch=1,
            grid=(steps,),
            in_specs=[
                pl.BlockSpec((COLS, DH), lambda i, at: (0, at[0])),
                pl.BlockSpec((COLS, DH), lambda i, at: (0, 1 - at[0])),
                pl.BlockSpec((rows, DH), lambda i, at: (i, 0)),
                pl.BlockSpec((rows, DH), lambda i, at: (i, 0)),
            ],
            out_specs=(
                pl.BlockSpec((COLS, rows), lambda i, at: (0, jnp.minimum(i, 1))),
                pl.BlockSpec((COLS, rows), lambda i, at: (0, jnp.maximum(i, 2) - 2)),
            ),
        ),
        out_shape=(jax.ShapeDtypeStruct((COLS, HALF), BF),) * 2,
        compiler_params=params(),
        cost_estimate=cost(2 * COLS * 2 * HALF * D, 7 * 2**20),
        name="attn_grad",
    )(place, og, og, mine, theirs)


def layer_out_kernel(core_ref, row_ref, col_ref, mine_ref, theirs_ref, o_ref):
    def product(w_ref):
        total = mm(row_ref[...], w_ref[:HALF, :]) + mm(col_ref[...], w_ref[HALF:, :])
        o_ref[...] = total.astype(BF)

    pl.when(pl.program_id(0) == 0)(lambda: product(mine_ref))
    pl.when(pl.program_id(0) == 1)(lambda: product(theirs_ref))


def layer_out_of(row_out, col_out, mine, theirs, core):
    steps = 2
    width = DH // steps

    def place(half, i, c):
        which = jnp.where(half == 0, c[0], 1 - c[0])
        return (0, which * steps + i)

    return pl.pallas_call(
        layer_out_kernel,
        grid_spec=pltpu.PrefetchScalarGridSpec(
            num_scalar_prefetch=1,
            grid=(2, steps),
            in_specs=[
                pl.BlockSpec((COLS, HALF), lambda half, i, c: (0, 0)),
                pl.BlockSpec((COLS, HALF), lambda half, i, c: (0, 0)),
                pl.BlockSpec((2 * HALF, width), lambda half, i, c: (0, jnp.where(half == 0, i, steps - 1))),
                pl.BlockSpec((2 * HALF, width), lambda half, i, c: (0, jnp.where(half == 0, 0, i))),
            ],
            out_specs=pl.BlockSpec((COLS, width), place),
        ),
        out_shape=jax.ShapeDtypeStruct((COLS, D), BF),
        compiler_params=params(),
        cost_estimate=cost(2 * COLS * 2 * HALF * D, 7 * 2**20),
        name="layer_out",
    )(core, row_out, col_out, mine, theirs)


def weight_grad_kernel(place, row_mine, row_theirs, col_mine, col_theirs, og_mine, og_theirs, *refs):
    outs, total = refs[:4], refs[4]
    step = pl.program_id(0)
    block = lax.rem(place[1] + step, 4)

    def product(a_ref, b_ref):
        total[...] = t_mm(a_ref[...], og_mine[...]) + t_mm(b_ref[...], og_theirs[...])

    pl.when(block < 2)(lambda: product(row_mine, row_theirs))
    pl.when(block >= 2)(lambda: product(col_mine, col_theirs))
    for target, out in enumerate(outs):

        @pl.when(step == target)
        def _(out=out):
            out[...] = total[...].astype(out.dtype)


def weight_grad_of(row_mine, row_theirs, col_mine, col_theirs, og, og_theirs, place):
    rows = 2 * HALF // 4

    def row_block(i, at):
        return (0, jnp.minimum(lax.rem(at[1] + i, 4), 1))

    def col_block(i, at):
        return (0, jnp.maximum(lax.rem(at[1] + i, 4), 2) - 2)

    return pl.pallas_call(
        weight_grad_kernel,
        grid_spec=pltpu.PrefetchScalarGridSpec(
            num_scalar_prefetch=1,
            grid=(4,),
            in_specs=[
                pl.BlockSpec((COLS, rows), row_block),
                pl.BlockSpec((COLS, rows), row_block),
                pl.BlockSpec((COLS, rows), col_block),
                pl.BlockSpec((COLS, rows), col_block),
                pl.BlockSpec((COLS, DH), lambda i, at: (0, at[0])),
                pl.BlockSpec((COLS, DH), lambda i, at: (0, 0)),
            ],
            out_specs=(pl.BlockSpec((rows, DH), lambda i, at: (0, 0)),) * 4,
            scratch_shapes=[pltpu.VMEM((rows, DH), F32)],
        ),
        out_shape=(jax.ShapeDtypeStruct((rows, DH), F32),) + (jax.ShapeDtypeStruct((rows, DH), BF),) * 3,
        compiler_params=params(),
        cost_estimate=cost(4 * COLS * 2 * HALF * DH, 7 * 2**20),
        name="weight_grad",
    )(place, row_mine, row_theirs, col_mine, col_theirs, og, og_theirs)


def gather_kernel(axis, pieces, place, own_ref, a_ref, b_ref, c_ref, o_ref):
    chunk = own_ref.shape[0] // pieces
    for step, ref in enumerate((own_ref, a_ref, b_ref, c_ref)):
        source = lax.rem(place[axis] + 4 - step, 4)
        for piece in range(pieces):
            rows = pl.ds(pl.multiple_of((piece * 4 + source) * chunk, chunk), chunk)
            o_ref[rows, :] = ref[piece * chunk : (piece + 1) * chunk, :]


def blocks_of(own, axis):
    return [own] + [along(own, axis, step) for step in (1, 2, 3)]


def gather_of(blocks, place, axis, index, pieces):
    return pl.pallas_call(
        functools.partial(gather_kernel, index, pieces),
        out_shape=jax.ShapeDtypeStruct((4 * blocks[0].shape[0], DH), BF),
        in_specs=[SMEM_SPEC] + [VMEM_SPEC] * 4,
        out_specs=VMEM_SPEC,
        compiler_params=params(),
        cost_estimate=cost(0, 16 * blocks[0].shape[0] * DH),
        name="gather_" + axis,
    )(place, *blocks)


def weight_sum_kernel(place, a_ref, b_ref, c_ref, d_ref, *outs):
    chunk = 2 * HD // 8
    for step, out in enumerate(outs):
        at_y = lax.rem(place[3] + step, 4)
        for at_z in range(2):
            rows = pl.ds(pl.multiple_of(at_z * HD + at_y * chunk, chunk), chunk)
            near = a_ref[rows, :] + b_ref[rows, :].astype(F32)
            far = c_ref[rows, :].astype(F32) + d_ref[rows, :].astype(F32)
            out[at_z * chunk : (at_z + 1) * chunk, :] = (near + far).astype(out.dtype)


def weight_sum(parts, place):
    rows = parts[0].shape[0] // 4
    return pl.pallas_call(
        weight_sum_kernel,
        out_shape=(jax.ShapeDtypeStruct((rows, DH), F32),) + (jax.ShapeDtypeStruct((rows, DH), BF),) * 3,
        in_specs=[SMEM_SPEC] + [VMEM_SPEC] * 4,
        out_specs=(VMEM_SPEC,) * 4,
        compiler_params=params(),
        cost_estimate=cost(16 * rows * DH, 4 * 2**20),
        name="weight_sum",
    )(place, *parts)


def y_sum_kernel(place, a_ref, b_ref, c_ref, d_ref, *refs):
    outs, total = refs[:-1], refs[-1]
    near = a_ref[...] + b_ref[...].astype(F32)
    total[...] = near + (c_ref[...].astype(F32) + d_ref[...].astype(F32))
    rows = outs[0].shape[0]
    for step, out in enumerate(outs):
        target = lax.rem(place[2] + step // 4, 2) * 4 + lax.rem(place[4] + step % 4, 4)
        out[...] = total[pl.ds(pl.multiple_of(target * rows, rows), rows), :].astype(out.dtype)


def y_sum(parts, place):
    rows = parts[0].shape[0] // 8
    return pl.pallas_call(
        y_sum_kernel,
        out_shape=(jax.ShapeDtypeStruct((rows, DH), F32),) + (jax.ShapeDtypeStruct((rows, DH), BF),) * 7,
        in_specs=[SMEM_SPEC] + [VMEM_SPEC] * 4,
        out_specs=(VMEM_SPEC,) * 8,
        scratch_shapes=[pltpu.VMEM(parts[0].shape, F32)],
        compiler_params=params(),
        cost_estimate=cost(32 * rows * DH, 2**20),
        name="y_sum",
    )(place, *parts)


def z_sum_kernel(place, *refs):
    ins, (keep_ref, send_ref) = refs[:8], refs[8:]
    total = ins[0][...]
    for ref in ins[1:]:
        total = total + ref[...].astype(F32)
    half = keep_ref.shape[0]
    first = jnp.broadcast_to(place[0], (half, DH)) == 0
    keep_ref[...] = jnp.where(first, total[:half], total[half:])
    send_ref[...] = jnp.where(first, total[half:], total[:half])


def z_sum(parts, place):
    out = jax.ShapeDtypeStruct((parts[0].shape[0] // 2, DH), F32)
    return pl.pallas_call(
        z_sum_kernel,
        out_shape=(out, out),
        in_specs=[SMEM_SPEC] + [VMEM_SPEC] * 8,
        out_specs=(VMEM_SPEC, VMEM_SPEC),
        compiler_params=params(),
        cost_estimate=cost(8 * 8 * DH, 2**18),
        name="z_sum",
    )(place, *parts)


def exchange(tensor, axes):
    return lax.all_to_all(tensor, axes, split_axis=0, concat_axis=0, tiled=True)


def other_core(tensor):
    return lax.ppermute(tensor, "c", [(0, 1), (1, 0)])


def together(*values):
    return lax.optimization_barrier(values)


def along(tensor, axis, step):
    return lax.ppermute(tensor, axis, [(i, (i + step) % 4) for i in range(4)])


def along_z(tensor, step):
    turns = [(z * 4 + h, (z + step // 4) % 2 * 4 + (h + step % 4) % 4) for z in range(2) for h in range(4)]
    return lax.ppermute(tensor, ("zl", "zh"), turns)


def shards(queries, keys, values, out_proj, out_grad, block_pattern, col_offset):
    q, k, v = (t.reshape(COLS, 2 * HALF) for t in (queries, keys, values))
    og = out_grad.reshape(COLS, D)
    rows_of = out_proj.shape[0]
    seq = ROWS
    near = seq // 2
    dp = lax.axis_size("x") * lax.axis_size("zl")
    core = lax.axis_index("c").astype(jnp.int32)
    place = jnp.stack([core] + [lax.axis_index(name).astype(jnp.int32) for name in ("x", "zl", "y", "zh")])

    halves = out_proj.reshape(rows_of, 2, DH).transpose(1, 0, 2)
    spread = jnp.broadcast_to(halves[None], (near // 2, 2, rows_of, DH)).reshape(near, rows_of, DH)
    own_rows = exchange(spread, NEAR)
    packed = pack(q, k, v, col_offset)
    og_sent = lax.dynamic_slice(og, (0, (1 - core) * DH), (COLS, DH))
    own_rows, packed, og_sent = together(own_rows, packed, og_sent)
    own_rows = own_rows.reshape(near * rows_of, DH)
    blocks = blocks_of(gather_of(blocks_of(own_rows, "y"), place, "y", 3, 2), "x")

    received = exchange(packed.reshape(seq, COLS // seq, 3 * HALF), SEQ)
    received = received.reshape(ROWS, 2, GRP, 3 * HALF)

    col_sent = column_forward(received).reshape(seq, COLS // seq, HALF)
    row_out = row_forward(q, k, v, block_pattern)
    row_theirs = other_core(row_out)
    col_sent, row_out, row_theirs, *blocks = together(col_sent, row_out, row_theirs, *blocks)
    col_mine = exchange(col_sent, SEQ)
    mine = gather_of(blocks, place, "x", 1, 1)
    theirs = other_core(mine)
    og_theirs = other_core(og_sent)
    grad_rows, grad_cols = attn_grad_of(og, mine, theirs, place)
    col_mine, grad_cols, og_theirs = together(col_mine, grad_cols, og_theirs)
    col_mine = col_mine.reshape(COLS, HALF)

    col_grads = exchange(grad_cols.reshape(seq, COLS // seq, HALF), SEQ)
    col_theirs = other_core(col_mine)
    parts = weight_grad_of(row_out, row_theirs, col_mine, col_theirs, og, og_theirs, place)
    x_parts = [parts[0]] + [along(parts[step], "x", step) for step in (1, 3, 2)]
    dq, dk, dv = row_backward(q, k, v, grad_rows, block_pattern)
    col_grads, dq, dk, dv = together(col_grads, dq, dk, dv)

    col_back = column_backward(received, col_grads.reshape(ROWS, 2, GRP, HALF)).reshape(seq, COLS // seq, 3 * HALF)
    col_back, *x_parts = together(col_back, *x_parts)
    back = exchange(col_back, SEQ).reshape(COLS, 3 * HALF)

    parts = weight_sum(x_parts, place)
    layer = layer_out_of(row_out, col_mine, mine, theirs, place)
    parts = [parts[0]] + [along(parts[step], "y", step) for step in (1, 2, 3)]
    layer, *parts = together(layer, *parts)
    parts = y_sum(parts, place)
    parts = [parts[0]] + [along_z(parts[step], step) for step in range(1, 8)]
    keep, give = z_sum(parts, place)
    taken = other_core(give)
    first = core == 0
    tokens = COLS * seq * dp
    w_grad = jnp.concatenate([jnp.where(first, keep, taken), jnp.where(first, taken, keep)], axis=1)
    w_grad = w_grad * tokens ** (-0.5)

    dq, dk, dv = finish(back, dq, dk, dv, col_offset)
    lead = (1, 1, COLS)
    return (
        layer.reshape(lead + (D,)),
        dq.reshape(lead + (2 * HALF,)),
        dk.reshape(lead + (2 * HALF,)),
        dv.reshape(lead + (2 * HALF,)),
        w_grad,
    )


def solution(mesh):
    fine = Mesh(mesh.devices.reshape(4, 2, 4, 4, 2), DP + SEQ)
    token = P(DP, SEQ, None, None)
    rows = P(DP + SEQ, None)
    in_specs = (token, token, token, rows, token, P(), P())
    out_specs = (token, token, token, token, rows)
    return jax.shard_map(shards, mesh=fine, in_specs=in_specs, out_specs=out_specs, check_vma=False)
```

```python
import functools

import jax
import jax.numpy as jnp
from jax import lax
from jax.experimental import pallas as pl
from jax.experimental.pallas import tpu as pltpu
from jax.sharding import Mesh, PartitionSpec as P

HD = 128
HR = 4
HC = 4
BLK = 128
NB = 4
COLS = 512
HALF = HR * HD
D = 2048
DH = D // 2
SCALE = HD ** (-0.5)
BF = jnp.bfloat16
F32 = jnp.float32
GRP = 8
ROWS = 32
TILE = GRP * ROWS
VMEM_LIMIT = 50 * 1024 * 1024

DP = ("x", "zl")
SEQ = ("y", "zh", "c")
NEAR = ("zl", "zh", "c")


def mm(a, b):
    return lax.dot_general(a, b, (((1,), (0,)), ((), ())), preferred_element_type=F32)


def mm_t(a, b):
    return lax.dot_general(a, b, (((1,), (1,)), ((), ())), preferred_element_type=F32)


def t_mm(a, b):
    return lax.dot_general(a, b, (((0,), (0,)), ((), ())), preferred_element_type=F32)


def params():
    return pltpu.CompilerParams(vmem_limit_bytes=VMEM_LIMIT)


def cost(flops, nbytes, trans=0):
    return pl.CostEstimate(flops=int(flops), transcendentals=int(trans), bytes_accessed=int(nbytes))


SMEM_SPEC = pl.BlockSpec(memory_space=pltpu.SMEM)
VMEM_SPEC = pl.BlockSpec(memory_space=pltpu.VMEM)


def head(index):
    return slice(index * HD, (index + 1) * HD)


def shift_selector(offset):
    row = lax.broadcasted_iota(jnp.int32, (COLS, COLS), 0)
    col = lax.broadcasted_iota(jnp.int32, (COLS, COLS), 1)
    source = row - offset
    source = jnp.where(source < 0, source + COLS, source)
    return jnp.where(source == col, 1.0, 0.0).astype(BF)


def pack_kernel(off_ref, q_ref, k_ref, v_ref, o_ref):
    o_ref[:, :HALF] = q_ref[...]
    for h in range(HC):
        pair = jnp.concatenate([k_ref[:, head(h)], v_ref[:, head(h)]], axis=1)
        moved = mm(shift_selector(off_ref[h]), pair).astype(BF)
        o_ref[:, head(HC + h)] = moved[:, :HD]
        o_ref[:, head(2 * HC + h)] = moved[:, HD:]


def pack(q, k, v, offset):
    half = pl.BlockSpec((COLS, HALF), lambda i: (0, 1))
    return pl.pallas_call(
        pack_kernel,
        grid=(1,),
        out_shape=jax.ShapeDtypeStruct((COLS, 3 * HALF), BF),
        in_specs=[SMEM_SPEC, half, half, half],
        out_specs=pl.BlockSpec((COLS, 3 * HALF), lambda i: (0, 0)),
        compiler_params=params(),
        cost_estimate=cost(2 * COLS * COLS * 2 * HALF, 6 * COLS * HALF * 2),
        name="pack",
    )(offset, q, k, v)


def tile_of(ref, lane):
    tile = ref[:, 0, :, lane * HD : (lane + 1) * HD]
    return tile.astype(F32).reshape(TILE, HD).astype(BF)


def store_tile(ref, lane, value):
    ref[:, 0, :, lane * HD : (lane + 1) * HD] = value.reshape(ROWS, GRP, HD).astype(BF)


def column_mask():
    row = lax.broadcasted_iota(jnp.int32, (TILE, TILE), 0)
    col = lax.broadcasted_iota(jnp.int32, (TILE, TILE), 1)
    return lax.rem(row, GRP) == lax.rem(col, GRP)


def softmax(scores):
    e = jnp.exp(scores - jnp.max(scores, axis=-1, keepdims=True))
    return e / jnp.sum(e, axis=-1, keepdims=True)


def column_probs(r_ref, h, mask):
    q = tile_of(r_ref, h)
    k = tile_of(r_ref, HC + h)
    v = tile_of(r_ref, 2 * HC + h)
    return q, k, v, softmax(jnp.where(mask, mm_t(q, k) * SCALE, -1e30))


def column_forward_kernel(r_ref, o_ref):
    mask = column_mask()
    for h in range(HC):
        _, _, v, probs = column_probs(r_ref, h, mask)
        store_tile(o_ref, h, mm(probs.astype(BF), v))


def group_block(lanes):
    return pl.BlockSpec((ROWS, 1, GRP, lanes), lambda i: (0, i, 0, 0))


def column_forward(received):
    return pl.pallas_call(
        column_forward_kernel,
        grid=(2,),
        out_shape=jax.ShapeDtypeStruct((ROWS, 2, GRP, HALF), BF),
        in_specs=[group_block(3 * HALF)],
        out_specs=group_block(HALF),
        compiler_params=params(),
        cost_estimate=cost(10**11, 4 * COLS * HALF * 2, 8 * TILE * TILE),
        name="column_forward",
    )(received)


def column_backward_kernel(r_ref, g_ref, o_ref):
    mask = column_mask()
    for h in range(HC):
        q, k, v, probs = column_probs(r_ref, h, mask)
        g = tile_of(g_ref, h)
        store_tile(o_ref, 2 * HC + h, t_mm(probs.astype(BF), g))
        prob_grad = mm_t(g, v)
        delta = jnp.sum(probs * prob_grad, axis=-1, keepdims=True)
        score_grad = (probs * (prob_grad - delta)).astype(BF)
        store_tile(o_ref, h, mm(score_grad, k) * SCALE)
        store_tile(o_ref, HC + h, t_mm(score_grad, q) * SCALE)


def column_backward(received, grads):
    return pl.pallas_call(
        column_backward_kernel,
        grid=(2,),
        out_shape=jax.ShapeDtypeStruct((ROWS, 2, GRP, 3 * HALF), BF),
        in_specs=[group_block(3 * HALF), group_block(HALF)],
        out_specs=group_block(3 * HALF),
        compiler_params=params(),
        cost_estimate=cost(8 * 10 * TILE * TILE * HD, 7 * COLS * HALF * 2, 8 * TILE * TILE),
        name="column_backward",
    )(received, grads)


def row_tile(pat_ref, q_ref, k_ref, v_ref, h, j):
    block = slice(j * BLK, (j + 1) * BLK)
    other = pl.ds(pl.multiple_of(pat_ref[h, j] * BLK, BLK), BLK)
    q = q_ref[block, head(h)]
    k = jnp.concatenate([k_ref[other, head(h)], k_ref[block, head(h)]], axis=0)
    v = jnp.concatenate([v_ref[other, head(h)], v_ref[block, head(h)]], axis=0)
    return block, other, q, k, v, softmax(mm_t(q, k) * SCALE)


def row_forward_kernel(pat_ref, q_ref, k_ref, v_ref, o_ref):
    for h in range(HR):
        for j in range(NB):
            block, _, _, _, v, probs = row_tile(pat_ref, q_ref, k_ref, v_ref, h, j)
            o_ref[block, head(h)] = mm(probs.astype(BF), v).astype(BF)


def first_half():
    return pl.BlockSpec((COLS, HALF), lambda i: (0, 0))


def row_forward(q, k, v, pattern):
    return pl.pallas_call(
        row_forward_kernel,
        grid=(1,),
        out_shape=jax.ShapeDtypeStruct((COLS, HALF), BF),
        in_specs=[SMEM_SPEC, first_half(), first_half(), first_half()],
        out_specs=first_half(),
        compiler_params=params(),
        cost_estimate=cost(16 * 4 * BLK * 2 * BLK * HD, 4 * COLS * HALF * 2, 16 * BLK * 2 * BLK),
        name="row_forward",
    )(pattern, q, k, v)


def row_backward_kernel(pat_ref, q_ref, k_ref, v_ref, g_ref, dq_ref, dk_ref, dv_ref, own, moved):
    for h in range(HR):
        for j in range(NB):
            block, other, q, k, v, probs = row_tile(pat_ref, q_ref, k_ref, v_ref, h, j)
            g = g_ref[block, head(h)]
            value_terms = t_mm(probs.astype(BF), g)
            prob_grad = mm_t(g, v)
            delta = jnp.sum(probs * prob_grad, axis=-1, keepdims=True)
            score_grad = (probs * (prob_grad - delta)).astype(BF)
            dq_ref[block, head(h)] = (mm(score_grad, k) * SCALE).astype(BF)
            key_terms = t_mm(score_grad, q) * SCALE
            moved[0, other, :] = key_terms[:BLK]
            own[0, block, :] = key_terms[BLK:]
            moved[1, other, :] = value_terms[:BLK]
            own[1, block, :] = value_terms[BLK:]
        dk_ref[:, head(h)] = (own[0] + moved[0]).astype(BF)
        dv_ref[:, head(h)] = (own[1] + moved[1]).astype(BF)


def row_backward(q, k, v, g, pattern):
    whole = jax.ShapeDtypeStruct((COLS, 2 * HALF), BF)
    return pl.pallas_call(
        row_backward_kernel,
        grid=(1,),
        out_shape=(whole, whole, whole),
        in_specs=[SMEM_SPEC] + [first_half()] * 4,
        out_specs=(first_half(),) * 3,
        scratch_shapes=[pltpu.VMEM((2, COLS, HD), F32), pltpu.VMEM((2, COLS, HD), F32)],
        compiler_params=params(),
        cost_estimate=cost(16 * 10 * BLK * 2 * BLK * HD, 7 * COLS * HALF * 2, 16 * BLK * 2 * BLK),
        name="row_backward",
    )(pattern, q, k, v, g)


def finish_kernel(off_ref, b_ref, dq_in, dk_in, dv_in, dq_ref, dk_ref, dv_ref):
    dq_ref[...] = b_ref[:, :HALF]
    for h in range(HC):
        pair = jnp.concatenate([b_ref[:, head(HC + h)], b_ref[:, head(2 * HC + h)]], axis=1)
        back = t_mm(shift_selector(off_ref[h]), pair).astype(BF)
        dk_ref[:, head(h)] = back[:, :HD]
        dv_ref[:, head(h)] = back[:, HD:]


def finish(back, dq, dk, dv, offset):
    whole = jax.ShapeDtypeStruct((COLS, 2 * HALF), BF)
    kept = pl.BlockSpec(memory_space=pl.ANY)
    second = pl.BlockSpec((COLS, HALF), lambda i: (0, 1))
    return pl.pallas_call(
        finish_kernel,
        grid=(1,),
        out_shape=(whole, whole, whole),
        in_specs=[SMEM_SPEC, pl.BlockSpec((COLS, 3 * HALF), lambda i: (0, 0)), kept, kept, kept],
        out_specs=(second, second, second),
        input_output_aliases={2: 0, 3: 1, 4: 2},
        compiler_params=params(),
        cost_estimate=cost(2 * COLS * COLS * 2 * HALF, 6 * COLS * HALF * 2),
        name="finish",
    )(offset, back, dq, dk, dv)


def attn_grad_kernel(place, og_mine, og_theirs, mine_ref, theirs_ref, row_ref, send_ref):
    total = mm_t(og_mine[...], mine_ref[...]) + mm_t(og_theirs[...], theirs_ref[...])
    total = total.astype(BF)

    @pl.when(pl.program_id(0) < 2)
    def _():
        row_ref[...] = total

    @pl.when(pl.program_id(0) >= 2)
    def _():
        send_ref[...] = total


def attn_grad_of(og, mine, theirs, place):
    steps = 4
    rows = 2 * HALF // steps
    return pl.pallas_call(
        attn_grad_kernel,
        grid_spec=pltpu.PrefetchScalarGridSpec(
            num_scalar_prefetch=1,
            grid=(steps,),
            in_specs=[
                pl.BlockSpec((COLS, DH), lambda i, at: (0, at[0])),
                pl.BlockSpec((COLS, DH), lambda i, at: (0, 1 - at[0])),
                pl.BlockSpec((rows, DH), lambda i, at: (i, 0)),
                pl.BlockSpec((rows, DH), lambda i, at: (i, 0)),
            ],
            out_specs=(
                pl.BlockSpec((COLS, rows), lambda i, at: (0, jnp.minimum(i, 1))),
                pl.BlockSpec((COLS, rows), lambda i, at: (0, jnp.maximum(i, 2) - 2)),
            ),
        ),
        out_shape=(jax.ShapeDtypeStruct((COLS, HALF), BF),) * 2,
        compiler_params=params(),
        cost_estimate=cost(2 * COLS * 2 * HALF * D, 7 * 2**20),
        name="attn_grad",
    )(place, og, og, mine, theirs)


def layer_out_kernel(core_ref, row_ref, col_ref, mine_ref, theirs_ref, o_ref):
    def product(w_ref):
        total = mm(row_ref[...], w_ref[:HALF, :]) + mm(col_ref[...], w_ref[HALF:, :])
        o_ref[...] = total.astype(BF)

    pl.when(pl.program_id(0) == 0)(lambda: product(mine_ref))
    pl.when(pl.program_id(0) == 1)(lambda: product(theirs_ref))


def layer_out_of(row_out, col_out, mine, theirs, core):
    steps = 2
    width = DH // steps

    def place(half, i, c):
        which = jnp.where(half == 0, c[0], 1 - c[0])
        return (0, which * steps + i)

    return pl.pallas_call(
        layer_out_kernel,
        grid_spec=pltpu.PrefetchScalarGridSpec(
            num_scalar_prefetch=1,
            grid=(2, steps),
            in_specs=[
                pl.BlockSpec((COLS, HALF), lambda half, i, c: (0, 0)),
                pl.BlockSpec((COLS, HALF), lambda half, i, c: (0, 0)),
                pl.BlockSpec((2 * HALF, width), lambda half, i, c: (0, jnp.where(half == 0, i, steps - 1))),
                pl.BlockSpec((2 * HALF, width), lambda half, i, c: (0, jnp.where(half == 0, 0, i))),
            ],
            out_specs=pl.BlockSpec((COLS, width), place),
        ),
        out_shape=jax.ShapeDtypeStruct((COLS, D), BF),
        compiler_params=params(),
        cost_estimate=cost(2 * COLS * 2 * HALF * D, 7 * 2**20),
        name="layer_out",
    )(core, row_out, col_out, mine, theirs)


def weight_grad_kernel(place, row_mine, row_theirs, col_mine, col_theirs, og_mine, og_theirs, *refs):
    outs, total = refs[:4], refs[4]
    step = pl.program_id(0)
    block = lax.rem(place[1] + step, 4)

    def product(a_ref, b_ref):
        total[...] = t_mm(a_ref[...], og_mine[...]) + t_mm(b_ref[...], og_theirs[...])

    pl.when(block < 2)(lambda: product(row_mine, row_theirs))
    pl.when(block >= 2)(lambda: product(col_mine, col_theirs))
    for target, out in enumerate(outs):

        @pl.when(step == target)
        def _(out=out):
            out[...] = total[...].astype(out.dtype)


def weight_grad_of(row_mine, row_theirs, col_mine, col_theirs, og, og_theirs, place):
    rows = 2 * HALF // 4

    def row_block(i, at):
        return (0, jnp.minimum(lax.rem(at[1] + i, 4), 1))

    def col_block(i, at):
        return (0, jnp.maximum(lax.rem(at[1] + i, 4), 2) - 2)

    return pl.pallas_call(
        weight_grad_kernel,
        grid_spec=pltpu.PrefetchScalarGridSpec(
            num_scalar_prefetch=1,
            grid=(4,),
            in_specs=[
                pl.BlockSpec((COLS, rows), row_block),
                pl.BlockSpec((COLS, rows), row_block),
                pl.BlockSpec((COLS, rows), col_block),
                pl.BlockSpec((COLS, rows), col_block),
                pl.BlockSpec((COLS, DH), lambda i, at: (0, at[0])),
                pl.BlockSpec((COLS, DH), lambda i, at: (0, 0)),
            ],
            out_specs=(pl.BlockSpec((rows, DH), lambda i, at: (0, 0)),) * 4,
            scratch_shapes=[pltpu.VMEM((rows, DH), F32)],
        ),
        out_shape=(jax.ShapeDtypeStruct((rows, DH), F32),) + (jax.ShapeDtypeStruct((rows, DH), BF),) * 3,
        compiler_params=params(),
        cost_estimate=cost(4 * COLS * 2 * HALF * DH, 7 * 2**20),
        name="weight_grad",
    )(place, row_mine, row_theirs, col_mine, col_theirs, og, og_theirs)


def gather_kernel(axis, pieces, place, own_ref, a_ref, b_ref, c_ref, o_ref):
    chunk = own_ref.shape[0] // pieces
    for step, ref in enumerate((own_ref, a_ref, b_ref, c_ref)):
        source = lax.rem(place[axis] + 4 - step, 4)
        for piece in range(pieces):
            rows = pl.ds(pl.multiple_of((piece * 4 + source) * chunk, chunk), chunk)
            o_ref[rows, :] = ref[piece * chunk : (piece + 1) * chunk, :]


def blocks_of(own, axis):
    return [own] + [along(own, axis, step) for step in (1, 2, 3)]


def gather_of(blocks, place, axis, index, pieces):
    return pl.pallas_call(
        functools.partial(gather_kernel, index, pieces),
        out_shape=jax.ShapeDtypeStruct((4 * blocks[0].shape[0], DH), BF),
        in_specs=[SMEM_SPEC] + [VMEM_SPEC] * 4,
        out_specs=VMEM_SPEC,
        compiler_params=params(),
        cost_estimate=cost(0, 16 * blocks[0].shape[0] * DH),
        name="gather_" + axis,
    )(place, *blocks)


def weight_sum_kernel(place, a_ref, b_ref, c_ref, d_ref, *outs):
    chunk = 2 * HD // 8
    for step, out in enumerate(outs):
        at_y = lax.rem(place[3] + step, 4)
        for at_z in range(2):
            rows = pl.ds(pl.multiple_of(at_z * HD + at_y * chunk, chunk), chunk)
            near = a_ref[rows, :] + b_ref[rows, :].astype(F32)
            far = c_ref[rows, :].astype(F32) + d_ref[rows, :].astype(F32)
            out[at_z * chunk : (at_z + 1) * chunk, :] = (near + far).astype(out.dtype)


def weight_sum(parts, place):
    rows = parts[0].shape[0] // 4
    return pl.pallas_call(
        weight_sum_kernel,
        out_shape=(jax.ShapeDtypeStruct((rows, DH), F32),) + (jax.ShapeDtypeStruct((rows, DH), BF),) * 3,
        in_specs=[SMEM_SPEC] + [VMEM_SPEC] * 4,
        out_specs=(VMEM_SPEC,) * 4,
        compiler_params=params(),
        cost_estimate=cost(16 * rows * DH, 4 * 2**20),
        name="weight_sum",
    )(place, *parts)


def y_sum_kernel(place, a_ref, b_ref, c_ref, d_ref, *refs):
    outs, total = refs[:-1], refs[-1]
    near = a_ref[...] + b_ref[...].astype(F32)
    total[...] = near + (c_ref[...].astype(F32) + d_ref[...].astype(F32))
    rows = outs[0].shape[0]
    for step, out in enumerate(outs):
        target = lax.rem(place[2] + step // 4, 2) * 4 + lax.rem(place[4] + step % 4, 4)
        out[...] = total[pl.ds(pl.multiple_of(target * rows, rows), rows), :].astype(out.dtype)


def y_sum(parts, place):
    rows = parts[0].shape[0] // 8
    return pl.pallas_call(
        y_sum_kernel,
        out_shape=(jax.ShapeDtypeStruct((rows, DH), F32),) + (jax.ShapeDtypeStruct((rows, DH), BF),) * 7,
        in_specs=[SMEM_SPEC] + [VMEM_SPEC] * 4,
        out_specs=(VMEM_SPEC,) * 8,
        scratch_shapes=[pltpu.VMEM(parts[0].shape, F32)],
        compiler_params=params(),
        cost_estimate=cost(32 * rows * DH, 2**20),
        name="y_sum",
    )(place, *parts)


def z_sum_kernel(place, *refs):
    ins, (keep_ref, send_ref) = refs[:8], refs[8:]
    total = ins[0][...]
    for ref in ins[1:]:
        total = total + ref[...].astype(F32)
    half = keep_ref.shape[0]
    first = jnp.broadcast_to(place[0], (half, DH)) == 0
    keep_ref[...] = jnp.where(first, total[:half], total[half:])
    send_ref[...] = jnp.where(first, total[half:], total[:half])


def z_sum(parts, place):
    out = jax.ShapeDtypeStruct((parts[0].shape[0] // 2, DH), F32)
    return pl.pallas_call(
        z_sum_kernel,
        out_shape=(out, out),
        in_specs=[SMEM_SPEC] + [VMEM_SPEC] * 8,
        out_specs=(VMEM_SPEC, VMEM_SPEC),
        compiler_params=params(),
        cost_estimate=cost(8 * 8 * DH, 2**18),
        name="z_sum",
    )(place, *parts)


def exchange(tensor, axes):
    return lax.all_to_all(tensor, axes, split_axis=0, concat_axis=0, tiled=True)


def other_core(tensor):
    return lax.ppermute(tensor, "c", [(0, 1), (1, 0)])


def together(*values):
    return lax.optimization_barrier(values)


def along(tensor, axis, step):
    return lax.ppermute(tensor, axis, [(i, (i + step) % 4) for i in range(4)])


def along_z(tensor, step):
    turns = [(z * 4 + h, (z + step // 4) % 2 * 4 + (h + step % 4) % 4) for z in range(2) for h in range(4)]
    return lax.ppermute(tensor, ("zl", "zh"), turns)


def shards(queries, keys, values, out_proj, out_grad, block_pattern, col_offset):
    q, k, v = (t.reshape(COLS, 2 * HALF) for t in (queries, keys, values))
    og = out_grad.reshape(COLS, D)
    rows_of = out_proj.shape[0]
    seq = ROWS
    near = seq // 2
    dp = lax.axis_size("x") * lax.axis_size("zl")
    core = lax.axis_index("c").astype(jnp.int32)
    place = jnp.stack([core] + [lax.axis_index(name).astype(jnp.int32) for name in ("x", "zl", "y", "zh")])

    halves = out_proj.reshape(rows_of, 2, DH).transpose(1, 0, 2)
    spread = jnp.broadcast_to(halves[None], (near // 2, 2, rows_of, DH)).reshape(near, rows_of, DH)
    own_rows = exchange(spread, NEAR)
    packed = pack(q, k, v, col_offset)
    og_sent = lax.dynamic_slice(og, (0, (1 - core) * DH), (COLS, DH))
    own_rows, packed, og_sent = together(own_rows, packed, og_sent)
    own_rows = own_rows.reshape(near * rows_of, DH)
    blocks = blocks_of(gather_of(blocks_of(own_rows, "y"), place, "y", 3, 2), "x")

    received = exchange(packed.reshape(seq, COLS // seq, 3 * HALF), SEQ)
    received = received.reshape(ROWS, 2, GRP, 3 * HALF)

    col_sent = column_forward(received).reshape(seq, COLS // seq, HALF)
    row_out = row_forward(q, k, v, block_pattern)
    row_theirs = other_core(row_out)
    col_sent, row_out, row_theirs, *blocks = together(col_sent, row_out, row_theirs, *blocks)
    col_mine = exchange(col_sent, SEQ)
    mine = gather_of(blocks, place, "x", 1, 1)
    theirs = other_core(mine)
    og_theirs = other_core(og_sent)
    grad_rows, grad_cols = attn_grad_of(og, mine, theirs, place)
    dq, dk, dv = row_backward(q, k, v, grad_rows, block_pattern)
    col_mine, grad_cols, og_theirs, dq, dk, dv = together(col_mine, grad_cols, og_theirs, dq, dk, dv)
    col_mine = col_mine.reshape(COLS, HALF)

    col_grads = exchange(grad_cols.reshape(seq, COLS // seq, HALF), SEQ)
    col_theirs = other_core(col_mine)
    parts = weight_grad_of(row_out, row_theirs, col_mine, col_theirs, og, og_theirs, place)
    next_x, far_x, last_x = (along(parts[step], "x", step) for step in (1, 2, 3))

    col_back = column_backward(received, col_grads.reshape(ROWS, 2, GRP, HALF)).reshape(seq, COLS // seq, 3 * HALF)
    col_back, next_x, last_x = together(col_back, next_x, last_x)
    back = exchange(col_back, SEQ).reshape(COLS, 3 * HALF)

    parts = weight_sum([parts[0], next_x, far_x, last_x], place)
    layer = layer_out_of(row_out, col_mine, mine, theirs, place)
    parts = [parts[0]] + [along(parts[step], "y", step) for step in (1, 2, 3)]
    layer, *parts = together(layer, *parts)
    parts = y_sum(parts, place)
    parts = [parts[0]] + [along_z(parts[step], step) for step in range(1, 8)]
    dq, dk, dv = finish(back, dq, dk, dv, col_offset)
    dq, dk, dv, *parts = together(dq, dk, dv, *parts)
    keep, give = z_sum(parts, place)
    taken = other_core(give)
    first = core == 0
    tokens = COLS * seq * dp
    w_grad = jnp.concatenate([jnp.where(first, keep, taken), jnp.where(first, taken, keep)], axis=1)
    w_grad = w_grad * tokens ** (-0.5)

    lead = (1, 1, COLS)
    return (
        layer.reshape(lead + (D,)),
        dq.reshape(lead + (2 * HALF,)),
        dk.reshape(lead + (2 * HALF,)),
        dv.reshape(lead + (2 * HALF,)),
        w_grad,
    )


def solution(mesh):
    fine = Mesh(mesh.devices.reshape(4, 2, 4, 4, 2), DP + SEQ)
    token = P(DP, SEQ, None, None)
    rows = P(DP + SEQ, None)
    in_specs = (token, token, token, rows, token, P(), P())
    out_specs = (token, token, token, token, rows)
    return jax.shard_map(shards, mesh=fine, in_specs=in_specs, out_specs=out_specs, check_vma=False)
```

```python
import functools

import jax
import jax.numpy as jnp
from jax import lax
from jax.experimental import pallas as pl
from jax.experimental.pallas import tpu as pltpu
from jax.sharding import Mesh, PartitionSpec as P

HD = 128
HR = 4
HC = 4
BLK = 128
NB = 4
COLS = 512
HALF = HR * HD
D = 2048
DH = D // 2
SCALE = HD ** (-0.5)
BF = jnp.bfloat16
F32 = jnp.float32
GRP = 8
ROWS = 32
TILE = GRP * ROWS
VMEM_LIMIT = 50 * 1024 * 1024

DP = ("x", "zl")
SEQ = ("y", "zh", "c")
NEAR = ("zl", "zh", "c")


def mm(a, b):
    return lax.dot_general(a, b, (((1,), (0,)), ((), ())), preferred_element_type=F32)


def mm_t(a, b):
    return lax.dot_general(a, b, (((1,), (1,)), ((), ())), preferred_element_type=F32)


def t_mm(a, b):
    return lax.dot_general(a, b, (((0,), (0,)), ((), ())), preferred_element_type=F32)


def params():
    return pltpu.CompilerParams(vmem_limit_bytes=VMEM_LIMIT)


def cost(flops, nbytes, trans=0):
    return pl.CostEstimate(flops=int(flops), transcendentals=int(trans), bytes_accessed=int(nbytes))


SMEM_SPEC = pl.BlockSpec(memory_space=pltpu.SMEM)
VMEM_SPEC = pl.BlockSpec(memory_space=pltpu.VMEM)


def head(index):
    return slice(index * HD, (index + 1) * HD)


def shift_selector(offset):
    row = lax.broadcasted_iota(jnp.int32, (COLS, COLS), 0)
    col = lax.broadcasted_iota(jnp.int32, (COLS, COLS), 1)
    source = row - offset
    source = jnp.where(source < 0, source + COLS, source)
    return jnp.where(source == col, 1.0, 0.0).astype(BF)


def pack_kernel(off_ref, q_ref, k_ref, v_ref, o_ref):
    o_ref[:, :HALF] = q_ref[...]
    for h in range(HC):
        pair = jnp.concatenate([k_ref[:, head(h)], v_ref[:, head(h)]], axis=1)
        moved = mm(shift_selector(off_ref[h]), pair).astype(BF)
        o_ref[:, head(HC + h)] = moved[:, :HD]
        o_ref[:, head(2 * HC + h)] = moved[:, HD:]


def pack(q, k, v, offset):
    half = pl.BlockSpec((COLS, HALF), lambda i: (0, 1))
    return pl.pallas_call(
        pack_kernel,
        grid=(1,),
        out_shape=jax.ShapeDtypeStruct((COLS, 3 * HALF), BF),
        in_specs=[SMEM_SPEC, half, half, half],
        out_specs=pl.BlockSpec((COLS, 3 * HALF), lambda i: (0, 0)),
        compiler_params=params(),
        cost_estimate=cost(2 * COLS * COLS * 2 * HALF, 6 * COLS * HALF * 2),
        name="pack",
    )(offset, q, k, v)


def tile_of(ref, lane):
    tile = ref[:, 0, :, lane * HD : (lane + 1) * HD]
    return tile.astype(F32).reshape(TILE, HD).astype(BF)


def store_tile(ref, lane, value):
    ref[:, 0, :, lane * HD : (lane + 1) * HD] = value.reshape(ROWS, GRP, HD).astype(BF)


def column_mask():
    row = lax.broadcasted_iota(jnp.int32, (TILE, TILE), 0)
    col = lax.broadcasted_iota(jnp.int32, (TILE, TILE), 1)
    return lax.rem(row, GRP) == lax.rem(col, GRP)


def softmax(scores):
    e = jnp.exp(scores - jnp.max(scores, axis=-1, keepdims=True))
    return e / jnp.sum(e, axis=-1, keepdims=True)


def column_probs(r_ref, h, mask):
    q = tile_of(r_ref, h)
    k = tile_of(r_ref, HC + h)
    v = tile_of(r_ref, 2 * HC + h)
    return q, k, v, softmax(jnp.where(mask, mm_t(q, k) * SCALE, -1e30))


def column_forward_kernel(r_ref, o_ref):
    mask = column_mask()
    for h in range(HC):
        _, _, v, probs = column_probs(r_ref, h, mask)
        store_tile(o_ref, h, mm(probs.astype(BF), v))


def group_block(lanes):
    return pl.BlockSpec((ROWS, 1, GRP, lanes), lambda i: (0, i, 0, 0))


def column_forward(received):
    return pl.pallas_call(
        column_forward_kernel,
        grid=(2,),
        out_shape=jax.ShapeDtypeStruct((ROWS, 2, GRP, HALF), BF),
        in_specs=[group_block(3 * HALF)],
        out_specs=group_block(HALF),
        compiler_params=params(),
        cost_estimate=cost(10**11, 4 * COLS * HALF * 2, 8 * TILE * TILE),
        name="column_forward",
    )(received)


def column_backward_kernel(r_ref, g_ref, o_ref):
    mask = column_mask()
    for h in range(HC):
        q, k, v, probs = column_probs(r_ref, h, mask)
        g = tile_of(g_ref, h)
        store_tile(o_ref, 2 * HC + h, t_mm(probs.astype(BF), g))
        prob_grad = mm_t(g, v)
        delta = jnp.sum(probs * prob_grad, axis=-1, keepdims=True)
        score_grad = (probs * (prob_grad - delta)).astype(BF)
        store_tile(o_ref, h, mm(score_grad, k) * SCALE)
        store_tile(o_ref, HC + h, t_mm(score_grad, q) * SCALE)


def column_backward(received, grads):
    return pl.pallas_call(
        column_backward_kernel,
        grid=(2,),
        out_shape=jax.ShapeDtypeStruct((ROWS, 2, GRP, 3 * HALF), BF),
        in_specs=[group_block(3 * HALF), group_block(HALF)],
        out_specs=group_block(3 * HALF),
        compiler_params=params(),
        cost_estimate=cost(8 * 10 * TILE * TILE * HD, 7 * COLS * HALF * 2, 8 * TILE * TILE),
        name="column_backward",
    )(received, grads)


def row_tile(pat_ref, q_ref, k_ref, v_ref, h, j):
    block = slice(j * BLK, (j + 1) * BLK)
    other = pl.ds(pl.multiple_of(pat_ref[h, j] * BLK, BLK), BLK)
    q = q_ref[block, head(h)]
    k = jnp.concatenate([k_ref[other, head(h)], k_ref[block, head(h)]], axis=0)
    v = jnp.concatenate([v_ref[other, head(h)], v_ref[block, head(h)]], axis=0)
    return block, other, q, k, v, softmax(mm_t(q, k) * SCALE)


def row_forward_kernel(pat_ref, q_ref, k_ref, v_ref, o_ref):
    for h in range(HR):
        for j in range(NB):
            block, _, _, _, v, probs = row_tile(pat_ref, q_ref, k_ref, v_ref, h, j)
            o_ref[block, head(h)] = mm(probs.astype(BF), v).astype(BF)


def first_half():
    return pl.BlockSpec((COLS, HALF), lambda i: (0, 0))


def row_forward(q, k, v, pattern):
    return pl.pallas_call(
        row_forward_kernel,
        grid=(1,),
        out_shape=jax.ShapeDtypeStruct((COLS, HALF), BF),
        in_specs=[SMEM_SPEC, first_half(), first_half(), first_half()],
        out_specs=first_half(),
        compiler_params=params(),
        cost_estimate=cost(16 * 4 * BLK * 2 * BLK * HD, 4 * COLS * HALF * 2, 16 * BLK * 2 * BLK),
        name="row_forward",
    )(pattern, q, k, v)


def row_backward_kernel(pat_ref, q_ref, k_ref, v_ref, g_ref, dq_ref, dk_ref, dv_ref, own, moved):
    for h in range(HR):
        for j in range(NB):
            block, other, q, k, v, probs = row_tile(pat_ref, q_ref, k_ref, v_ref, h, j)
            g = g_ref[block, head(h)]
            value_terms = t_mm(probs.astype(BF), g)
            prob_grad = mm_t(g, v)
            delta = jnp.sum(probs * prob_grad, axis=-1, keepdims=True)
            score_grad = (probs * (prob_grad - delta)).astype(BF)
            dq_ref[block, head(h)] = (mm(score_grad, k) * SCALE).astype(BF)
            key_terms = t_mm(score_grad, q) * SCALE
            moved[0, other, :] = key_terms[:BLK]
            own[0, block, :] = key_terms[BLK:]
            moved[1, other, :] = value_terms[:BLK]
            own[1, block, :] = value_terms[BLK:]
        dk_ref[:, head(h)] = (own[0] + moved[0]).astype(BF)
        dv_ref[:, head(h)] = (own[1] + moved[1]).astype(BF)


def row_backward(q, k, v, g, pattern):
    whole = jax.ShapeDtypeStruct((COLS, 2 * HALF), BF)
    return pl.pallas_call(
        row_backward_kernel,
        grid=(1,),
        out_shape=(whole, whole, whole),
        in_specs=[SMEM_SPEC] + [first_half()] * 4,
        out_specs=(first_half(),) * 3,
        scratch_shapes=[pltpu.VMEM((2, COLS, HD), F32), pltpu.VMEM((2, COLS, HD), F32)],
        compiler_params=params(),
        cost_estimate=cost(16 * 10 * BLK * 2 * BLK * HD, 7 * COLS * HALF * 2, 16 * BLK * 2 * BLK),
        name="row_backward",
    )(pattern, q, k, v, g)


def finish_kernel(off_ref, b_ref, dq_in, dk_in, dv_in, dq_ref, dk_ref, dv_ref):
    dq_ref[...] = b_ref[:, :HALF]
    for h in range(HC):
        pair = jnp.concatenate([b_ref[:, head(HC + h)], b_ref[:, head(2 * HC + h)]], axis=1)
        back = t_mm(shift_selector(off_ref[h]), pair).astype(BF)
        dk_ref[:, head(h)] = back[:, :HD]
        dv_ref[:, head(h)] = back[:, HD:]


def finish(back, dq, dk, dv, offset):
    whole = jax.ShapeDtypeStruct((COLS, 2 * HALF), BF)
    kept = pl.BlockSpec(memory_space=pl.ANY)
    second = pl.BlockSpec((COLS, HALF), lambda i: (0, 1))
    return pl.pallas_call(
        finish_kernel,
        grid=(1,),
        out_shape=(whole, whole, whole),
        in_specs=[SMEM_SPEC, pl.BlockSpec((COLS, 3 * HALF), lambda i: (0, 0)), kept, kept, kept],
        out_specs=(second, second, second),
        input_output_aliases={2: 0, 3: 1, 4: 2},
        compiler_params=params(),
        cost_estimate=cost(2 * COLS * COLS * 2 * HALF, 6 * COLS * HALF * 2),
        name="finish",
    )(offset, back, dq, dk, dv)


def attn_grad_kernel(place, og_mine, og_theirs, mine_ref, theirs_ref, row_ref, send_ref):
    total = mm_t(og_mine[...], mine_ref[...]) + mm_t(og_theirs[...], theirs_ref[...])
    total = total.astype(BF)

    @pl.when(pl.program_id(0) < 2)
    def _():
        row_ref[...] = total

    @pl.when(pl.program_id(0) >= 2)
    def _():
        send_ref[...] = total


def attn_grad_of(og, mine, theirs, place):
    steps = 4
    rows = 2 * HALF // steps
    return pl.pallas_call(
        attn_grad_kernel,
        grid_spec=pltpu.PrefetchScalarGridSpec(
            num_scalar_prefetch=1,
            grid=(steps,),
            in_specs=[
                pl.BlockSpec((COLS, DH), lambda i, at: (0, at[0])),
                pl.BlockSpec((COLS, DH), lambda i, at: (0, 1 - at[0])),
                pl.BlockSpec((rows, DH), lambda i, at: (i, 0)),
                pl.BlockSpec((rows, DH), lambda i, at: (i, 0)),
            ],
            out_specs=(
                pl.BlockSpec((COLS, rows), lambda i, at: (0, jnp.minimum(i, 1))),
                pl.BlockSpec((COLS, rows), lambda i, at: (0, jnp.maximum(i, 2) - 2)),
            ),
        ),
        out_shape=(jax.ShapeDtypeStruct((COLS, HALF), BF),) * 2,
        compiler_params=params(),
        cost_estimate=cost(2 * COLS * 2 * HALF * D, 7 * 2**20),
        name="attn_grad",
    )(place, og, og, mine, theirs)


def layer_out_kernel(core_ref, row_ref, col_ref, mine_ref, theirs_ref, o_ref):
    def product(w_ref):
        total = mm(row_ref[...], w_ref[:HALF, :]) + mm(col_ref[...], w_ref[HALF:, :])
        o_ref[...] = total.astype(BF)

    pl.when(pl.program_id(0) == 0)(lambda: product(mine_ref))
    pl.when(pl.program_id(0) == 1)(lambda: product(theirs_ref))


def layer_out_of(row_out, col_out, mine, theirs, core):
    steps = 2
    width = DH // steps

    def place(half, i, c):
        which = jnp.where(half == 0, c[0], 1 - c[0])
        return (0, which * steps + i)

    return pl.pallas_call(
        layer_out_kernel,
        grid_spec=pltpu.PrefetchScalarGridSpec(
            num_scalar_prefetch=1,
            grid=(2, steps),
            in_specs=[
                pl.BlockSpec((COLS, HALF), lambda half, i, c: (0, 0)),
                pl.BlockSpec((COLS, HALF), lambda half, i, c: (0, 0)),
                pl.BlockSpec((2 * HALF, width), lambda half, i, c: (0, jnp.where(half == 0, i, steps - 1))),
                pl.BlockSpec((2 * HALF, width), lambda half, i, c: (0, jnp.where(half == 0, 0, i))),
            ],
            out_specs=pl.BlockSpec((COLS, width), place),
        ),
        out_shape=jax.ShapeDtypeStruct((COLS, D), BF),
        compiler_params=params(),
        cost_estimate=cost(2 * COLS * 2 * HALF * D, 7 * 2**20),
        name="layer_out",
    )(core, row_out, col_out, mine, theirs)


def weight_grad_kernel(low, place, a_mine, a_theirs, og_mine, og_theirs, *refs):
    outs, total = refs[:4], refs[4]
    step = pl.program_id(0)
    local = lax.rem(place[1] + step, 4) - low
    inside = jnp.logical_and(local >= 0, local < 2)

    @pl.when(inside)
    def _():
        total[...] = t_mm(a_mine[...], og_mine[...]) + t_mm(a_theirs[...], og_theirs[...])

    @pl.when(jnp.logical_not(inside))
    def _():
        total[...] = jnp.zeros_like(total)

    for target, out in enumerate(outs):

        @pl.when(step == target)
        def _(out=out):
            out[...] = total[...].astype(out.dtype)


def weight_grad_of(mine, theirs, og, og_theirs, place, low):
    rows = 2 * HALF // 4

    def block(i, at):
        return (0, jnp.clip(lax.rem(at[1] + i, 4) - low, 0, 1))

    return pl.pallas_call(
        functools.partial(weight_grad_kernel, low),
        grid_spec=pltpu.PrefetchScalarGridSpec(
            num_scalar_prefetch=1,
            grid=(4,),
            in_specs=[
                pl.BlockSpec((COLS, rows), block),
                pl.BlockSpec((COLS, rows), block),
                pl.BlockSpec((COLS, DH), lambda i, at: (0, at[0])),
                pl.BlockSpec((COLS, DH), lambda i, at: (0, 0)),
            ],
            out_specs=(pl.BlockSpec((rows, DH), lambda i, at: (0, 0)),) * 4,
            scratch_shapes=[pltpu.VMEM((rows, DH), F32)],
        ),
        out_shape=(jax.ShapeDtypeStruct((rows, DH), F32),) + (jax.ShapeDtypeStruct((rows, DH), BF),) * 3,
        compiler_params=params(),
        cost_estimate=cost(2 * COLS * 2 * HALF * DH, 6 * 2**20),
        name="weight_grad",
    )(place, mine, theirs, og, og_theirs)


def gather_kernel(axis, pieces, place, own_ref, a_ref, b_ref, c_ref, o_ref):
    chunk = own_ref.shape[0] // pieces
    for step, ref in enumerate((own_ref, a_ref, b_ref, c_ref)):
        source = lax.rem(place[axis] + 4 - step, 4)
        for piece in range(pieces):
            rows = pl.ds(pl.multiple_of((piece * 4 + source) * chunk, chunk), chunk)
            o_ref[rows, :] = ref[piece * chunk : (piece + 1) * chunk, :]


def blocks_of(own, axis):
    return [own] + [along(own, axis, step) for step in (1, 2, 3)]


def gather_of(blocks, place, axis, index, pieces):
    return pl.pallas_call(
        functools.partial(gather_kernel, index, pieces),
        out_shape=jax.ShapeDtypeStruct((4 * blocks[0].shape[0], DH), BF),
        in_specs=[SMEM_SPEC] + [VMEM_SPEC] * 4,
        out_specs=VMEM_SPEC,
        compiler_params=params(),
        cost_estimate=cost(0, 16 * blocks[0].shape[0] * DH),
        name="gather_" + axis,
    )(place, *blocks)


def weight_sum_kernel(place, *refs):
    ins, outs = refs[:8], refs[8:]
    chunk = 2 * HD // 8
    for step, out in enumerate(outs):
        at_y = lax.rem(place[3] + step, 4)
        for at_z in range(2):
            rows = pl.ds(pl.multiple_of(at_z * HD + at_y * chunk, chunk), chunk)
            total = ins[0][rows, :] + ins[1][rows, :]
            for ref in ins[2:]:
                total = total + ref[rows, :].astype(F32)
            out[at_z * chunk : (at_z + 1) * chunk, :] = total.astype(out.dtype)


def weight_sum(parts, place):
    rows = parts[0].shape[0] // 4
    return pl.pallas_call(
        weight_sum_kernel,
        out_shape=(jax.ShapeDtypeStruct((rows, DH), F32),) + (jax.ShapeDtypeStruct((rows, DH), BF),) * 3,
        in_specs=[SMEM_SPEC] + [VMEM_SPEC] * 8,
        out_specs=(VMEM_SPEC,) * 4,
        compiler_params=params(),
        cost_estimate=cost(32 * rows * DH, 6 * 2**20),
        name="weight_sum",
    )(place, *parts)


def y_sum_kernel(place, a_ref, b_ref, c_ref, d_ref, *refs):
    outs, total = refs[:-1], refs[-1]
    near = a_ref[...] + b_ref[...].astype(F32)
    total[...] = near + (c_ref[...].astype(F32) + d_ref[...].astype(F32))
    rows = outs[0].shape[0]
    for step, out in enumerate(outs):
        target = lax.rem(place[2] + step // 4, 2) * 4 + lax.rem(place[4] + step % 4, 4)
        out[...] = total[pl.ds(pl.multiple_of(target * rows, rows), rows), :].astype(out.dtype)


def y_sum(parts, place):
    rows = parts[0].shape[0] // 8
    return pl.pallas_call(
        y_sum_kernel,
        out_shape=(jax.ShapeDtypeStruct((rows, DH), F32),) + (jax.ShapeDtypeStruct((rows, DH), BF),) * 7,
        in_specs=[SMEM_SPEC] + [VMEM_SPEC] * 4,
        out_specs=(VMEM_SPEC,) * 8,
        scratch_shapes=[pltpu.VMEM(parts[0].shape, F32)],
        compiler_params=params(),
        cost_estimate=cost(32 * rows * DH, 2**20),
        name="y_sum",
    )(place, *parts)


def z_sum_kernel(place, *refs):
    ins, (keep_ref, send_ref) = refs[:8], refs[8:]
    total = ins[0][...]
    for ref in ins[1:]:
        total = total + ref[...].astype(F32)
    half = keep_ref.shape[0]
    first = jnp.broadcast_to(place[0], (half, DH)) == 0
    keep_ref[...] = jnp.where(first, total[:half], total[half:])
    send_ref[...] = jnp.where(first, total[half:], total[:half])


def z_sum(parts, place):
    out = jax.ShapeDtypeStruct((parts[0].shape[0] // 2, DH), F32)
    return pl.pallas_call(
        z_sum_kernel,
        out_shape=(out, out),
        in_specs=[SMEM_SPEC] + [VMEM_SPEC] * 8,
        out_specs=(VMEM_SPEC, VMEM_SPEC),
        compiler_params=params(),
        cost_estimate=cost(8 * 8 * DH, 2**18),
        name="z_sum",
    )(place, *parts)


def exchange(tensor, axes):
    return lax.all_to_all(tensor, axes, split_axis=0, concat_axis=0, tiled=True)


def other_core(tensor):
    return lax.ppermute(tensor, "c", [(0, 1), (1, 0)])


def together(*values):
    return lax.optimization_barrier(values)


def along(tensor, axis, step):
    return lax.ppermute(tensor, axis, [(i, (i + step) % 4) for i in range(4)])


def part_along_x(tensor, low, step):
    pairs = [(i, (i + step) % 4) for i in range(4) if low <= (i + step) % 4 < low + 2]
    return lax.ppermute(tensor, "x", pairs)


def along_z(tensor, step):
    turns = [(z * 4 + h, (z + step // 4) % 2 * 4 + (h + step % 4) % 4) for z in range(2) for h in range(4)]
    return lax.ppermute(tensor, ("zl", "zh"), turns)


def shards(queries, keys, values, out_proj, out_grad, block_pattern, col_offset):
    q, k, v = (t.reshape(COLS, 2 * HALF) for t in (queries, keys, values))
    og = out_grad.reshape(COLS, D)
    rows_of = out_proj.shape[0]
    seq = ROWS
    near = seq // 2
    dp = lax.axis_size("x") * lax.axis_size("zl")
    core = lax.axis_index("c").astype(jnp.int32)
    place = jnp.stack([core] + [lax.axis_index(name).astype(jnp.int32) for name in ("x", "zl", "y", "zh")])

    halves = out_proj.reshape(rows_of, 2, DH).transpose(1, 0, 2)
    spread = jnp.broadcast_to(halves[None], (near // 2, 2, rows_of, DH)).reshape(near, rows_of, DH)
    own_rows = exchange(spread, NEAR)
    packed = pack(q, k, v, col_offset)
    og_sent = lax.dynamic_slice(og, (0, (1 - core) * DH), (COLS, DH))
    own_rows, packed, og_sent = together(own_rows, packed, og_sent)
    own_rows = own_rows.reshape(near * rows_of, DH)
    blocks = blocks_of(gather_of(blocks_of(own_rows, "y"), place, "y", 3, 2), "x")

    received = exchange(packed.reshape(seq, COLS // seq, 3 * HALF), SEQ)
    received = received.reshape(ROWS, 2, GRP, 3 * HALF)

    col_sent = column_forward(received).reshape(seq, COLS // seq, HALF)
    row_out = row_forward(q, k, v, block_pattern)
    row_theirs = other_core(row_out)
    col_sent, row_out, row_theirs, *blocks = together(col_sent, row_out, row_theirs, *blocks)
    col_mine = exchange(col_sent, SEQ)
    mine = gather_of(blocks, place, "x", 1, 1)
    theirs = other_core(mine)
    og_theirs = other_core(og_sent)
    grad_rows, grad_cols = attn_grad_of(og, mine, theirs, place)
    early = weight_grad_of(row_out, row_theirs, og, og_theirs, place, 0)
    col_mine, grad_cols, *early = together(col_mine, grad_cols, *early)
    col_mine = col_mine.reshape(COLS, HALF)

    col_grads = exchange(grad_cols.reshape(seq, COLS // seq, HALF), SEQ)
    col_theirs = other_core(col_mine)
    late = weight_grad_of(col_mine, col_theirs, og, og_theirs, place, 2)
    early_x = [part_along_x(early[step], 0, step) for step in (1, 2, 3)]
    late_x = [part_along_x(late[step], 2, step) for step in (1, 2, 3)]
    dq, dk, dv = row_backward(q, k, v, grad_rows, block_pattern)
    col_grads, dq, dk, dv, *early_x = together(col_grads, dq, dk, dv, *early_x)

    col_back = column_backward(received, col_grads.reshape(ROWS, 2, GRP, HALF)).reshape(seq, COLS // seq, 3 * HALF)
    col_back, *late_x = together(col_back, *late_x)
    back = exchange(col_back, SEQ).reshape(COLS, 3 * HALF)

    parts = weight_sum([early[0], late[0]] + early_x + late_x, place)
    layer = layer_out_of(row_out, col_mine, mine, theirs, place)
    parts = [parts[0]] + [along(parts[step], "y", step) for step in (1, 2, 3)]
    layer, *parts = together(layer, *parts)
    parts = y_sum(parts, place)
    parts = [parts[0]] + [along_z(parts[step], step) for step in range(1, 8)]
    dq, dk, dv = finish(back, dq, dk, dv, col_offset)
    dq, dk, dv, *parts = together(dq, dk, dv, *parts)
    keep, give = z_sum(parts, place)
    taken = other_core(give)
    first = core == 0
    tokens = COLS * seq * dp
    w_grad = jnp.concatenate([jnp.where(first, keep, taken), jnp.where(first, taken, keep)], axis=1)
    w_grad = w_grad * tokens ** (-0.5)

    lead = (1, 1, COLS)
    return (
        layer.reshape(lead + (D,)),
        dq.reshape(lead + (2 * HALF,)),
        dk.reshape(lead + (2 * HALF,)),
        dv.reshape(lead + (2 * HALF,)),
        w_grad,
    )


def solution(mesh):
    fine = Mesh(mesh.devices.reshape(4, 2, 4, 4, 2), DP + SEQ)
    token = P(DP, SEQ, None, None)
    rows = P(DP + SEQ, None)
    in_specs = (token, token, token, rows, token, P(), P())
    out_specs = (token, token, token, token, rows)
    return jax.shard_map(shards, mesh=fine, in_specs=in_specs, out_specs=out_specs, check_vma=False)
```

```python
import functools

import jax
import jax.numpy as jnp
from jax import lax
from jax.experimental import pallas as pl
from jax.experimental.pallas import tpu as pltpu
from jax.sharding import Mesh, PartitionSpec as P

HD = 128
HR = 4
HC = 4
BLK = 128
NB = 4
COLS = 512
HALF = HR * HD
D = 2048
DH = D // 2
SCALE = HD ** (-0.5)
BF = jnp.bfloat16
F32 = jnp.float32
GRP = 8
ROWS = 32
TILE = GRP * ROWS
VMEM_LIMIT = 50 * 1024 * 1024

DP = ("x", "zl")
SEQ = ("y", "zh", "c")
NEAR = ("zl", "zh", "c")


def mm(a, b):
    return lax.dot_general(a, b, (((1,), (0,)), ((), ())), preferred_element_type=F32)


def mm_t(a, b):
    return lax.dot_general(a, b, (((1,), (1,)), ((), ())), preferred_element_type=F32)


def t_mm(a, b):
    return lax.dot_general(a, b, (((0,), (0,)), ((), ())), preferred_element_type=F32)


def params():
    return pltpu.CompilerParams(vmem_limit_bytes=VMEM_LIMIT)


def cost(flops, nbytes, trans=0):
    return pl.CostEstimate(flops=int(flops), transcendentals=int(trans), bytes_accessed=int(nbytes))


SMEM_SPEC = pl.BlockSpec(memory_space=pltpu.SMEM)
VMEM_SPEC = pl.BlockSpec(memory_space=pltpu.VMEM)


def head(index):
    return slice(index * HD, (index + 1) * HD)


def shift_selector(offset):
    row = lax.broadcasted_iota(jnp.int32, (COLS, COLS), 0)
    col = lax.broadcasted_iota(jnp.int32, (COLS, COLS), 1)
    source = row - offset
    source = jnp.where(source < 0, source + COLS, source)
    return jnp.where(source == col, 1.0, 0.0).astype(BF)


def pack_kernel(off_ref, q_ref, k_ref, v_ref, o_ref):
    o_ref[:, :HALF] = q_ref[...]
    for h in range(HC):
        pair = jnp.concatenate([k_ref[:, head(h)], v_ref[:, head(h)]], axis=1)
        moved = mm(shift_selector(off_ref[h]), pair).astype(BF)
        o_ref[:, head(HC + h)] = moved[:, :HD]
        o_ref[:, head(2 * HC + h)] = moved[:, HD:]


def pack(q, k, v, offset):
    half = pl.BlockSpec((COLS, HALF), lambda i: (0, 1))
    return pl.pallas_call(
        pack_kernel,
        grid=(1,),
        out_shape=jax.ShapeDtypeStruct((COLS, 3 * HALF), BF),
        in_specs=[SMEM_SPEC, half, half, half],
        out_specs=pl.BlockSpec((COLS, 3 * HALF), lambda i: (0, 0)),
        compiler_params=params(),
        cost_estimate=cost(2 * COLS * COLS * 2 * HALF, 6 * COLS * HALF * 2),
        name="pack",
    )(offset, q, k, v)


def tile_of(ref, lane):
    tile = ref[:, 0, :, lane * HD : (lane + 1) * HD]
    return tile.astype(F32).reshape(TILE, HD).astype(BF)


def store_tile(ref, lane, value):
    ref[:, 0, :, lane * HD : (lane + 1) * HD] = value.reshape(ROWS, GRP, HD).astype(BF)


def column_mask():
    row = lax.broadcasted_iota(jnp.int32, (TILE, TILE), 0)
    col = lax.broadcasted_iota(jnp.int32, (TILE, TILE), 1)
    return lax.rem(row, GRP) == lax.rem(col, GRP)


def softmax(scores):
    e = jnp.exp(scores - jnp.max(scores, axis=-1, keepdims=True))
    return e / jnp.sum(e, axis=-1, keepdims=True)


def column_probs(r_ref, h, mask):
    q = tile_of(r_ref, h)
    k = tile_of(r_ref, HC + h)
    v = tile_of(r_ref, 2 * HC + h)
    return q, k, v, softmax(jnp.where(mask, mm_t(q, k) * SCALE, -1e30))


def column_forward_kernel(r_ref, o_ref):
    mask = column_mask()
    for h in range(HC):
        _, _, v, probs = column_probs(r_ref, h, mask)
        store_tile(o_ref, h, mm(probs.astype(BF), v))


def group_block(lanes):
    return pl.BlockSpec((ROWS, 1, GRP, lanes), lambda i: (0, i, 0, 0))


def column_forward(received):
    return pl.pallas_call(
        column_forward_kernel,
        grid=(2,),
        out_shape=jax.ShapeDtypeStruct((ROWS, 2, GRP, HALF), BF),
        in_specs=[group_block(3 * HALF)],
        out_specs=group_block(HALF),
        compiler_params=params(),
        cost_estimate=cost(10**11, 4 * COLS * HALF * 2, 8 * TILE * TILE),
        name="column_forward",
    )(received)


def column_backward_kernel(r_ref, g_ref, o_ref):
    mask = column_mask()
    for h in range(HC):
        q, k, v, probs = column_probs(r_ref, h, mask)
        g = tile_of(g_ref, h)
        store_tile(o_ref, 2 * HC + h, t_mm(probs.astype(BF), g))
        prob_grad = mm_t(g, v)
        delta = jnp.sum(probs * prob_grad, axis=-1, keepdims=True)
        score_grad = (probs * (prob_grad - delta)).astype(BF)
        store_tile(o_ref, h, mm(score_grad, k) * SCALE)
        store_tile(o_ref, HC + h, t_mm(score_grad, q) * SCALE)


def column_backward(received, grads):
    return pl.pallas_call(
        column_backward_kernel,
        grid=(2,),
        out_shape=jax.ShapeDtypeStruct((ROWS, 2, GRP, 3 * HALF), BF),
        in_specs=[group_block(3 * HALF), group_block(HALF)],
        out_specs=group_block(3 * HALF),
        compiler_params=params(),
        cost_estimate=cost(8 * 10 * TILE * TILE * HD, 7 * COLS * HALF * 2, 8 * TILE * TILE),
        name="column_backward",
    )(received, grads)


def row_tile(pat_ref, q_ref, k_ref, v_ref, h, j):
    block = slice(j * BLK, (j + 1) * BLK)
    other = pl.ds(pl.multiple_of(pat_ref[h, j] * BLK, BLK), BLK)
    q = q_ref[block, head(h)]
    k = jnp.concatenate([k_ref[other, head(h)], k_ref[block, head(h)]], axis=0)
    v = jnp.concatenate([v_ref[other, head(h)], v_ref[block, head(h)]], axis=0)
    return block, other, q, k, v, softmax(mm_t(q, k) * SCALE)


def row_forward_kernel(pat_ref, q_ref, k_ref, v_ref, o_ref):
    for h in range(HR):
        for j in range(NB):
            block, _, _, _, v, probs = row_tile(pat_ref, q_ref, k_ref, v_ref, h, j)
            o_ref[block, head(h)] = mm(probs.astype(BF), v).astype(BF)


def first_half():
    return pl.BlockSpec((COLS, HALF), lambda i: (0, 0))


def row_forward(q, k, v, pattern):
    return pl.pallas_call(
        row_forward_kernel,
        grid=(1,),
        out_shape=jax.ShapeDtypeStruct((COLS, HALF), BF),
        in_specs=[SMEM_SPEC, first_half(), first_half(), first_half()],
        out_specs=first_half(),
        compiler_params=params(),
        cost_estimate=cost(16 * 4 * BLK * 2 * BLK * HD, 4 * COLS * HALF * 2, 16 * BLK * 2 * BLK),
        name="row_forward",
    )(pattern, q, k, v)


def row_backward_kernel(pat_ref, q_ref, k_ref, v_ref, g_ref, dq_ref, dk_ref, dv_ref, own, moved):
    for h in range(HR):
        for j in range(NB):
            block, other, q, k, v, probs = row_tile(pat_ref, q_ref, k_ref, v_ref, h, j)
            g = g_ref[block, head(h)]
            value_terms = t_mm(probs.astype(BF), g)
            prob_grad = mm_t(g, v)
            delta = jnp.sum(probs * prob_grad, axis=-1, keepdims=True)
            score_grad = (probs * (prob_grad - delta)).astype(BF)
            dq_ref[block, head(h)] = (mm(score_grad, k) * SCALE).astype(BF)
            key_terms = t_mm(score_grad, q) * SCALE
            moved[0, other, :] = key_terms[:BLK]
            own[0, block, :] = key_terms[BLK:]
            moved[1, other, :] = value_terms[:BLK]
            own[1, block, :] = value_terms[BLK:]
        dk_ref[:, head(h)] = (own[0] + moved[0]).astype(BF)
        dv_ref[:, head(h)] = (own[1] + moved[1]).astype(BF)


def row_backward(q, k, v, g, pattern):
    whole = jax.ShapeDtypeStruct((COLS, 2 * HALF), BF)
    return pl.pallas_call(
        row_backward_kernel,
        grid=(1,),
        out_shape=(whole, whole, whole),
        in_specs=[SMEM_SPEC] + [first_half()] * 4,
        out_specs=(first_half(),) * 3,
        scratch_shapes=[pltpu.VMEM((2, COLS, HD), F32), pltpu.VMEM((2, COLS, HD), F32)],
        compiler_params=params(),
        cost_estimate=cost(16 * 10 * BLK * 2 * BLK * HD, 7 * COLS * HALF * 2, 16 * BLK * 2 * BLK),
        name="row_backward",
    )(pattern, q, k, v, g)


def finish_kernel(off_ref, b_ref, dq_in, dk_in, dv_in, dq_ref, dk_ref, dv_ref):
    dq_ref[...] = b_ref[:, :HALF]
    for h in range(HC):
        pair = jnp.concatenate([b_ref[:, head(HC + h)], b_ref[:, head(2 * HC + h)]], axis=1)
        back = t_mm(shift_selector(off_ref[h]), pair).astype(BF)
        dk_ref[:, head(h)] = back[:, :HD]
        dv_ref[:, head(h)] = back[:, HD:]


def finish(back, dq, dk, dv, offset):
    whole = jax.ShapeDtypeStruct((COLS, 2 * HALF), BF)
    kept = pl.BlockSpec(memory_space=pl.ANY)
    second = pl.BlockSpec((COLS, HALF), lambda i: (0, 1))
    return pl.pallas_call(
        finish_kernel,
        grid=(1,),
        out_shape=(whole, whole, whole),
        in_specs=[SMEM_SPEC, pl.BlockSpec((COLS, 3 * HALF), lambda i: (0, 0)), kept, kept, kept],
        out_specs=(second, second, second),
        input_output_aliases={2: 0, 3: 1, 4: 2},
        compiler_params=params(),
        cost_estimate=cost(2 * COLS * COLS * 2 * HALF, 6 * COLS * HALF * 2),
        name="finish",
    )(offset, back, dq, dk, dv)


def attn_grad_kernel(place, og_mine, og_theirs, mine_ref, theirs_ref, row_ref, send_ref):
    total = mm_t(og_mine[...], mine_ref[...]) + mm_t(og_theirs[...], theirs_ref[...])
    total = total.astype(BF)

    @pl.when(pl.program_id(0) < 2)
    def _():
        row_ref[...] = total

    @pl.when(pl.program_id(0) >= 2)
    def _():
        send_ref[...] = total


def attn_grad_of(og, mine, theirs, place):
    steps = 4
    rows = 2 * HALF // steps
    return pl.pallas_call(
        attn_grad_kernel,
        grid_spec=pltpu.PrefetchScalarGridSpec(
            num_scalar_prefetch=1,
            grid=(steps,),
            in_specs=[
                pl.BlockSpec((COLS, DH), lambda i, at: (0, at[0])),
                pl.BlockSpec((COLS, DH), lambda i, at: (0, 1 - at[0])),
                pl.BlockSpec((rows, DH), lambda i, at: (i, 0)),
                pl.BlockSpec((rows, DH), lambda i, at: (i, 0)),
            ],
            out_specs=(
                pl.BlockSpec((COLS, rows), lambda i, at: (0, jnp.minimum(i, 1))),
                pl.BlockSpec((COLS, rows), lambda i, at: (0, jnp.maximum(i, 2) - 2)),
            ),
        ),
        out_shape=(jax.ShapeDtypeStruct((COLS, HALF), BF),) * 2,
        compiler_params=params(),
        cost_estimate=cost(2 * COLS * 2 * HALF * D, 7 * 2**20),
        name="attn_grad",
    )(place, og, og, mine, theirs)


def layer_out_kernel(core_ref, row_ref, col_ref, mine_ref, theirs_ref, o_ref):
    def product(w_ref):
        total = mm(row_ref[...], w_ref[:HALF, :]) + mm(col_ref[...], w_ref[HALF:, :])
        o_ref[...] = total.astype(BF)

    pl.when(pl.program_id(0) == 0)(lambda: product(mine_ref))
    pl.when(pl.program_id(0) == 1)(lambda: product(theirs_ref))


def layer_out_of(row_out, col_out, mine, theirs, core):
    steps = 2
    width = DH // steps

    def place(half, i, c):
        which = jnp.where(half == 0, c[0], 1 - c[0])
        return (0, which * steps + i)

    return pl.pallas_call(
        layer_out_kernel,
        grid_spec=pltpu.PrefetchScalarGridSpec(
            num_scalar_prefetch=1,
            grid=(2, steps),
            in_specs=[
                pl.BlockSpec((COLS, HALF), lambda half, i, c: (0, 0)),
                pl.BlockSpec((COLS, HALF), lambda half, i, c: (0, 0)),
                pl.BlockSpec((2 * HALF, width), lambda half, i, c: (0, jnp.where(half == 0, i, steps - 1))),
                pl.BlockSpec((2 * HALF, width), lambda half, i, c: (0, jnp.where(half == 0, 0, i))),
            ],
            out_specs=pl.BlockSpec((COLS, width), place),
        ),
        out_shape=jax.ShapeDtypeStruct((COLS, D), BF),
        compiler_params=params(),
        cost_estimate=cost(2 * COLS * 2 * HALF * D, 7 * 2**20),
        name="layer_out",
    )(core, row_out, col_out, mine, theirs)


def weight_grad_kernel(low, place, a_mine, a_theirs, og_mine, og_theirs, *refs):
    early, outs, total = refs[:-5], refs[-5:-1], refs[-1]
    step = pl.program_id(0)
    local = lax.rem(place[1] + step, 4) - low
    inside = jnp.logical_and(local >= 0, local < 2)

    @pl.when(inside)
    def _():
        total[...] = t_mm(a_mine[...], og_mine[...]) + t_mm(a_theirs[...], og_theirs[...])

    for target, out in enumerate(outs):

        @pl.when(jnp.logical_and(step == target, inside))
        def _(out=out):
            out[...] = total[...].astype(out.dtype)

        if early:

            @pl.when(jnp.logical_and(step == target, jnp.logical_not(inside)))
            def _(out=out, kept=early[target]):
                out[...] = kept[...]


def weight_grad_of(mine, theirs, og, og_theirs, place, low, early=()):
    rows = 2 * HALF // 4

    def block(i, at):
        return (0, jnp.clip(lax.rem(at[1] + i, 4) - low, 0, 1))

    whole = pl.BlockSpec((rows, DH), lambda i, at: (0, 0))
    return pl.pallas_call(
        functools.partial(weight_grad_kernel, low),
        grid_spec=pltpu.PrefetchScalarGridSpec(
            num_scalar_prefetch=1,
            grid=(4,),
            in_specs=[
                pl.BlockSpec((COLS, rows), block),
                pl.BlockSpec((COLS, rows), block),
                pl.BlockSpec((COLS, DH), lambda i, at: (0, at[0])),
                pl.BlockSpec((COLS, DH), lambda i, at: (0, 0)),
            ]
            + [whole] * len(early),
            out_specs=(whole,) * 4,
            scratch_shapes=[pltpu.VMEM((rows, DH), F32)],
        ),
        out_shape=(jax.ShapeDtypeStruct((rows, DH), F32),) + (jax.ShapeDtypeStruct((rows, DH), BF),) * 3,
        compiler_params=params(),
        cost_estimate=cost(2 * COLS * 2 * HALF * DH, 6 * 2**20),
        name="weight_grad",
    )(place, mine, theirs, og, og_theirs, *early)


def gather_kernel(axis, pieces, place, own_ref, a_ref, b_ref, c_ref, o_ref):
    chunk = own_ref.shape[0] // pieces
    for step, ref in enumerate((own_ref, a_ref, b_ref, c_ref)):
        source = lax.rem(place[axis] + 4 - step, 4)
        for piece in range(pieces):
            rows = pl.ds(pl.multiple_of((piece * 4 + source) * chunk, chunk), chunk)
            o_ref[rows, :] = ref[piece * chunk : (piece + 1) * chunk, :]


def blocks_of(own, axis):
    return [own] + [along(own, axis, step) for step in (1, 2, 3)]


def gather_of(blocks, place, axis, index, pieces):
    return pl.pallas_call(
        functools.partial(gather_kernel, index, pieces),
        out_shape=jax.ShapeDtypeStruct((4 * blocks[0].shape[0], DH), BF),
        in_specs=[SMEM_SPEC] + [VMEM_SPEC] * 4,
        out_specs=VMEM_SPEC,
        compiler_params=params(),
        cost_estimate=cost(0, 16 * blocks[0].shape[0] * DH),
        name="gather_" + axis,
    )(place, *blocks)


def weight_sum_kernel(place, a_ref, b_ref, c_ref, d_ref, *outs):
    chunk = 2 * HD // 8
    for step, out in enumerate(outs):
        at_y = lax.rem(place[3] + step, 4)
        for at_z in range(2):
            rows = pl.ds(pl.multiple_of(at_z * HD + at_y * chunk, chunk), chunk)
            near = a_ref[rows, :] + b_ref[rows, :].astype(F32)
            far = c_ref[rows, :].astype(F32) + d_ref[rows, :].astype(F32)
            out[at_z * chunk : (at_z + 1) * chunk, :] = (near + far).astype(out.dtype)


def weight_sum(parts, place):
    rows = parts[0].shape[0] // 4
    return pl.pallas_call(
        weight_sum_kernel,
        out_shape=(jax.ShapeDtypeStruct((rows, DH), F32),) + (jax.ShapeDtypeStruct((rows, DH), BF),) * 3,
        in_specs=[SMEM_SPEC] + [VMEM_SPEC] * 4,
        out_specs=(VMEM_SPEC,) * 4,
        compiler_params=params(),
        cost_estimate=cost(16 * rows * DH, 4 * 2**20),
        name="weight_sum",
    )(place, *parts)


def y_sum_kernel(place, a_ref, b_ref, c_ref, d_ref, *refs):
    outs, total = refs[:-1], refs[-1]
    near = a_ref[...] + b_ref[...].astype(F32)
    total[...] = near + (c_ref[...].astype(F32) + d_ref[...].astype(F32))
    rows = outs[0].shape[0]
    for step, out in enumerate(outs):
        target = lax.rem(place[2] + step // 4, 2) * 4 + lax.rem(place[4] + step % 4, 4)
        out[...] = total[pl.ds(pl.multiple_of(target * rows, rows), rows), :].astype(out.dtype)


def y_sum(parts, place):
    rows = parts[0].shape[0] // 8
    return pl.pallas_call(
        y_sum_kernel,
        out_shape=(jax.ShapeDtypeStruct((rows, DH), F32),) + (jax.ShapeDtypeStruct((rows, DH), BF),) * 7,
        in_specs=[SMEM_SPEC] + [VMEM_SPEC] * 4,
        out_specs=(VMEM_SPEC,) * 8,
        scratch_shapes=[pltpu.VMEM(parts[0].shape, F32)],
        compiler_params=params(),
        cost_estimate=cost(32 * rows * DH, 2**20),
        name="y_sum",
    )(place, *parts)


def z_sum_kernel(place, *refs):
    ins, (keep_ref, send_ref) = refs[:8], refs[8:]
    total = ins[0][...]
    for ref in ins[1:]:
        total = total + ref[...].astype(F32)
    half = keep_ref.shape[0]
    first = jnp.broadcast_to(place[0], (half, DH)) == 0
    keep_ref[...] = jnp.where(first, total[:half], total[half:])
    send_ref[...] = jnp.where(first, total[half:], total[:half])


def z_sum(parts, place):
    out = jax.ShapeDtypeStruct((parts[0].shape[0] // 2, DH), F32)
    return pl.pallas_call(
        z_sum_kernel,
        out_shape=(out, out),
        in_specs=[SMEM_SPEC] + [VMEM_SPEC] * 8,
        out_specs=(VMEM_SPEC, VMEM_SPEC),
        compiler_params=params(),
        cost_estimate=cost(8 * 8 * DH, 2**18),
        name="z_sum",
    )(place, *parts)


def exchange(tensor, axes):
    return lax.all_to_all(tensor, axes, split_axis=0, concat_axis=0, tiled=True)


def other_core(tensor):
    return lax.ppermute(tensor, "c", [(0, 1), (1, 0)])


def together(*values):
    return lax.optimization_barrier(values)


def along(tensor, axis, step):
    return lax.ppermute(tensor, axis, [(i, (i + step) % 4) for i in range(4)])


def along_z(tensor, step):
    turns = [(z * 4 + h, (z + step // 4) % 2 * 4 + (h + step % 4) % 4) for z in range(2) for h in range(4)]
    return lax.ppermute(tensor, ("zl", "zh"), turns)


def shards(queries, keys, values, out_proj, out_grad, block_pattern, col_offset):
    q, k, v = (t.reshape(COLS, 2 * HALF) for t in (queries, keys, values))
    og = out_grad.reshape(COLS, D)
    rows_of = out_proj.shape[0]
    seq = ROWS
    near = seq // 2
    dp = lax.axis_size("x") * lax.axis_size("zl")
    core = lax.axis_index("c").astype(jnp.int32)
    place = jnp.stack([core] + [lax.axis_index(name).astype(jnp.int32) for name in ("x", "zl", "y", "zh")])

    halves = out_proj.reshape(rows_of, 2, DH).transpose(1, 0, 2)
    spread = jnp.broadcast_to(halves[None], (near // 2, 2, rows_of, DH)).reshape(near, rows_of, DH)
    own_rows = exchange(spread, NEAR)
    packed = pack(q, k, v, col_offset)
    og_sent = lax.dynamic_slice(og, (0, (1 - core) * DH), (COLS, DH))
    own_rows, packed, og_sent = together(own_rows, packed, og_sent)
    own_rows = own_rows.reshape(near * rows_of, DH)
    blocks = blocks_of(gather_of(blocks_of(own_rows, "y"), place, "y", 3, 2), "x")

    received = exchange(packed.reshape(seq, COLS // seq, 3 * HALF), SEQ)
    received = received.reshape(ROWS, 2, GRP, 3 * HALF)

    col_sent = column_forward(received).reshape(seq, COLS // seq, HALF)
    row_out = row_forward(q, k, v, block_pattern)
    row_theirs = other_core(row_out)
    col_sent, row_out, row_theirs, *blocks = together(col_sent, row_out, row_theirs, *blocks)
    col_mine = exchange(col_sent, SEQ)
    mine = gather_of(blocks, place, "x", 1, 1)
    theirs = other_core(mine)
    og_theirs = other_core(og_sent)
    grad_rows, grad_cols = attn_grad_of(og, mine, theirs, place)
    early = weight_grad_of(row_out, row_theirs, og, og_theirs, place, 0)
    col_mine, grad_cols, *early = together(col_mine, grad_cols, *early)
    col_mine = col_mine.reshape(COLS, HALF)

    col_grads = exchange(grad_cols.reshape(seq, COLS // seq, HALF), SEQ)
    col_theirs = other_core(col_mine)
    parts = weight_grad_of(col_mine, col_theirs, og, og_theirs, place, 2, early)
    x_parts = [parts[0]] + [along(parts[step], "x", step) for step in (1, 3, 2)]
    dq, dk, dv = row_backward(q, k, v, grad_rows, block_pattern)
    col_grads, dq, dk, dv = together(col_grads, dq, dk, dv)

    col_back = column_backward(received, col_grads.reshape(ROWS, 2, GRP, HALF)).reshape(seq, COLS // seq, 3 * HALF)
    col_back, *x_parts = together(col_back, *x_parts)
    back = exchange(col_back, SEQ).reshape(COLS, 3 * HALF)

    parts = weight_sum(x_parts, place)
    layer = layer_out_of(row_out, col_mine, mine, theirs, place)
    parts = [parts[0]] + [along(parts[step], "y", step) for step in (1, 2, 3)]
    layer, *parts = together(layer, *parts)
    parts = y_sum(parts, place)
    parts = [parts[0]] + [along_z(parts[step], step) for step in range(1, 8)]
    dq, dk, dv = finish(back, dq, dk, dv, col_offset)
    dq, dk, dv, *parts = together(dq, dk, dv, *parts)
    keep, give = z_sum(parts, place)
    taken = other_core(give)
    first = core == 0
    tokens = COLS * seq * dp
    w_grad = jnp.concatenate([jnp.where(first, keep, taken), jnp.where(first, taken, keep)], axis=1)
    w_grad = w_grad * tokens ** (-0.5)

    lead = (1, 1, COLS)
    return (
        layer.reshape(lead + (D,)),
        dq.reshape(lead + (2 * HALF,)),
        dk.reshape(lead + (2 * HALF,)),
        dv.reshape(lead + (2 * HALF,)),
        w_grad,
    )


def solution(mesh):
    fine = Mesh(mesh.devices.reshape(4, 2, 4, 4, 2), DP + SEQ)
    token = P(DP, SEQ, None, None)
    rows = P(DP + SEQ, None)
    in_specs = (token, token, token, rows, token, P(), P())
    out_specs = (token, token, token, token, rows)
    return jax.shard_map(shards, mesh=fine, in_specs=in_specs, out_specs=out_specs, check_vma=False)
```
